32 devices in a mesh: dp: 16 (over z, y, x), mp: 2 (over core).
Axes of the slice: x: 2, y: 2, z: 4, core: 2. Of those that a mesh axis runs over, the one named last changes fastest.
Arguments:
- query: bfloat16 [1024, 4096], P('dp', 'mp'), may hold values from -144 to 144
- new_key: bfloat16 [1024, 4096], P('dp', 'mp'), may hold values from -6 to 6
- new_value: bfloat16 [1024, 4096], P('dp', 'mp'), may hold values from -6 to 6
- cache_key: bfloat16 [1024, 32, 16, 128], P('dp', 'mp'), may hold values from -6 to 6
- cache_value: bfloat16 [1024, 32, 16, 128], P('dp', 'mp'), may hold values from -6 to 6
- cache_len: int32 [1024], P('dp'), may hold values from 2 to 16
- residual: bfloat16 [1024, 8192], P('dp'), may hold values from -6 to 6
- out_weight: bfloat16 [4096, 8192], P('mp'), may hold values from -0.1875 to 0.1875
- norm_gain: bfloat16 [8192], P('mp'), may hold values from 0.25 to 1.75
- codec_weight: bfloat16 [8192, 1024], P('mp'), may hold values from -0.125 to 0.125
- finished: int32 [1024], P('dp'), may hold values from 0 to 1
- owner: int32 [1024], P('dp'), may hold values from 0 to 15, as said below
- frames: bfloat16 [16384, 1024], P('dp', 'mp'), may hold values from -6 to 6
- snake_alpha: float32 [1024], P('mp'), may hold values from 0.5 to 2
- filter_weight: bfloat16 [7, 1024, 1024], P(None, None, 'mp'), may hold values from -0.125 to 0.125
- conv_bias: float32 [1024], P('mp'), may hold values from -4 to 4
Outputs:
- hidden: bfloat16 [1024, 8192], P('dp', 'mp')
- audio: bfloat16 [16384, 1024], P('dp', 'mp')
The draws below stay inside these ranges and needn't reach their ends.
Inputs may be any that keep to these rules, and one draw needn't show every extreme that they name: Within each aligned block of 64 rows, at most 4 finished rows name the same owner, and some owner is named by exactly 4 finished rows of the block.
All inputs are finite; a program needn't handle non-finite values.
Results may differ from the reference program's by a relative error of at most 0.0056.
Values may be sent and summed in bfloat16 or wider, within the bound.
A program may use at most 128 MiB of HBM per device.

```python
import math
import jax
import jax.numpy as jnp
from jax import lax

D = 8192
HEADS = 32
HD = 128
CODEC = 1024
ROW_DEV = 64
CACHE = 16
FRAMES = 1024
KERNEL_TAPS = 7
DILATION_STEP = 3
CAP = 4
ROWS = 1024
TOTAL_FRAMES = 16384
N_DP = 16


def key_tables(key):
    base = jax.random.fold_in(key, 11)
    first, second = jax.random.split(base, 2)
    keys = jnp.clip(jax.random.normal(first, (ROWS, HEADS, CACHE, HD), jnp.float32), -6.0, 6.0)
    queries = jnp.clip(jax.random.normal(second, (ROWS, HEADS, HD), jnp.float32), -6.0, 6.0)
    return (keys, queries.reshape(ROWS, HEADS * HD))


def draw_query(key, part):
    return key_tables(key)[1].astype(jnp.bfloat16)


def draw_cache_key(key, part):
    return key_tables(key)[0].astype(jnp.bfloat16)


def route_tables(key):
    base = jax.random.fold_in(key, 23)
    first, second, third = jax.random.split(base, 3)
    owners_perm = jax.vmap(lambda sub: jax.random.permutation(sub, N_DP))(jax.random.split(first, N_DP))
    orders = jax.vmap(lambda sub: jax.random.permutation(sub, ROW_DEV))(jax.random.split(second, N_DP))
    owners = jnp.take_along_axis(owners_perm, orders // CAP, axis=1)
    coins = (jax.random.randint(third, (N_DP, ROW_DEV), 0, 8) < 7).astype(jnp.int32)
    done = jnp.where(orders < CAP, 1, coins)
    return (owners.reshape(ROWS).astype(jnp.int32), done.reshape(ROWS).astype(jnp.int32))


def draw_owner(key, part):
    return route_tables(key)[0]


def draw_finished(key, part):
    return route_tables(key)[1]


def touch_ends(array, stream_key, smallest, top_value):
    dims = array.shape
    spot = [jax.random.randint(jax.random.fold_in(stream_key, axis), (), 0, dims[axis]) for axis in range(len(dims))]
    array = array.at[tuple(spot)].set(smallest)
    longest = dims.index(max(dims))
    spot[longest] = (spot[longest] + 1) % dims[longest]
    return array.at[tuple(spot)].set(top_value)


def steps_of(rng, dims, shards, smallest, high):
    factor_of, own = 1.0, jax.random.fold_in(rng, 6)
    for dim, shards_of in shards:
        heights = jnp.exp(jax.random.uniform(jax.random.fold_in(own, dim), (shards_of,), jnp.float32, smallest / len(shards), high / len(shards)))
        factor_of = factor_of * jnp.repeat(heights, dims[dim] // shards_of).reshape([-1 if axis == dim else 1 for axis in range(len(dims))])
    return factor_of


def noise(own_key, shape, width, reach, cuts=(), held_as=jnp.bfloat16):
    loudness = steps_of(own_key, shape, cuts, -0.22, 0.18) if cuts else 1.0
    result = jax.random.normal(own_key, shape, jnp.float32) * width * loudness
    return jnp.minimum(jnp.maximum(result, -reach), reach).astype(held_as)


def setup_inputs(seed: int = 0) -> dict:
    arg_keys = jax.random.split(jax.random.key(seed), 17)
    query = draw_query(jax.random.fold_in(arg_keys[16], 71), 0)
    new_key = noise(arg_keys[1], (ROWS, HEADS * HD), 1.0, 6.0, ((0, 16), (1, 2)))
    new_value = noise(arg_keys[2], (ROWS, HEADS * HD), 1.0, 6.0, ((0, 16), (1, 2)))
    cache_key = draw_cache_key(jax.random.fold_in(arg_keys[16], 71), 0)
    cache_value = noise(arg_keys[4], (ROWS, HEADS, CACHE, HD), 1.0, 6.0, ((0, 16), (1, 2)))
    cache_len = touch_ends(jax.random.randint(arg_keys[5], (ROWS,), 2, CACHE + 1), jax.random.fold_in(arg_keys[5], 1), 2, CACHE).astype(jnp.int32)
    residual = noise(arg_keys[6], (ROWS, D), 1.0, 6.0, ((0, 16),))
    out_weight = noise(arg_keys[7], (HEADS * HD, D), (HEADS * HD // 4) ** -0.5, 0.1875, ((0, 2),))
    norm_gain = jnp.clip(1.0 + 0.15 * jax.random.normal(arg_keys[8], (D,), jnp.float32), 0.25, 1.75).astype(jnp.bfloat16)
    codec_weight = noise(arg_keys[9], (D, CODEC), (D // 4) ** -0.5, 0.125, ((0, 2),))
    finished = draw_finished(jax.random.fold_in(arg_keys[16], 71), 0)
    owner = draw_owner(jax.random.fold_in(arg_keys[16], 71), 0)
    frames = noise(arg_keys[12], (TOTAL_FRAMES, CODEC), 1.0, 6.0, ((0, 16), (1, 2)))
    snake_alpha = jnp.clip(jnp.exp(math.log(2.0) - 1.3862944 * jax.random.uniform(arg_keys[13], (CODEC,), jnp.float32) ** steps_of(arg_keys[13], (CODEC,), ((0, 2),), -0.2, 0.2)), 0.5, 2.0)
    filter_weight = noise(arg_keys[14], (KERNEL_TAPS, CODEC, CODEC), (KERNEL_TAPS * CODEC // 4) ** -0.5, 0.125, ((2, 2),))
    conv_bias = noise(arg_keys[15], (CODEC,), 1.0, 4.0, ((0, 2),), jnp.float32)
    return dict(query=query, new_key=new_key, new_value=new_value, cache_key=cache_key, cache_value=cache_value, cache_len=cache_len, residual=residual, out_weight=out_weight, norm_gain=norm_gain, codec_weight=codec_weight, finished=finished, owner=owner, frames=frames, snake_alpha=snake_alpha, filter_weight=filter_weight, conv_bias=conv_bias)


def reference(query, new_key, new_value, cache_key, cache_value, cache_len, residual, out_weight, norm_gain, codec_weight, finished, owner, frames, snake_alpha, filter_weight, conv_bias):
    count = query.shape[0]
    heads = cache_key.shape[1]
    depth = cache_key.shape[3]
    positions = cache_key.shape[2]
    scale = 1.0 / jnp.sqrt(jnp.float32(depth))
    queries = query.reshape(count, heads, depth).astype(jnp.float32)
    fresh_key = new_key.reshape(count, heads, depth).astype(jnp.float32)
    fresh_value = new_value.reshape(count, heads, depth).astype(jnp.float32)
    scores = jnp.einsum('rhd,rhld->rhl', queries, cache_key.astype(jnp.float32)) * scale
    own_score = jnp.einsum('rhd,rhd->rh', queries, fresh_key) * scale
    valid = jnp.arange(positions, dtype=jnp.int32)[None, :] < cache_len[:, None]
    scores = jnp.where(valid[:, None, :], scores, -1e+30)
    top = jnp.maximum(lax.optimization_barrier(jnp.max(scores, axis=-1)), own_score)
    expo = jnp.where(valid[:, None, :], jnp.exp(scores - top[..., None]), 0.0)
    own_expo = jnp.exp(own_score - top)
    total = lax.optimization_barrier(jnp.sum(expo, axis=-1)) + own_expo
    weights = (expo / total[..., None]).astype(jnp.bfloat16)
    own_weight = (own_expo / total).astype(jnp.bfloat16)
    attended = jnp.einsum('rhl,rhld->rhd', weights.astype(jnp.float32), cache_value.astype(jnp.float32))
    attended = attended + own_weight.astype(jnp.float32)[..., None] * fresh_value
    attended = attended.astype(jnp.bfloat16).reshape(count, heads * depth)
    projected = jnp.dot(attended, out_weight, preferred_element_type=jnp.float32)
    hidden = (residual.astype(jnp.float32) + projected).astype(jnp.bfloat16)
    wide = hidden.astype(jnp.float32)
    meansq = lax.optimization_barrier(jnp.mean(wide * wide, axis=-1))
    normed = (wide * norm_gain.astype(jnp.float32)).astype(jnp.bfloat16)
    latent = jnp.dot(normed, codec_weight, preferred_element_type=jnp.float32) * lax.rsqrt(meansq + 1e-05)[:, None]
    latent = latent.astype(jnp.bfloat16)
    index = jnp.arange(count, dtype=jnp.int32)
    block = index // ROW_DEV
    earlier = (block[:, None] == block[None, :]) & (owner[:, None] == owner[None, :]) & (finished[None, :] == 1) & (index[None, :] < index[:, None])
    slot = lax.optimization_barrier(jnp.sum(earlier.astype(jnp.int32), axis=1)).astype(jnp.int32)
    overall_frames = frames.shape[0]
    target = (owner * FRAMES + block * CAP + slot).astype(jnp.int32)
    target = jnp.where(finished == 1, target, overall_frames).astype(jnp.int32)
    added = jnp.zeros(frames.shape, jnp.float32).at[target].add(latent.astype(jnp.float32), mode='drop')
    mix = frames.astype(jnp.float32) + added
    alpha = snake_alpha.astype(jnp.float32)
    act = (mix + jnp.sin(alpha * mix) ** 2 / alpha).astype(jnp.bfloat16)
    filter_span = KERNEL_TAPS // 2 * DILATION_STEP
    padded_frames = jnp.pad(act, ((filter_span, filter_span), (0, 0)))
    dilated_filter = jnp.zeros(mix.shape, jnp.float32)
    for tap_index in range(KERNEL_TAPS):
        dilated_filter = dilated_filter + jnp.dot(padded_frames[tap_index * DILATION_STEP:tap_index * DILATION_STEP + overall_frames], filter_weight[tap_index], preferred_element_type=jnp.float32)
    audio = (mix + conv_bias.astype(jnp.float32) + dilated_filter).astype(jnp.bfloat16)
    return (hidden, audio)
```

```python
import functools
import jax
import jax.numpy as jnp
from jax import lax
from jax.experimental import pallas as pl
from jax.experimental.pallas import tpu as pltpu
from jax.sharding import PartitionSpec as P

KERNEL_TAPS = 7
DILATION_STEP = 3
CAP = 4
ROW_TILE = 16


def swap(x):
    return lax.ppermute(x, "mp", [(0, 1), (1, 0)])


def gather_mp(x, axis):
    if lax.axis_size("mp") != 2:
        return lax.all_gather(x, "mp", axis=axis, tiled=True)
    other = swap(x)
    first = lax.axis_index("mp") == 0
    return jnp.concatenate([jnp.where(first, x, other), jnp.where(first, other, x)], axis=axis)


def sin_squared(x):
    turns = jnp.round(x * 0.3183098861837907)
    r = (x - turns * 3.140625) - turns * 0.0009676535897932
    q = r * r
    p = -2.5052108e-08 + q * 1.6059044e-10
    p = 2.7557319e-06 + q * p
    p = -1.9841270e-04 + q * p
    p = 8.3333333e-03 + q * p
    p = -1.6666667e-01 + q * p
    sine = r + r * (q * p)
    return sine * sine


def snake(mix, alpha):
    return (mix + sin_squared(alpha * mix) / alpha).astype(jnp.bfloat16)


def columns_kernel(start_ref, x_ref, w_ref, o_ref):
    del start_ref
    o_ref[...] = jnp.dot(x_ref[...], w_ref[...], preferred_element_type=jnp.float32).astype(
        o_ref.dtype
    )


def columns_dot(x, w, start, width, tile, dtype):
    rows, depth = x.shape
    return pl.pallas_call(
        columns_kernel,
        out_shape=jax.ShapeDtypeStruct((rows, width), dtype),
        grid_spec=pltpu.PrefetchScalarGridSpec(
            num_scalar_prefetch=1,
            grid=(width // tile,),
            in_specs=[
                pl.BlockSpec((rows, depth), lambda j, s: (0, 0)),
                pl.BlockSpec((depth, tile), lambda j, s: (0, s[0] + j)),
            ],
            out_specs=pl.BlockSpec((rows, tile), lambda j, s: (0, j)),
        ),
        compiler_params=pltpu.CompilerParams(vmem_limit_bytes=28 * 1024 * 1024),
        cost_estimate=pl.CostEstimate(
            flops=2 * rows * depth * width, bytes_accessed=2 * depth * width, transcendentals=0
        ),
    )(jnp.full((1,), start, jnp.int32), x, w)


def handoff_kernel(
    n_dp, n_mp, near, out_ref, a_ref, b_ref, land_a, land_b, send_a, recv_a, send_b, recv_b
):
    dp = lax.axis_index("dp")
    mp = lax.axis_index("mp")
    count = n_dp * n_mp
    me = dp * n_mp + mp
    barrier = pltpu.get_barrier_semaphore()

    def place(step):
        peer = lax.rem(me + step, count)
        return peer, peer // n_mp, lax.rem(peer, n_mp)

    def greet(step, carry):
        _, pd, pm = place(step)
        pl.semaphore_signal(
            barrier, inc=1, device_id=(pd, pm), device_id_type=pl.DeviceIdType.MESH
        )
        return carry

    lax.fori_loop(1, count, greet, 0)
    pl.semaphore_wait(barrier, count - 1)

    def copy_a(pd, pm, send, recv):
        return pltpu.make_async_remote_copy(
            src_ref=out_ref.at[pd],
            dst_ref=land_a.at[me],
            send_sem=send_a.at[send],
            recv_sem=recv_a.at[recv],
            device_id=(pd, pm),
            device_id_type=pl.DeviceIdType.MESH,
        )

    def copy_b(slot, pd, pm, send, recv):
        return pltpu.make_async_remote_copy(
            src_ref=out_ref.at[pd + 1],
            dst_ref=land_b.at[slot],
            send_sem=send_b.at[send],
            recv_sem=recv_b.at[recv],
            device_id=(pd, pm),
            device_id_type=pl.DeviceIdType.MESH,
        )

    def send(step, carry):
        peer, pd, pm = place(step)
        copy_a(pd, pm, peer, me).start()
        return carry

    def send_near(step, carry):
        peer, pd, pm = place(step)
        copy_b(me, pd, pm, peer, me).start()
        return carry

    @pl.when(dp < near)
    def _():
        lax.fori_loop(1, count, send_near, 0)

    lax.fori_loop(1, count, send, 0)
    land_a[me] = out_ref[dp]

    @pl.when(dp < near)
    def _():
        land_b[me] = out_ref[dp + 1]

    def finish(step, carry):
        peer, pd, pm = place(step)
        copy = copy_a(pd, pm, peer, peer)
        copy.wait_recv()
        copy.wait_send()
        return carry

    def finish_near(step, carry):
        peer, pd, pm = place(step)
        copy_b(me, pd, pm, peer, me).wait_send()
        return carry

    def take_near(sender, carry):
        @pl.when(sender != me)
        def _():
            copy_b(sender, 0, 0, sender, sender).wait_recv()

        return carry

    lax.fori_loop(1, count, finish, 0)

    @pl.when(dp < near)
    def _():
        lax.fori_loop(1, count, finish_near, 0)

    lax.fori_loop(0, near * n_mp, take_near, 0)

    def total_of(land, first):
        total = land[first].astype(jnp.float32)
        for m in range(1, n_mp):
            total = total + land[first + m].astype(jnp.float32)
        return total

    def put(d, carry):
        a_ref[d] = total_of(land_a, d * n_mp)
        return carry

    lax.fori_loop(0, n_dp, put, 0)
    for d in range(near):
        b_ref[d] = total_of(land_b, d * n_mp)


def handoff(outgoing, near):
    n_dp, n_mp = lax.axis_size("dp"), lax.axis_size("mp")
    count = n_dp * n_mp
    _, cap, width = outgoing.shape
    vmem = pl.BlockSpec(memory_space=pltpu.VMEM)
    return pl.pallas_call(
        functools.partial(handoff_kernel, n_dp, n_mp, near),
        out_shape=(
            jax.ShapeDtypeStruct((n_dp, cap, width), jnp.float32),
            jax.ShapeDtypeStruct((near, cap, width), jnp.float32),
        ),
        in_specs=[vmem],
        out_specs=(vmem, vmem),
        scratch_shapes=[
            pltpu.VMEM((count, cap, width), jnp.bfloat16),
            pltpu.VMEM((near * n_mp, cap, width), jnp.bfloat16),
            pltpu.SemaphoreType.DMA((count,)),
            pltpu.SemaphoreType.DMA((count,)),
            pltpu.SemaphoreType.DMA((count,)),
            pltpu.SemaphoreType.DMA((near * n_mp,)),
        ],
        compiler_params=pltpu.CompilerParams(
            collective_id=0, has_side_effects=True, vmem_limit_bytes=16 * 1024 * 1024
        ),
    )(outgoing)


def round_up(n, tile):
    return -(-n // tile) * tile


def taps_of(cells, rows):
    parts = [cells[t * DILATION_STEP : t * DILATION_STEP + rows] for t in range(KERNEL_TAPS)]
    return jnp.concatenate(parts, axis=1)


def attend(query, new_key, new_value, cache_key, cache_value, cache_len):
    count, heads, positions, depth = cache_key.shape
    scale = 1.0 / jnp.sqrt(jnp.float32(depth))
    queries = query.reshape(count, heads, depth)
    fresh_key = new_key.reshape(count, heads, depth)
    fresh_value = new_value.reshape(count, heads, depth)
    scores = (
        jnp.einsum("rhd,rhld->rhl", queries, cache_key, preferred_element_type=jnp.float32) * scale
    )
    own_score = (
        jnp.einsum("rhd,rhd->rh", queries, fresh_key, preferred_element_type=jnp.float32) * scale
    )
    valid = jnp.arange(positions, dtype=jnp.int32)[None, :] < cache_len[:, None]
    scores = jnp.where(valid[:, None, :], scores, -1e30)
    top = jnp.maximum(jnp.max(scores, axis=-1), own_score)
    expo = jnp.where(valid[:, None, :], jnp.exp(scores - top[..., None]), 0.0)
    own_expo = jnp.exp(own_score - top)
    total = jnp.sum(expo, axis=-1) + own_expo
    weights = (expo / total[..., None]).astype(jnp.bfloat16)
    own_weight = (own_expo / total).astype(jnp.bfloat16)
    mixed = jnp.einsum("rhl,rhld->rhd", weights, cache_value, preferred_element_type=jnp.float32)
    mixed = mixed + own_weight.astype(jnp.float32)[..., None] * fresh_value.astype(jnp.float32)
    return mixed.astype(jnp.bfloat16).reshape(count, heads * depth)


def body(
    query,
    new_key,
    new_value,
    cache_key,
    cache_value,
    cache_len,
    residual,
    out_weight,
    norm_gain,
    codec_weight,
    finished,
    owner,
    frames,
    snake_alpha,
    filter_weight,
    conv_bias,
):
    owners = lax.axis_size("dp")
    n_mp = lax.axis_size("mp")
    core = lax.axis_index("mp")
    tally, own = frames.shape
    span = KERNEL_TAPS // 2 * DILATION_STEP
    late = owners * CAP
    near = -(-span // CAP)
    front = round_up(late + span, ROW_TILE)
    back = round_up(span, ROW_TILE)

    wide_frames = frames.astype(jnp.float32)
    alpha_all = gather_mp(snake_alpha, 0)
    early = gather_mp(snake(wide_frames, snake_alpha), 1)
    head_frames = gather_mp(frames[:late], 1)
    before = lax.ppermute(early[tally - span :], "dp", [(i, i + 1) for i in range(owners - 1)])
    after_frames = lax.ppermute(
        head_frames[: near * CAP], "dp", [(i + 1, i) for i in range(owners - 1)]
    )
    middle = tally - front - back
    main = wide_frames[front : tally - back] + conv_bias
    for t in range(KERNEL_TAPS):
        start = front - span + t * DILATION_STEP
        main = main + jnp.dot(
            early[start : start + middle], filter_weight[t], preferred_element_type=jnp.float32
        )
    main = main.astype(jnp.bfloat16)

    attended = attend(query, new_key, new_value, cache_key, cache_value, cache_len)
    count = attended.shape[0]
    width = out_weight.shape[1]
    local_width = norm_gain.shape[0]
    residual_part = lax.dynamic_slice_in_dim(residual, core * local_width, local_width, 1)
    if n_mp == 2:
        tile = 1024
        theirs = columns_dot(
            attended, out_weight, (1 - core) * (local_width // tile), local_width, tile, jnp.bfloat16
        )
        arrived = swap(theirs)
        mine = columns_dot(
            attended, out_weight, core * (local_width // tile), local_width, tile, jnp.float32
        )
        projected = mine + arrived.astype(jnp.float32)
    else:
        term = jnp.dot(attended, out_weight, preferred_element_type=jnp.float32)
        projected = lax.psum_scatter(term, "mp", scatter_dimension=1, tiled=True)
    hidden = (residual_part.astype(jnp.float32) + projected).astype(jnp.bfloat16)
    wide = hidden.astype(jnp.float32)
    squares = jnp.sum(wide * wide, axis=-1)
    squares = squares + swap(squares) if n_mp == 2 else lax.psum(squares, "mp")
    meansq = squares / width
    normed = (wide * norm_gain.astype(jnp.float32)).astype(jnp.bfloat16)
    channels = codec_weight.shape[1]
    share = columns_dot(normed, codec_weight, 0, channels, 256, jnp.float32)
    share = (share * lax.rsqrt(meansq + 1e-05)[:, None]).astype(jnp.bfloat16)

    index = jnp.arange(count, dtype=jnp.int32)
    earlier = (
        (owner[:, None] == owner[None, :])
        & (finished[None, :] == 1)
        & (index[None, :] < index[:, None])
    )
    slot = jnp.sum(earlier.astype(jnp.int32), axis=1)
    target = owner * CAP + slot
    places = jnp.arange((owners + 1) * CAP, dtype=jnp.int32)
    onehot = ((places[:, None] == target[None, :]) & (finished[None, :] == 1)).astype(jnp.bfloat16)
    outgoing = jnp.dot(onehot, share, preferred_element_type=jnp.float32).astype(jnp.bfloat16)
    here, there = handoff(outgoing.reshape(owners + 1, CAP, channels), near)
    here = here.reshape(late, channels).astype(jnp.bfloat16).astype(jnp.float32)
    there = there.reshape(near * CAP, channels).astype(jnp.bfloat16).astype(jnp.float32)

    head_mix = head_frames.astype(jnp.float32) + here
    head_act = snake(head_mix, alpha_all)
    after = snake(after_frames.astype(jnp.float32) + there, alpha_all)[:span]
    cells_a = jnp.concatenate([before, head_act, early[late : front + span]], axis=0)
    cells_b = jnp.concatenate([early[tally - back - span :], after], axis=0)
    edges = jnp.concatenate([taps_of(cells_a, front), taps_of(cells_b, back)], axis=0)
    flat = filter_weight.reshape(KERNEL_TAPS * channels, own)
    own_mix = lax.dynamic_slice_in_dim(head_mix, core * own, own, 1)
    edge_mix = jnp.concatenate(
        [own_mix, wide_frames[late:front], wide_frames[tally - back :]], axis=0
    )
    edge = jnp.dot(edges, flat, preferred_element_type=jnp.float32) + edge_mix + conv_bias
    edge = edge.astype(jnp.bfloat16)
    audio = jnp.concatenate([edge[:front], main, edge[front:]], axis=0)
    return (hidden, audio)


MESH = pl.DeviceIdType.MESH
SIN_SQUARED = (
    1.0,
    -0.3333333134651184,
    0.04444440081715584,
    -0.003174516372382641,
    0.00014100516273174435,
    -4.2275191844964866e-06,
    8.055603473167139e-08,
)
ROUNDER = 12582912.0


def fast_snake(mix, alpha, turn, inverse):
    turns = (mix * turn + ROUNDER) - ROUNDER
    r = (mix * alpha - turns * 3.140625) - turns * 0.0009676535897932
    q = r * r
    p = SIN_SQUARED[-1] * q + SIN_SQUARED[-2]
    for c in SIN_SQUARED[-3::-1]:
        p = p * q + c
    return (mix + (q * p) * inverse).astype(jnp.bfloat16)


def iota(shape, axis):
    return lax.broadcasted_iota(jnp.int32, shape, axis)


def column_of(row, size):
    spread = jnp.broadcast_to(row, (size, size))
    return jnp.sum(
        jnp.where(iota((size, size), 0) == iota((size, size), 1), spread, 0), axis=1, keepdims=True
    )


class Plan:
    def __init__(self, query, cache_key, residual, norm_gain, codec_weight, frames):
        self.n_dp, self.n_mp = lax.axis_size("dp"), lax.axis_size("mp")
        self.rows, self.heads, self.positions, self.depth = cache_key.shape
        self.width = residual.shape[1]
        self.local = norm_gain.shape[0]
        self.channels = codec_weight.shape[1]
        self.tally, self.own = frames.shape
        self.late = self.n_dp * CAP
        self.span = KERNEL_TAPS // 2 * DILATION_STEP
        self.near = -(-self.span // CAP)
        self.pad = round_up(self.span, ROW_TILE)
        self.front = round_up(self.late + self.span, ROW_TILE)
        self.back = self.pad
        self.middle = self.tally - self.front - self.back
        self.chunk = 512
        self.steps = self.local // self.chunk
        self.slots = min(8, self.steps)
        self.group = ROW_TILE
        self.snake_rows = 32
        self.send_blocks = 4
        self.depth_in = self.heads * self.depth
        self.unroll = 4


def blocks_of(plan):
    count = 4
    unit = plan.middle // ROW_TILE
    sizes = [(unit // count + (1 if i < unit % count else 0)) * ROW_TILE for i in range(count)]
    starts = [plan.front + sum(sizes[:i]) for i in range(count)]
    return list(zip(starts, sizes))


def fused_kernel(
    P_,
    query,
    new_key,
    new_value,
    cache_key,
    cache_value,
    lens,
    residual,
    out_weight,
    gain,
    codec_weight,
    finished,
    owner,
    frames,
    alpha,
    filters,
    bias,
    hidden_out,
    audio_out,
    q_v,
    nk_v,
    nv_v,
    k_v,
    v_v,
    len_v,
    res_v,
    w_v,
    gain_raw,
    gain_v,
    cw_v,
    fin_v,
    own_v,
    fr_v,
    al_v,
    fw_v,
    bias_v,
    act_v,
    hf_v,
    af_v,
    valid_v,
    hot_v,
    att_v,
    score_v,
    p_v,
    o_v,
    out_v,
    in_v,
    hid_v,
    acc_v,
    sq_v,
    sendc_v,
    recvc_v,
    sendh_v,
    land_v,
    near_v,
    here_v,
    there_v,
    lhs_v,
    audio_v,
    s_in,
    s_k,
    s_v,
    s_w,
    s_cw,
    s_fw,
    s_out,
    x_alpha,
    x_head,
    x_early,
    x_before,
    x_after,
    x_part,
    x_codec,
    send_a,
    recv_a,
    send_b,
    recv_b,
):
    n_dp, n_mp = P_.n_dp, P_.n_mp
    count = n_dp * n_mp
    rows, heads, positions, depth = P_.rows, P_.heads, P_.positions, P_.depth
    chunk, steps, slots = P_.chunk, P_.steps, P_.slots
    own, channels, tally, pad = P_.own, P_.channels, P_.tally, P_.pad
    late, span, front, back = P_.late, P_.span, P_.front, P_.back
    dp = lax.axis_index("dp")
    core = lax.axis_index("mp")
    me = dp * n_mp + core
    other = 1 - core
    mine_cols = pl.ds(pl.multiple_of(core * own, own), own)
    local_cols = pl.ds(pl.multiple_of(core * P_.local, P_.local), P_.local)

    def local(src, dst, sem):
        return pltpu.make_async_copy(src, dst, sem)

    def remote(src, dst, send, recv, to_dp, to_mp):
        return pltpu.make_async_remote_copy(
            src_ref=src,
            dst_ref=dst,
            send_sem=send,
            recv_sem=recv,
            device_id=(to_dp, to_mp),
            device_id_type=MESH,
        )

    frames_in = local(frames, fr_v, s_in.at[0])
    alpha_in = local(alpha, al_v.at[:, mine_cols], s_in.at[1])
    lens_in = local(lens, len_v, s_in.at[2])
    fin_in = local(finished, fin_v, s_in.at[3])
    own_in = local(owner, own_v, s_in.at[4])
    q_in = local(query, q_v, s_in.at[5])
    nk_in = local(new_key, nk_v, s_in.at[6])
    nv_in = local(new_value, nv_v, s_in.at[7])
    res_in = local(residual.at[:, local_cols], res_v, s_in.at[8])
    gain_in = local(gain, gain_raw, s_in.at[9])
    bias_in = local(bias, bias_v, s_in.at[10])

    def key_in(h):
        return local(cache_key.at[:, h], k_v.at[h], s_k.at[h])

    def value_in(h):
        return local(cache_value.at[:, h], v_v.at[h], s_v.at[h])

    def weight_in(i):
        begin = lax.select(i < steps, other * P_.local, core * P_.local) + lax.rem(i, steps) * chunk
        return local(
            out_weight.at[:, pl.ds(pl.multiple_of(begin, chunk), chunk)],
            w_v.at[lax.rem(i, slots)],
            s_w.at[lax.rem(i, slots)],
        )

    def codec_in(i):
        part = pl.ds(pl.multiple_of(i * chunk, chunk), chunk)
        return local(codec_weight.at[part, :], cw_v.at[part, :], s_cw.at[i])

    def filter_in(t):
        part = pl.ds(pl.multiple_of(t * channels, channels), channels)
        return local(filters.at[part, :], fw_v.at[part, :], s_fw.at[t])

    for copy in (frames_in, alpha_in, lens_in, fin_in, own_in, q_in, nk_in, nv_in):
        copy.start()

    def start_cache(h, carry):
        key_in(h).start()
        value_in(h).start()
        return carry

    lax.fori_loop(0, heads, start_cache, 0)

    barrier = pltpu.get_barrier_semaphore()

    def place(step):
        peer = lax.rem(me + step, count)
        return peer, peer // n_mp, lax.rem(peer, n_mp)

    def greet(step, carry):
        _, pd, pm = place(step)
        pl.semaphore_signal(barrier, inc=1, device_id=(pd, pm), device_id_type=MESH)
        return carry

    lax.fori_loop(1, count, greet, 0)

    def start_weight(i, carry):
        weight_in(i).start()
        return carry

    lax.fori_loop(0, slots, start_weight, 0)
    for copy in (res_in, gain_in, bias_in):
        copy.start()

    for copy in (alpha_in, frames_in):
        copy.wait()

    my_alpha = al_v[:, mine_cols]
    my_turn = my_alpha * 0.3183098861837907
    my_inverse = 1.0 / my_alpha

    def snake_step(i, carry):
        part = pl.ds(pl.multiple_of(i * P_.snake_rows, P_.snake_rows), P_.snake_rows)
        where_to = pl.ds(pl.multiple_of(pad + i * P_.snake_rows, ROW_TILE), P_.snake_rows)
        act_v[where_to, mine_cols] = fast_snake(
            fr_v[part, :].astype(jnp.float32), my_alpha, my_turn, my_inverse
        )
        return carry

    lax.fori_loop(0, tally // P_.snake_rows, snake_step, 0)

    pl.semaphore_wait(barrier, count - 1)

    alpha_x = remote(
        alpha, al_v.at[:, mine_cols], x_alpha.at[0], x_alpha.at[1], dp, other
    )
    alpha_x.start()
    head_x = remote(frames.at[0:late], hf_v, x_head.at[0], x_head.at[1], dp, other)
    head_x.start()

    block = tally // P_.send_blocks

    def early_x(b):
        part = pl.ds(pl.multiple_of(pad + b * block, ROW_TILE), block)
        return remote(
            act_v.at[part, mine_cols],
            act_v.at[part, mine_cols],
            x_early.at[0, b],
            x_early.at[1, b],
            dp,
            other,
        )

    def before_x(m, to_dp, sender):
        cols = pl.ds(pl.multiple_of(sender * own, own), own)
        return remote(
            act_v.at[tally : tally + pad, mine_cols],
            act_v.at[0:pad, cols],
            x_before.at[0, m],
            x_before.at[1, sender],
            to_dp,
            m,
        )

    def after_x(m, to_dp, sender):
        return remote(
            frames.at[0:pad],
            af_v.at[sender],
            x_after.at[0, m],
            x_after.at[1, sender],
            to_dp,
            m,
        )

    for b in range(P_.send_blocks):
        early_x(b).start()

    @pl.when(dp < n_dp - 1)
    def _():
        for m in range(n_mp):
            before_x(m, dp + 1, core).start()

    @pl.when(dp > 0)
    def _():
        for m in range(n_mp):
            after_x(m, dp - 1, core).start()

    for copy in (lens_in, fin_in, own_in):
        copy.wait()

    length = column_of(len_v[...], rows)
    lanes = P_.group * positions
    lane = iota((rows, lanes), 1)
    line = lax.rem(iota((rows, lanes), 0), P_.group)
    valid = (lane // positions == line) & (lax.rem(lane, positions) < length)
    valid_v[...] = jnp.where(valid, 0.0, -1e30)

    owner_row, done_row = own_v[...], fin_v[...]
    owner_col, done_col = column_of(owner_row, rows), column_of(done_row, rows)
    earlier = (
        (owner_col == owner_row)
        & (done_col == 1)
        & (iota((rows, rows), 0) < iota((rows, rows), 1))
    )
    slot = jnp.sum(jnp.where(earlier, 1, 0), axis=0, keepdims=True)
    target = jnp.where(done_row == 1, owner_row * CAP + slot, -1)
    hot_v[...] = jnp.where(iota((late, rows), 0) == target, 1.0, 0.0).astype(jnp.bfloat16)

    for copy in (q_in, nk_in, nv_in):
        copy.wait()
    scale = 1.0 / jnp.sqrt(jnp.float32(depth))

    def score_step(j, carry):
        for u in range(P_.unroll):
            key_in(j * P_.unroll + u).wait()
        for u in range(P_.unroll):
            h = j * P_.unroll + u
            cols = pl.ds(pl.multiple_of(h * depth, depth), depth)
            for g in range(rows // P_.group):
                part = slice(g * P_.group, (g + 1) * P_.group)
                keys = k_v[h, part].reshape(lanes, depth)
                score_v[h, part, :] = lax.dot_general(
                    q_v[part, cols],
                    keys,
                    (((1,), (1,)), ((), ())),
                    preferred_element_type=jnp.float32,
                )
        return carry

    lax.fori_loop(0, heads // P_.unroll, score_step, 0)

    def soft_step(h, carry):
        cols = pl.ds(pl.multiple_of(h * depth, depth), depth)
        s = jnp.where(valid_v[...] < 0.0, -1e30, score_v[h] * scale)
        mine = q_v[:, cols].astype(jnp.float32) * nk_v[:, cols].astype(jnp.float32)
        mine = jnp.sum(mine, axis=1, keepdims=True) * scale
        top = jnp.maximum(jnp.max(s, axis=1, keepdims=True), mine)
        expo = jnp.exp(s - top)
        mine_expo = jnp.exp(mine - top)
        share = 1.0 / (jnp.sum(expo, axis=1, keepdims=True) + mine_expo)
        p_v[h] = (expo * share).astype(jnp.bfloat16)
        mine_weight = (mine_expo * share).astype(jnp.bfloat16).astype(jnp.float32)
        o_v[h] = mine_weight * nv_v[:, cols].astype(jnp.float32)
        return carry

    lax.fori_loop(0, heads, soft_step, 0)

    def value_step(j, carry):
        for u in range(P_.unroll):
            value_in(j * P_.unroll + u).wait()
        for u in range(P_.unroll):
            h = j * P_.unroll + u
            cols = pl.ds(pl.multiple_of(h * depth, depth), depth)
            for g in range(rows // P_.group):
                part = slice(g * P_.group, (g + 1) * P_.group)
                values = v_v[h, part].reshape(lanes, depth)
                mixed = jnp.dot(p_v[h, part, :], values, preferred_element_type=jnp.float32)
                att_v[part, cols] = (mixed + o_v[h, part, :]).astype(jnp.bfloat16)
        return carry

    lax.fori_loop(0, heads // P_.unroll, value_step, 0)

    def part_x(i):
        return remote(out_v.at[i], in_v.at[i], x_part.at[0, i], x_part.at[1, i], dp, other)

    def their_step(i, carry):
        weight_in(i).wait()
        out_v[i] = jnp.dot(
            att_v[...], w_v[lax.rem(i, slots)], preferred_element_type=jnp.float32
        ).astype(jnp.bfloat16)
        weight_in(i + slots).start()
        codec_in(i).start()

        @pl.when(i > 0)
        def _():
            part_x(i - 1).start()

        return carry

    lax.fori_loop(0, steps, their_step, 0)

    def start_filter(t, carry):
        filter_in(t).start()
        return carry

    lax.fori_loop(0, KERNEL_TAPS, start_filter, 0)
    for copy in (res_in, gain_in, bias_in):
        copy.wait()
    gains = gain_raw[...].astype(jnp.float32)
    for k in range(P_.local // 128):
        gain_v[:, k * 128 : (k + 1) * 128] = gains[k : k + 1]
    acc_v[...] = jnp.zeros_like(acc_v)
    sq_v[...] = jnp.zeros_like(sq_v)

    def mine_step(i, carry):
        weight_in(i + steps).wait()
        total = jnp.dot(att_v[...], w_v[lax.rem(i, slots)], preferred_element_type=jnp.float32)

        @pl.when(i == 0)
        def _():
            part_x(steps - 1).start()

        @pl.when(i + slots < steps)
        def _():
            weight_in(i + steps + slots).start()

        part_x(i).wait_recv()
        cols = pl.ds(pl.multiple_of(i * chunk, chunk), chunk)
        total = total + in_v[i].astype(jnp.float32) + res_v[:, cols].astype(jnp.float32)
        hidden = total.astype(jnp.bfloat16)
        hid_v[:, cols] = hidden
        wide = hidden.astype(jnp.float32)
        square = wide * wide
        squares = square[:, :128]
        for k in range(1, chunk // 128):
            squares = squares + square[:, k * 128 : (k + 1) * 128]
        sq_v[...] += squares
        normed = (wide * gain_v[:, cols]).astype(jnp.bfloat16)
        codec_in(i).wait()
        acc_v[...] += jnp.dot(normed, cw_v[cols, :], preferred_element_type=jnp.float32)
        return carry

    lax.fori_loop(0, steps, mine_step, 0)
    hidden_x = local(hid_v, hidden_out, s_out.at[0])
    hidden_x.start()

    other_cols = pl.ds(pl.multiple_of(other * own, own), own)
    sendc_v[:, :own] = acc_v[:, other_cols]
    sendc_v[:, own:] = sq_v[...]
    codec_x = remote(sendc_v, recvc_v, x_codec.at[0], x_codec.at[1], dp, other)
    codec_x.start()

    def wait_filter(t, carry):
        filter_in(t).wait()
        return carry

    lax.fori_loop(0, KERNEL_TAPS, wait_filter, 0)
    for b in range(P_.send_blocks):
        early_x(b).wait_recv()

    def conv_block(index):
        begin, size = blocks_of(P_)[index]
        for t in range(KERNEL_TAPS):
            at = pad + begin - span + t * DILATION_STEP
            lhs_v[:size, t * channels : (t + 1) * channels] = act_v[at : at + size, :]
        audio_v[begin : begin + size, :] = (
            jnp.dot(lhs_v[:size, :], fw_v[...], preferred_element_type=jnp.float32)
            + fr_v[begin : begin + size, :].astype(jnp.float32)
            + bias_v[...]
        ).astype(jnp.bfloat16)

    conv_block(0)
    codec_x.wait_recv()
    square = jnp.sum(sq_v[...] + recvc_v[:, own:], axis=1, keepdims=True)
    latent = (
        (acc_v[:, mine_cols] + recvc_v[:, :own]) * lax.rsqrt(square / P_.width + 1e-05)
    ).astype(jnp.bfloat16)
    outgoing = jnp.dot(hot_v[...], latent, preferred_element_type=jnp.float32)
    for d in range(n_dp):
        sendh_v[d] = outgoing[d * CAP : (d + 1) * CAP].astype(jnp.bfloat16)

    def copy_a(pd, pm, src_dp, src_mp, send, recv):
        return remote(
            sendh_v.at[pd], land_v.at[src_mp, src_dp], send_a.at[send], recv_a.at[recv], pd, pm
        )

    def copy_b(pd, pm, src_dp, src_mp, send, recv):
        return remote(
            sendh_v.at[pd + 1], near_v.at[src_mp, src_dp], send_b.at[send], recv_b.at[recv], pd, pm
        )

    def send_near(step, carry):
        peer, pd, pm = place(step)

        @pl.when(pd < n_dp - 1)
        def _():
            copy_b(pd, pm, dp, core, peer, me).start()

        return carry

    @pl.when(dp < P_.near)
    def _():
        lax.fori_loop(1, count, send_near, 0)

    def send(step, carry):
        peer, pd, pm = place(step)
        copy_a(pd, pm, dp, core, peer, me).start()
        return carry

    lax.fori_loop(1, count, send, 0)
    land_v[core, dp] = sendh_v[dp]

    @pl.when(dp < P_.near)
    def _():
        near_v[core, dp] = sendh_v[lax.rem(dp + 1, n_dp)]

    for index in range(1, len(blocks_of(P_))):
        conv_block(index)
    middle_x = local(
        audio_v.at[front : tally - back], audio_out.at[front : tally - back], s_out.at[1]
    )
    middle_x.start()

    alpha_x.wait_recv()
    head_x.wait_recv()

    def finish(step, carry):
        peer, pd, pm = place(step)
        copy_a(pd, pm, pd, pm, peer, peer).wait_recv()
        return carry

    lax.fori_loop(1, count, finish, 0)
    for s in range(n_dp):
        for m in range(n_mp):
            here_v[s * CAP : (s + 1) * CAP, m * own : (m + 1) * own] = land_v[m, s].astype(
                jnp.float32
            )
    for b in range(P_.send_blocks):
        early_x(b).wait_send()
    hf = hf_v[...].astype(jnp.float32)
    mf = fr_v[0:late, :].astype(jnp.float32)

    all_alpha = al_v[...]
    all_turn = all_alpha * 0.3183098861837907
    all_inverse = 1.0 / all_alpha
    here_v[:, mine_cols] += mf
    here_v[:, other_cols] += hf
    act_v[pad : pad + late, :] = fast_snake(here_v[...], all_alpha, all_turn, all_inverse)

    @pl.when(dp < n_dp - 1)
    def _():
        for m in range(n_mp):
            after_x(0, 0, m).wait_recv()

        def take_near(sender, carry):
            @pl.when(sender != me)
            def _():
                copy_b(0, 0, sender // n_mp, lax.rem(sender, n_mp), 0, sender).wait_recv()

            return carry

        lax.fori_loop(0, P_.near * n_mp, take_near, 0)
        for m in range(n_mp):
            there_v[:, m * own : (m + 1) * own] = af_v[m].astype(jnp.float32)
            for s in range(P_.near):
                there_v[s * CAP : (s + 1) * CAP, m * own : (m + 1) * own] += near_v[m, s].astype(
                    jnp.float32
                )
        act_v[pad + tally :, :] = fast_snake(there_v[...], all_alpha, all_turn, all_inverse)

    @pl.when(dp == n_dp - 1)
    def _():
        act_v[pad + tally :, :] = jnp.zeros((pad, channels), jnp.bfloat16)

    @pl.when(dp > 0)
    def _():
        for m in range(n_mp):
            before_x(0, 0, m).wait_recv()

    @pl.when(dp == 0)
    def _():
        act_v[0:pad, :] = jnp.zeros((pad, channels), jnp.bfloat16)

    for t in range(KERNEL_TAPS):
        cols = slice(t * channels, (t + 1) * channels)
        at = pad - span + t * DILATION_STEP
        lhs_v[:front, cols] = act_v[at : at + front, :]
        at = at + tally - back
        lhs_v[front : front + back, cols] = act_v[at : at + back, :]
    edge = (
        jnp.dot(lhs_v[: front + back, :], fw_v[...], preferred_element_type=jnp.float32)
        + bias_v[...]
    )
    audio_v[:late, :] = (edge[:late] + here_v[:, mine_cols]).astype(jnp.bfloat16)
    audio_v[late:front, :] = (edge[late:front] + fr_v[late:front, :].astype(jnp.float32)).astype(
        jnp.bfloat16
    )
    audio_v[tally - back :, :] = (edge[front:] + fr_v[tally - back :, :].astype(jnp.float32)).astype(
        jnp.bfloat16
    )
    first_x = local(audio_v.at[:front], audio_out.at[:front], s_out.at[2])
    last_x = local(audio_v.at[tally - back :], audio_out.at[tally - back :], s_out.at[3])
    first_x.start()
    last_x.start()

    alpha_x.wait_send()
    head_x.wait_send()

    @pl.when(dp < n_dp - 1)
    def _():
        for m in range(n_mp):
            before_x(m, 0, core).wait_send()

    @pl.when(dp > 0)
    def _():
        for m in range(n_mp):
            after_x(m, 0, core).wait_send()

    def part_sent(i, carry):
        part_x(i).wait_send()
        return carry

    lax.fori_loop(0, steps, part_sent, 0)
    codec_x.wait_send()

    def sent(step, carry):
        peer, pd, pm = place(step)
        copy_a(pd, pm, dp, core, peer, me).wait_send()
        return carry

    lax.fori_loop(1, count, sent, 0)

    def sent_near(step, carry):
        peer, pd, pm = place(step)

        @pl.when(pd < n_dp - 1)
        def _():
            copy_b(pd, pm, dp, core, peer, me).wait_send()

        return carry

    @pl.when(dp < P_.near)
    def _():
        lax.fori_loop(1, count, sent_near, 0)

    hidden_x.wait()
    middle_x.wait()
    first_x.wait()
    last_x.wait()


def fused(
    query,
    new_key,
    new_value,
    cache_key,
    cache_value,
    cache_len,
    residual,
    out_weight,
    norm_gain,
    codec_weight,
    finished,
    owner,
    frames,
    snake_alpha,
    filter_weight,
    conv_bias,
):
    plan = Plan(query, cache_key, residual, norm_gain, codec_weight, frames)
    n_dp, n_mp = plan.n_dp, plan.n_mp
    count = n_dp * n_mp
    bf, f32, i32 = jnp.bfloat16, jnp.float32, jnp.int32
    vm = pltpu.VMEM
    dma = pltpu.SemaphoreType.DMA
    rows, own, channels, tally = plan.rows, plan.own, plan.channels, plan.tally
    taps = KERNEL_TAPS * channels
    biggest = max([size for _, size in blocks_of(plan)] + [plan.front + plan.back])
    scratch = [
        vm(query.shape, bf),
        vm(query.shape, bf),
        vm(query.shape, bf),
        vm((plan.heads, rows, plan.positions, plan.depth), bf),
        vm((plan.heads, rows, plan.positions, plan.depth), bf),
        vm((1, rows), i32),
        vm((rows, plan.local), bf),
        vm((plan.slots, plan.depth_in, plan.chunk), bf),
        vm((plan.local // 128, 128), bf),
        vm((1, plan.local), f32),
        vm((plan.local, channels), bf),
        vm((1, rows), i32),
        vm((1, rows), i32),
        vm((tally, own), bf),
        vm((1, channels), f32),
        vm((taps, own), bf),
        vm((1, own), f32),
        vm((tally + 2 * plan.pad, channels), bf),
        vm((plan.late, own), bf),
        vm((n_mp, plan.pad, own), bf),
        vm((rows, plan.group * plan.positions), f32),
        vm((plan.late, rows), bf),
        vm((rows, plan.depth_in), bf),
        vm((plan.heads, rows, plan.group * plan.positions), f32),
        vm((plan.heads, rows, plan.group * plan.positions), bf),
        vm((plan.heads, rows, plan.depth), f32),
        vm((plan.steps, rows, plan.chunk), bf),
        vm((plan.steps, rows, plan.chunk), bf),
        vm((rows, plan.local), bf),
        vm((rows, channels), f32),
        vm((rows, 128), f32),
        vm((rows, own + 128), f32),
        vm((rows, own + 128), f32),
        vm((n_dp, CAP, own), bf),
        vm((n_mp, n_dp, CAP, own), bf),
        vm((n_mp, plan.near, CAP, own), bf),
        vm((plan.late, channels), f32),
        vm((plan.pad, channels), f32),
        vm((biggest, taps), bf),
        vm((tally, own), bf),
        dma((11,)),
        dma((plan.heads,)),
        dma((plan.heads,)),
        dma((plan.slots,)),
        dma((plan.steps,)),
        dma((KERNEL_TAPS,)),
        dma((4,)),
        dma((2,)),
        dma((2,)),
        dma((2, plan.send_blocks)),
        dma((2, n_mp)),
        dma((2, n_mp)),
        dma((2, plan.steps)),
        dma((2,)),
        dma((count,)),
        dma((count,)),
        dma((count,)),
        dma((plan.near * n_mp,)),
    ]
    anywhere = pl.BlockSpec(memory_space=pl.ANY)
    return pl.pallas_call(
        functools.partial(fused_kernel, plan),
        out_shape=(
            jax.ShapeDtypeStruct((rows, plan.local), bf),
            jax.ShapeDtypeStruct((tally, own), bf),
        ),
        in_specs=[anywhere] * 16,
        out_specs=(anywhere, anywhere),
        scratch_shapes=scratch,
        compiler_params=pltpu.CompilerParams(
            collective_id=1, has_side_effects=True, vmem_limit_bytes=VMEM_BYTES
        ),
    )(
        query,
        new_key,
        new_value,
        cache_key,
        cache_value,
        cache_len.reshape(1, -1),
        residual,
        out_weight,
        norm_gain.reshape(-1, 128),
        codec_weight,
        finished.reshape(1, -1),
        owner.reshape(1, -1),
        frames,
        snake_alpha.reshape(1, -1),
        filter_weight.reshape(taps, own),
        conv_bias.reshape(1, -1),
    )


VMEM_BYTES = 66 * 1000 * 1000


def step(*args):
    return fused(*args) if lax.axis_size("mp") == 2 else body(*args)


def solution(mesh):
    placed = (
        P("dp", "mp"),
        P("dp", "mp"),
        P("dp", "mp"),
        P("dp", "mp", None, None),
        P("dp", "mp", None, None),
        P("dp"),
        P("dp", None),
        P("mp", None),
        P("mp"),
        P("mp", None),
        P("dp"),
        P("dp"),
        P("dp", "mp"),
        P("mp"),
        P(None, None, "mp"),
        P("mp"),
    )
    return jax.shard_map(
        step, mesh=mesh, in_specs=placed, out_specs=(P("dp", "mp"), P("dp", "mp")), check_vma=False
    )
```

```python
import functools
import jax
import jax.numpy as jnp
from jax import lax
from jax.experimental import pallas as pl
from jax.experimental.pallas import tpu as pltpu
from jax.sharding import PartitionSpec as P

KERNEL_TAPS = 7
DILATION_STEP = 3
CAP = 4
ROW_TILE = 16


def swap(x):
    return lax.ppermute(x, "mp", [(0, 1), (1, 0)])


def gather_mp(x, axis):
    if lax.axis_size("mp") != 2:
        return lax.all_gather(x, "mp", axis=axis, tiled=True)
    other = swap(x)
    first = lax.axis_index("mp") == 0
    return jnp.concatenate([jnp.where(first, x, other), jnp.where(first, other, x)], axis=axis)


def sin_squared(x):
    turns = jnp.round(x * 0.3183098861837907)
    r = (x - turns * 3.140625) - turns * 0.0009676535897932
    q = r * r
    p = -2.5052108e-08 + q * 1.6059044e-10
    p = 2.7557319e-06 + q * p
    p = -1.9841270e-04 + q * p
    p = 8.3333333e-03 + q * p
    p = -1.6666667e-01 + q * p
    sine = r + r * (q * p)
    return sine * sine


def snake(mix, alpha):
    return (mix + sin_squared(alpha * mix) / alpha).astype(jnp.bfloat16)


def columns_kernel(start_ref, x_ref, w_ref, o_ref):
    del start_ref
    o_ref[...] = jnp.dot(x_ref[...], w_ref[...], preferred_element_type=jnp.float32).astype(
        o_ref.dtype
    )


def columns_dot(x, w, start, width, tile, dtype):
    rows, depth = x.shape
    return pl.pallas_call(
        columns_kernel,
        out_shape=jax.ShapeDtypeStruct((rows, width), dtype),
        grid_spec=pltpu.PrefetchScalarGridSpec(
            num_scalar_prefetch=1,
            grid=(width // tile,),
            in_specs=[
                pl.BlockSpec((rows, depth), lambda j, s: (0, 0)),
                pl.BlockSpec((depth, tile), lambda j, s: (0, s[0] + j)),
            ],
            out_specs=pl.BlockSpec((rows, tile), lambda j, s: (0, j)),
        ),
        compiler_params=pltpu.CompilerParams(vmem_limit_bytes=28 * 1024 * 1024),
        cost_estimate=pl.CostEstimate(
            flops=2 * rows * depth * width, bytes_accessed=2 * depth * width, transcendentals=0
        ),
    )(jnp.full((1,), start, jnp.int32), x, w)


def handoff_kernel(
    n_dp, n_mp, near, out_ref, a_ref, b_ref, land_a, land_b, send_a, recv_a, send_b, recv_b
):
    dp = lax.axis_index("dp")
    mp = lax.axis_index("mp")
    count = n_dp * n_mp
    me = dp * n_mp + mp
    barrier = pltpu.get_barrier_semaphore()

    def place(step):
        peer = lax.rem(me + step, count)
        return peer, peer // n_mp, lax.rem(peer, n_mp)

    def greet(step, carry):
        _, pd, pm = place(step)
        pl.semaphore_signal(
            barrier, inc=1, device_id=(pd, pm), device_id_type=pl.DeviceIdType.MESH
        )
        return carry

    lax.fori_loop(1, count, greet, 0)
    pl.semaphore_wait(barrier, count - 1)

    def copy_a(pd, pm, send, recv):
        return pltpu.make_async_remote_copy(
            src_ref=out_ref.at[pd],
            dst_ref=land_a.at[me],
            send_sem=send_a.at[send],
            recv_sem=recv_a.at[recv],
            device_id=(pd, pm),
            device_id_type=pl.DeviceIdType.MESH,
        )

    def copy_b(slot, pd, pm, send, recv):
        return pltpu.make_async_remote_copy(
            src_ref=out_ref.at[pd + 1],
            dst_ref=land_b.at[slot],
            send_sem=send_b.at[send],
            recv_sem=recv_b.at[recv],
            device_id=(pd, pm),
            device_id_type=pl.DeviceIdType.MESH,
        )

    def send(step, carry):
        peer, pd, pm = place(step)
        copy_a(pd, pm, peer, me).start()
        return carry

    def send_near(step, carry):
        peer, pd, pm = place(step)
        copy_b(me, pd, pm, peer, me).start()
        return carry

    @pl.when(dp < near)
    def _():
        lax.fori_loop(1, count, send_near, 0)

    lax.fori_loop(1, count, send, 0)
    land_a[me] = out_ref[dp]

    @pl.when(dp < near)
    def _():
        land_b[me] = out_ref[dp + 1]

    def finish(step, carry):
        peer, pd, pm = place(step)
        copy = copy_a(pd, pm, peer, peer)
        copy.wait_recv()
        copy.wait_send()
        return carry

    def finish_near(step, carry):
        peer, pd, pm = place(step)
        copy_b(me, pd, pm, peer, me).wait_send()
        return carry

    def take_near(sender, carry):
        @pl.when(sender != me)
        def _():
            copy_b(sender, 0, 0, sender, sender).wait_recv()

        return carry

    lax.fori_loop(1, count, finish, 0)

    @pl.when(dp < near)
    def _():
        lax.fori_loop(1, count, finish_near, 0)

    lax.fori_loop(0, near * n_mp, take_near, 0)

    def total_of(land, first):
        total = land[first].astype(jnp.float32)
        for m in range(1, n_mp):
            total = total + land[first + m].astype(jnp.float32)
        return total

    def put(d, carry):
        a_ref[d] = total_of(land_a, d * n_mp)
        return carry

    lax.fori_loop(0, n_dp, put, 0)
    for d in range(near):
        b_ref[d] = total_of(land_b, d * n_mp)


def handoff(outgoing, near):
    n_dp, n_mp = lax.axis_size("dp"), lax.axis_size("mp")
    count = n_dp * n_mp
    _, cap, width = outgoing.shape
    vmem = pl.BlockSpec(memory_space=pltpu.VMEM)
    return pl.pallas_call(
        functools.partial(handoff_kernel, n_dp, n_mp, near),
        out_shape=(
            jax.ShapeDtypeStruct((n_dp, cap, width), jnp.float32),
            jax.ShapeDtypeStruct((near, cap, width), jnp.float32),
        ),
        in_specs=[vmem],
        out_specs=(vmem, vmem),
        scratch_shapes=[
            pltpu.VMEM((count, cap, width), jnp.bfloat16),
            pltpu.VMEM((near * n_mp, cap, width), jnp.bfloat16),
            pltpu.SemaphoreType.DMA((count,)),
            pltpu.SemaphoreType.DMA((count,)),
            pltpu.SemaphoreType.DMA((count,)),
            pltpu.SemaphoreType.DMA((near * n_mp,)),
        ],
        compiler_params=pltpu.CompilerParams(
            collective_id=0, has_side_effects=True, vmem_limit_bytes=16 * 1024 * 1024
        ),
    )(outgoing)


def round_up(n, tile):
    return -(-n // tile) * tile


def taps_of(cells, rows):
    parts = [cells[t * DILATION_STEP : t * DILATION_STEP + rows] for t in range(KERNEL_TAPS)]
    return jnp.concatenate(parts, axis=1)


def attend(query, new_key, new_value, cache_key, cache_value, cache_len):
    count, heads, positions, depth = cache_key.shape
    scale = 1.0 / jnp.sqrt(jnp.float32(depth))
    queries = query.reshape(count, heads, depth)
    fresh_key = new_key.reshape(count, heads, depth)
    fresh_value = new_value.reshape(count, heads, depth)
    scores = (
        jnp.einsum("rhd,rhld->rhl", queries, cache_key, preferred_element_type=jnp.float32) * scale
    )
    own_score = (
        jnp.einsum("rhd,rhd->rh", queries, fresh_key, preferred_element_type=jnp.float32) * scale
    )
    valid = jnp.arange(positions, dtype=jnp.int32)[None, :] < cache_len[:, None]
    scores = jnp.where(valid[:, None, :], scores, -1e30)
    top = jnp.maximum(jnp.max(scores, axis=-1), own_score)
    expo = jnp.where(valid[:, None, :], jnp.exp(scores - top[..., None]), 0.0)
    own_expo = jnp.exp(own_score - top)
    total = jnp.sum(expo, axis=-1) + own_expo
    weights = (expo / total[..., None]).astype(jnp.bfloat16)
    own_weight = (own_expo / total).astype(jnp.bfloat16)
    mixed = jnp.einsum("rhl,rhld->rhd", weights, cache_value, preferred_element_type=jnp.float32)
    mixed = mixed + own_weight.astype(jnp.float32)[..., None] * fresh_value.astype(jnp.float32)
    return mixed.astype(jnp.bfloat16).reshape(count, heads * depth)


def body(
    query,
    new_key,
    new_value,
    cache_key,
    cache_value,
    cache_len,
    residual,
    out_weight,
    norm_gain,
    codec_weight,
    finished,
    owner,
    frames,
    snake_alpha,
    filter_weight,
    conv_bias,
):
    owners = lax.axis_size("dp")
    n_mp = lax.axis_size("mp")
    core = lax.axis_index("mp")
    tally, own = frames.shape
    span = KERNEL_TAPS // 2 * DILATION_STEP
    late = owners * CAP
    near = -(-span // CAP)
    front = round_up(late + span, ROW_TILE)
    back = round_up(span, ROW_TILE)

    wide_frames = frames.astype(jnp.float32)
    alpha_all = gather_mp(snake_alpha, 0)
    early = gather_mp(snake(wide_frames, snake_alpha), 1)
    head_frames = gather_mp(frames[:late], 1)
    before = lax.ppermute(early[tally - span :], "dp", [(i, i + 1) for i in range(owners - 1)])
    after_frames = lax.ppermute(
        head_frames[: near * CAP], "dp", [(i + 1, i) for i in range(owners - 1)]
    )
    middle = tally - front - back
    main = wide_frames[front : tally - back] + conv_bias
    for t in range(KERNEL_TAPS):
        start = front - span + t * DILATION_STEP
        main = main + jnp.dot(
            early[start : start + middle], filter_weight[t], preferred_element_type=jnp.float32
        )
    main = main.astype(jnp.bfloat16)

    attended = attend(query, new_key, new_value, cache_key, cache_value, cache_len)
    count = attended.shape[0]
    width = out_weight.shape[1]
    local_width = norm_gain.shape[0]
    residual_part = lax.dynamic_slice_in_dim(residual, core * local_width, local_width, 1)
    if n_mp == 2:
        tile = 1024
        theirs = columns_dot(
            attended, out_weight, (1 - core) * (local_width // tile), local_width, tile, jnp.bfloat16
        )
        arrived = swap(theirs)
        mine = columns_dot(
            attended, out_weight, core * (local_width // tile), local_width, tile, jnp.float32
        )
        projected = mine + arrived.astype(jnp.float32)
    else:
        term = jnp.dot(attended, out_weight, preferred_element_type=jnp.float32)
        projected = lax.psum_scatter(term, "mp", scatter_dimension=1, tiled=True)
    hidden = (residual_part.astype(jnp.float32) + projected).astype(jnp.bfloat16)
    wide = hidden.astype(jnp.float32)
    squares = jnp.sum(wide * wide, axis=-1)
    squares = squares + swap(squares) if n_mp == 2 else lax.psum(squares, "mp")
    meansq = squares / width
    normed = (wide * norm_gain.astype(jnp.float32)).astype(jnp.bfloat16)
    channels = codec_weight.shape[1]
    share = columns_dot(normed, codec_weight, 0, channels, 256, jnp.float32)
    share = (share * lax.rsqrt(meansq + 1e-05)[:, None]).astype(jnp.bfloat16)

    index = jnp.arange(count, dtype=jnp.int32)
    earlier = (
        (owner[:, None] == owner[None, :])
        & (finished[None, :] == 1)
        & (index[None, :] < index[:, None])
    )
    slot = jnp.sum(earlier.astype(jnp.int32), axis=1)
    target = owner * CAP + slot
    places = jnp.arange((owners + 1) * CAP, dtype=jnp.int32)
    onehot = ((places[:, None] == target[None, :]) & (finished[None, :] == 1)).astype(jnp.bfloat16)
    outgoing = jnp.dot(onehot, share, preferred_element_type=jnp.float32).astype(jnp.bfloat16)
    here, there = handoff(outgoing.reshape(owners + 1, CAP, channels), near)
    here = here.reshape(late, channels).astype(jnp.bfloat16).astype(jnp.float32)
    there = there.reshape(near * CAP, channels).astype(jnp.bfloat16).astype(jnp.float32)

    head_mix = head_frames.astype(jnp.float32) + here
    head_act = snake(head_mix, alpha_all)
    after = snake(after_frames.astype(jnp.float32) + there, alpha_all)[:span]
    cells_a = jnp.concatenate([before, head_act, early[late : front + span]], axis=0)
    cells_b = jnp.concatenate([early[tally - back - span :], after], axis=0)
    edges = jnp.concatenate([taps_of(cells_a, front), taps_of(cells_b, back)], axis=0)
    flat = filter_weight.reshape(KERNEL_TAPS * channels, own)
    own_mix = lax.dynamic_slice_in_dim(head_mix, core * own, own, 1)
    edge_mix = jnp.concatenate(
        [own_mix, wide_frames[late:front], wide_frames[tally - back :]], axis=0
    )
    edge = jnp.dot(edges, flat, preferred_element_type=jnp.float32) + edge_mix + conv_bias
    edge = edge.astype(jnp.bfloat16)
    audio = jnp.concatenate([edge[:front], main, edge[front:]], axis=0)
    return (hidden, audio)


MESH = pl.DeviceIdType.MESH
SIN_SQUARED = (
    1.0,
    -0.3333333134651184,
    0.04444440081715584,
    -0.003174516372382641,
    0.00014100516273174435,
    -4.2275191844964866e-06,
    8.055603473167139e-08,
)
ROUNDER = 12582912.0


def fast_snake(mix, alpha, turn, inverse):
    turns = (mix * turn + ROUNDER) - ROUNDER
    r = (mix * alpha - turns * 3.140625) - turns * 0.0009676535897932
    q = r * r
    p = SIN_SQUARED[-1] * q + SIN_SQUARED[-2]
    for c in SIN_SQUARED[-3::-1]:
        p = p * q + c
    return (mix + (q * p) * inverse).astype(jnp.bfloat16)


def iota(shape, axis):
    return lax.broadcasted_iota(jnp.int32, shape, axis)


def column_of(row, size):
    spread = jnp.broadcast_to(row, (size, size))
    return jnp.sum(
        jnp.where(iota((size, size), 0) == iota((size, size), 1), spread, 0), axis=1, keepdims=True
    )


class Plan:
    def __init__(self, query, cache_key, residual, norm_gain, codec_weight, frames):
        self.n_dp, self.n_mp = lax.axis_size("dp"), lax.axis_size("mp")
        self.rows, self.heads, self.positions, self.depth = cache_key.shape
        self.width = residual.shape[1]
        self.local = norm_gain.shape[0]
        self.channels = codec_weight.shape[1]
        self.tally, self.own = frames.shape
        self.late = self.n_dp * CAP
        self.span = KERNEL_TAPS // 2 * DILATION_STEP
        self.near = -(-self.span // CAP)
        self.pad = round_up(self.span, ROW_TILE)
        self.front = round_up(self.late + self.span, ROW_TILE)
        self.back = self.pad
        self.middle = self.tally - self.front - self.back
        self.chunk = 512
        self.steps = self.local // self.chunk
        self.slots = min(8, self.steps)
        self.group = ROW_TILE
        self.snake_rows = 32
        self.send_blocks = 4
        self.depth_in = self.heads * self.depth
        self.unroll = 4


def blocks_of(plan):
    count = 4
    unit = plan.middle // ROW_TILE
    sizes = [(unit // count + (1 if i < unit % count else 0)) * ROW_TILE for i in range(count)]
    starts = [plan.front + sum(sizes[:i]) for i in range(count)]
    return list(zip(starts, sizes))


def fused_kernel(
    P_,
    query,
    new_key,
    new_value,
    cache_key,
    cache_value,
    lens,
    residual,
    out_weight,
    gain,
    codec_weight,
    finished,
    owner,
    frames,
    alpha,
    filters,
    bias,
    hidden_out,
    audio_out,
    q_v,
    nk_v,
    nv_v,
    k_v,
    v_v,
    len_v,
    res_v,
    w_v,
    normed_v,
    gain_raw,
    gain_v,
    cw_v,
    fin_v,
    own_v,
    fr_v,
    al_v,
    fw_v,
    bias_v,
    act_v,
    hf_v,
    af_v,
    valid_v,
    hot_v,
    att_v,
    score_v,
    p_v,
    o_v,
    out_v,
    in_v,
    hid_v,
    acc_v,
    sq_v,
    sendc_v,
    recvc_v,
    sendh_v,
    land_v,
    near_v,
    here_v,
    there_v,
    lhs_v,
    audio_v,
    s_in,
    s_k,
    s_v,
    s_w,
    s_cw,
    s_fw,
    s_out,
    x_alpha,
    x_head,
    x_early,
    x_before,
    x_after,
    x_part,
    x_codec,
    send_a,
    recv_a,
    send_b,
    recv_b,
):
    n_dp, n_mp = P_.n_dp, P_.n_mp
    count = n_dp * n_mp
    rows, heads, positions, depth = P_.rows, P_.heads, P_.positions, P_.depth
    chunk, steps, slots = P_.chunk, P_.steps, P_.slots
    own, channels, tally, pad = P_.own, P_.channels, P_.tally, P_.pad
    late, span, front, back = P_.late, P_.span, P_.front, P_.back
    dp = lax.axis_index("dp")
    core = lax.axis_index("mp")
    me = dp * n_mp + core
    other = 1 - core
    mine_cols = pl.ds(pl.multiple_of(core * own, own), own)
    local_cols = pl.ds(pl.multiple_of(core * P_.local, P_.local), P_.local)

    def local(src, dst, sem):
        return pltpu.make_async_copy(src, dst, sem)

    def remote(src, dst, send, recv, to_dp, to_mp):
        return pltpu.make_async_remote_copy(
            src_ref=src,
            dst_ref=dst,
            send_sem=send,
            recv_sem=recv,
            device_id=(to_dp, to_mp),
            device_id_type=MESH,
        )

    frames_in = local(frames, fr_v, s_in.at[0])
    alpha_in = local(alpha, al_v.at[:, mine_cols], s_in.at[1])
    lens_in = local(lens, len_v, s_in.at[2])
    fin_in = local(finished, fin_v, s_in.at[3])
    own_in = local(owner, own_v, s_in.at[4])
    q_in = local(query, q_v, s_in.at[5])
    nk_in = local(new_key, nk_v, s_in.at[6])
    nv_in = local(new_value, nv_v, s_in.at[7])
    res_in = local(residual.at[:, local_cols], res_v, s_in.at[8])
    gain_in = local(gain, gain_raw, s_in.at[9])
    bias_in = local(bias, bias_v, s_in.at[10])

    def key_in(h):
        return local(cache_key.at[:, h], k_v.at[h], s_k.at[h])

    def value_in(h):
        return local(cache_value.at[:, h], v_v.at[h], s_v.at[h])

    def weight_in(i):
        begin = lax.select(i < steps, other * P_.local, core * P_.local) + lax.rem(i, steps) * chunk
        return local(
            out_weight.at[:, pl.ds(pl.multiple_of(begin, chunk), chunk)],
            w_v.at[lax.rem(i, slots)],
            s_w.at[lax.rem(i, slots)],
        )

    def codec_in(i):
        part = pl.ds(pl.multiple_of(i * chunk, chunk), chunk)
        return local(codec_weight.at[part, :], cw_v.at[part, :], s_cw.at[i])

    def filter_in(t):
        part = pl.ds(pl.multiple_of(t * channels, channels), channels)
        return local(filters.at[part, :], fw_v.at[part, :], s_fw.at[t])

    for copy in (lens_in, q_in, nk_in):
        copy.start()

    def start_key(h, carry):
        key_in(h).start()
        return carry

    def start_value(h, carry):
        value_in(h).start()
        return carry

    lax.fori_loop(0, heads, start_key, 0)
    lax.fori_loop(0, heads, start_value, 0)
    for copy in (nv_in, alpha_in, fin_in, own_in, frames_in):
        copy.start()

    barrier = pltpu.get_barrier_semaphore()

    def place(step):
        peer = lax.rem(me + step, count)
        return peer, peer // n_mp, lax.rem(peer, n_mp)

    def greet(step, carry):
        _, pd, pm = place(step)
        pl.semaphore_signal(barrier, inc=1, device_id=(pd, pm), device_id_type=MESH)
        return carry

    lax.fori_loop(1, count, greet, 0)

    def start_weight(i, carry):
        weight_in(i).start()
        return carry

    lax.fori_loop(0, slots, start_weight, 0)
    for copy in (res_in, gain_in, bias_in):
        copy.start()

    def start_codec(i, carry):
        codec_in(i).start()
        return carry

    lax.fori_loop(0, steps, start_codec, 0)

    for copy in (lens_in, fin_in, own_in):
        copy.wait()

    length = column_of(len_v[...], rows)
    lanes = P_.group * positions
    lane = iota((rows, lanes), 1)
    line = lax.rem(iota((rows, lanes), 0), P_.group)
    valid = (lane // positions == line) & (lax.rem(lane, positions) < length)
    valid_v[...] = jnp.where(valid, 0.0, -1e30)

    owner_row, done_row = own_v[...], fin_v[...]
    owner_col, done_col = column_of(owner_row, rows), column_of(done_row, rows)
    earlier = (
        (owner_col == owner_row)
        & (done_col == 1)
        & (iota((rows, rows), 0) < iota((rows, rows), 1))
    )
    slot = jnp.sum(jnp.where(earlier, 1, 0), axis=0, keepdims=True)
    target = jnp.where(done_row == 1, owner_row * CAP + slot, -1)
    hot_v[...] = jnp.where(iota((late, rows), 0) == target, 1.0, 0.0).astype(jnp.bfloat16)

    for copy in (q_in, nk_in, nv_in):
        copy.wait()
    scale = 1.0 / jnp.sqrt(jnp.float32(depth))

    def score_step(j, carry):
        for u in range(P_.unroll):
            key_in(j * P_.unroll + u).wait()
        for u in range(P_.unroll):
            h = j * P_.unroll + u
            cols = pl.ds(pl.multiple_of(h * depth, depth), depth)
            for g in range(rows // P_.group):
                part = slice(g * P_.group, (g + 1) * P_.group)
                keys = k_v[h, part].reshape(lanes, depth)
                score_v[h, part, :] = lax.dot_general(
                    q_v[part, cols],
                    keys,
                    (((1,), (1,)), ((), ())),
                    preferred_element_type=jnp.float32,
                )
        return carry

    lax.fori_loop(0, heads // P_.unroll, score_step, 0)

    def soft_step(h, carry):
        cols = pl.ds(pl.multiple_of(h * depth, depth), depth)
        s = jnp.where(valid_v[...] < 0.0, -1e30, score_v[h] * scale)
        mine = q_v[:, cols].astype(jnp.float32) * nk_v[:, cols].astype(jnp.float32)
        mine = jnp.sum(mine, axis=1, keepdims=True) * scale
        top = jnp.maximum(jnp.max(s, axis=1, keepdims=True), mine)
        expo = jnp.exp(s - top)
        mine_expo = jnp.exp(mine - top)
        share = 1.0 / (jnp.sum(expo, axis=1, keepdims=True) + mine_expo)
        p_v[h] = (expo * share).astype(jnp.bfloat16)
        mine_weight = (mine_expo * share).astype(jnp.bfloat16).astype(jnp.float32)
        o_v[h] = mine_weight * nv_v[:, cols].astype(jnp.float32)
        return carry

    lax.fori_loop(0, heads, soft_step, 0)

    def value_step(j, carry):
        for u in range(P_.unroll):
            value_in(j * P_.unroll + u).wait()
        for u in range(P_.unroll):
            h = j * P_.unroll + u
            cols = pl.ds(pl.multiple_of(h * depth, depth), depth)
            for g in range(rows // P_.group):
                part = slice(g * P_.group, (g + 1) * P_.group)
                values = v_v[h, part].reshape(lanes, depth)
                mixed = jnp.dot(p_v[h, part, :], values, preferred_element_type=jnp.float32)
                att_v[part, cols] = (mixed + o_v[h, part, :]).astype(jnp.bfloat16)
        return carry

    lax.fori_loop(0, heads // P_.unroll, value_step, 0)

    alpha_x = remote(
        alpha, al_v.at[:, mine_cols], x_alpha.at[0], x_alpha.at[1], dp, other
    )
    head_x = remote(frames.at[0:late], hf_v, x_head.at[0], x_head.at[1], dp, other)

    block = tally // P_.send_blocks

    def early_x(b):
        part = pl.ds(pl.multiple_of(pad + b * block, ROW_TILE), block)
        return remote(
            act_v.at[part, mine_cols],
            act_v.at[part, mine_cols],
            x_early.at[0, b],
            x_early.at[1, b],
            dp,
            other,
        )

    def before_x(m, to_dp, sender):
        cols = pl.ds(pl.multiple_of(sender * own, own), own)
        return remote(
            act_v.at[tally : tally + pad, mine_cols],
            act_v.at[0:pad, cols],
            x_before.at[0, m],
            x_before.at[1, sender],
            to_dp,
            m,
        )

    def after_x(m, to_dp, sender):
        return remote(
            frames.at[0:pad],
            af_v.at[sender],
            x_after.at[0, m],
            x_after.at[1, sender],
            to_dp,
            m,
        )

    pl.semaphore_wait(barrier, count - 1)
    alpha_x.start()
    head_x.start()

    @pl.when(dp > 0)
    def _():
        for m in range(n_mp):
            after_x(m, dp - 1, core).start()

    for copy in (alpha_in, frames_in):
        copy.wait()
    my_alpha = al_v[:, mine_cols]
    my_turn = my_alpha * 0.3183098861837907
    my_inverse = 1.0 / my_alpha
    snake_rows = tally // steps

    def part_x(i):
        return remote(out_v.at[i], in_v.at[i], x_part.at[0, i], x_part.at[1, i], dp, other)

    def their_step(i, carry):
        @pl.when(i > 0)
        def _():
            part_x(i - 1).start()

        weight_in(i).wait()
        for k in range(snake_rows // P_.snake_rows):
            begin = i * snake_rows + k * P_.snake_rows
            part = pl.ds(pl.multiple_of(begin, P_.snake_rows), P_.snake_rows)
            where_to = pl.ds(pl.multiple_of(pad + begin, ROW_TILE), P_.snake_rows)
            act_v[where_to, mine_cols] = fast_snake(
                fr_v[part, :].astype(jnp.float32), my_alpha, my_turn, my_inverse
            )
        out_v[i] = jnp.dot(
            att_v[...], w_v[lax.rem(i, slots)], preferred_element_type=jnp.float32
        ).astype(jnp.bfloat16)
        weight_in(i + slots).start()
        return carry

    lax.fori_loop(0, steps, their_step, 0)
    part_x(steps - 1).start()

    for b in range(P_.send_blocks):
        early_x(b).start()

    @pl.when(dp < n_dp - 1)
    def _():
        for m in range(n_mp):
            before_x(m, dp + 1, core).start()


    def start_filter(t, carry):
        filter_in(t).start()
        return carry

    lax.fori_loop(0, KERNEL_TAPS, start_filter, 0)
    for copy in (res_in, gain_in, bias_in):
        copy.wait()
    gains = gain_raw[...].astype(jnp.float32)
    for k in range(P_.local // 128):
        gain_v[:, k * 128 : (k + 1) * 128] = gains[k : k + 1]
    acc_v[...] = jnp.zeros_like(acc_v)
    sq_v[...] = jnp.zeros_like(sq_v)

    def produce(i):
        cols = pl.ds(pl.multiple_of(i * chunk, chunk), chunk)
        total = jnp.dot(att_v[...], w_v[lax.rem(i, slots)], preferred_element_type=jnp.float32)
        total = total + in_v[i].astype(jnp.float32) + res_v[:, cols].astype(jnp.float32)
        hidden = total.astype(jnp.bfloat16)
        hid_v[:, cols] = hidden
        wide = hidden.astype(jnp.float32)
        square = wide * wide
        squares = square[:, :128]
        for k in range(1, chunk // 128):
            squares = squares + square[:, k * 128 : (k + 1) * 128]
        sq_v[...] += squares
        normed_v[lax.rem(i, 2)] = (wide * gain_v[:, cols]).astype(jnp.bfloat16)

    def consume(i):
        cols = pl.ds(pl.multiple_of(i * chunk, chunk), chunk)
        acc_v[...] += jnp.dot(
            normed_v[lax.rem(i, 2)], cw_v[cols, :], preferred_element_type=jnp.float32
        )

    def mine_step(i, carry):
        codec_in(i - 1).wait()
        weight_in(i + steps).wait()
        part_x(i).wait_recv()
        consume(i - 1)
        produce(i)

        @pl.when(i + slots < steps)
        def _():
            weight_in(i + steps + slots).start()

        return carry

    weight_in(jnp.int32(steps)).wait()
    part_x(0).wait_recv()
    produce(jnp.int32(0))
    lax.fori_loop(1, steps, mine_step, 0)
    codec_in(steps - 1).wait()
    consume(jnp.int32(steps - 1))
    hidden_x = local(hid_v, hidden_out, s_out.at[0])
    hidden_x.start()

    other_cols = pl.ds(pl.multiple_of(other * own, own), own)
    sendc_v[:, :own] = acc_v[:, other_cols]
    sendc_v[:, own:] = sq_v[...]
    codec_x = remote(sendc_v, recvc_v, x_codec.at[0], x_codec.at[1], dp, other)
    codec_x.start()

    def conv_block(index):
        begin, size = blocks_of(P_)[index]
        for t in range(KERNEL_TAPS):
            at = pad + begin - span + t * DILATION_STEP
            lhs_v[:size, t * channels : (t + 1) * channels] = act_v[at : at + size, :]
        audio_v[begin : begin + size, :] = (
            jnp.dot(lhs_v[:size, :], fw_v[...], preferred_element_type=jnp.float32)
            + fr_v[begin : begin + size, :].astype(jnp.float32)
            + bias_v[...]
        ).astype(jnp.bfloat16)

    codec_x.wait_recv()
    square = jnp.sum(sq_v[...] + recvc_v[:, own:], axis=1, keepdims=True)
    latent = (
        (acc_v[:, mine_cols] + recvc_v[:, :own]) * lax.rsqrt(square / P_.width + 1e-05)
    ).astype(jnp.bfloat16)
    outgoing = jnp.dot(hot_v[...], latent, preferred_element_type=jnp.float32)
    for d in range(n_dp):
        sendh_v[d] = outgoing[d * CAP : (d + 1) * CAP].astype(jnp.bfloat16)

    def copy_a(pd, pm, src_dp, src_mp, send, recv):
        return remote(
            sendh_v.at[pd], land_v.at[src_mp, src_dp], send_a.at[send], recv_a.at[recv], pd, pm
        )

    def copy_b(pd, pm, src_dp, src_mp, send, recv):
        return remote(
            sendh_v.at[pd + 1], near_v.at[src_mp, src_dp], send_b.at[send], recv_b.at[recv], pd, pm
        )

    def send_near(step, carry):
        peer, pd, pm = place(step)

        @pl.when(pd < n_dp - 1)
        def _():
            copy_b(pd, pm, dp, core, peer, me).start()

        return carry

    def send(step, carry):
        peer, pd, pm = place(step)
        copy_a(pd, pm, dp, core, peer, me).start()
        return carry

    lax.fori_loop(1, count, send, 0)

    @pl.when(dp < P_.near)
    def _():
        lax.fori_loop(1, count, send_near, 0)

    land_v[core, dp] = sendh_v[dp]

    @pl.when(dp < P_.near)
    def _():
        near_v[core, dp] = sendh_v[lax.rem(dp + 1, n_dp)]

    def wait_filter(t, carry):
        filter_in(t).wait()
        return carry

    lax.fori_loop(0, KERNEL_TAPS, wait_filter, 0)
    for b in range(P_.send_blocks):
        early_x(b).wait_recv()

    for index in range(len(blocks_of(P_))):
        conv_block(index)
    middle_x = local(
        audio_v.at[front : tally - back], audio_out.at[front : tally - back], s_out.at[1]
    )
    middle_x.start()

    alpha_x.wait_recv()
    head_x.wait_recv()

    def finish(step, carry):
        peer, pd, pm = place(step)
        copy_a(pd, pm, pd, pm, peer, peer).wait_recv()
        return carry

    lax.fori_loop(1, count, finish, 0)
    for s in range(n_dp):
        for m in range(n_mp):
            here_v[s * CAP : (s + 1) * CAP, m * own : (m + 1) * own] = land_v[m, s].astype(
                jnp.float32
            )
    for b in range(P_.send_blocks):
        early_x(b).wait_send()
    hf = hf_v[...].astype(jnp.float32)
    mf = fr_v[0:late, :].astype(jnp.float32)

    all_alpha = al_v[...]
    all_turn = all_alpha * 0.3183098861837907
    all_inverse = 1.0 / all_alpha
    here_v[:, mine_cols] += mf
    here_v[:, other_cols] += hf
    act_v[pad : pad + late, :] = fast_snake(here_v[...], all_alpha, all_turn, all_inverse)

    @pl.when(dp < n_dp - 1)
    def _():
        for m in range(n_mp):
            after_x(0, 0, m).wait_recv()

        def take_near(sender, carry):
            @pl.when(sender != me)
            def _():
                copy_b(0, 0, sender // n_mp, lax.rem(sender, n_mp), 0, sender).wait_recv()

            return carry

        lax.fori_loop(0, P_.near * n_mp, take_near, 0)
        for m in range(n_mp):
            there_v[:, m * own : (m + 1) * own] = af_v[m].astype(jnp.float32)
            for s in range(P_.near):
                there_v[s * CAP : (s + 1) * CAP, m * own : (m + 1) * own] += near_v[m, s].astype(
                    jnp.float32
                )
        act_v[pad + tally :, :] = fast_snake(there_v[...], all_alpha, all_turn, all_inverse)

    @pl.when(dp == n_dp - 1)
    def _():
        act_v[pad + tally :, :] = jnp.zeros((pad, channels), jnp.bfloat16)

    @pl.when(dp > 0)
    def _():
        for m in range(n_mp):
            before_x(0, 0, m).wait_recv()

    @pl.when(dp == 0)
    def _():
        act_v[0:pad, :] = jnp.zeros((pad, channels), jnp.bfloat16)

    for t in range(KERNEL_TAPS):
        cols = slice(t * channels, (t + 1) * channels)
        at = pad - span + t * DILATION_STEP
        lhs_v[:front, cols] = act_v[at : at + front, :]
        at = at + tally - back
        lhs_v[front : front + back, cols] = act_v[at : at + back, :]
    edge = (
        jnp.dot(lhs_v[: front + back, :], fw_v[...], preferred_element_type=jnp.float32)
        + bias_v[...]
    )
    audio_v[:late, :] = (edge[:late] + here_v[:, mine_cols]).astype(jnp.bfloat16)
    audio_v[late:front, :] = (edge[late:front] + fr_v[late:front, :].astype(jnp.float32)).astype(
        jnp.bfloat16
    )
    audio_v[tally - back :, :] = (edge[front:] + fr_v[tally - back :, :].astype(jnp.float32)).astype(
        jnp.bfloat16
    )
    first_x = local(audio_v.at[:front], audio_out.at[:front], s_out.at[2])
    last_x = local(audio_v.at[tally - back :], audio_out.at[tally - back :], s_out.at[3])
    first_x.start()
    last_x.start()

    alpha_x.wait_send()
    head_x.wait_send()

    @pl.when(dp < n_dp - 1)
    def _():
        for m in range(n_mp):
            before_x(m, 0, core).wait_send()

    @pl.when(dp > 0)
    def _():
        for m in range(n_mp):
            after_x(m, 0, core).wait_send()

    def part_sent(i, carry):
        part_x(i).wait_send()
        return carry

    lax.fori_loop(0, steps, part_sent, 0)
    codec_x.wait_send()

    def sent(step, carry):
        peer, pd, pm = place(step)
        copy_a(pd, pm, dp, core, peer, me).wait_send()
        return carry

    lax.fori_loop(1, count, sent, 0)

    def sent_near(step, carry):
        peer, pd, pm = place(step)

        @pl.when(pd < n_dp - 1)
        def _():
            copy_b(pd, pm, dp, core, peer, me).wait_send()

        return carry

    @pl.when(dp < P_.near)
    def _():
        lax.fori_loop(1, count, sent_near, 0)

    hidden_x.wait()
    middle_x.wait()
    first_x.wait()
    last_x.wait()


def fused(
    query,
    new_key,
    new_value,
    cache_key,
    cache_value,
    cache_len,
    residual,
    out_weight,
    norm_gain,
    codec_weight,
    finished,
    owner,
    frames,
    snake_alpha,
    filter_weight,
    conv_bias,
):
    plan = Plan(query, cache_key, residual, norm_gain, codec_weight, frames)
    n_dp, n_mp = plan.n_dp, plan.n_mp
    count = n_dp * n_mp
    bf, f32, i32 = jnp.bfloat16, jnp.float32, jnp.int32
    vm = pltpu.VMEM
    dma = pltpu.SemaphoreType.DMA
    rows, own, channels, tally = plan.rows, plan.own, plan.channels, plan.tally
    taps = KERNEL_TAPS * channels
    biggest = max([size for _, size in blocks_of(plan)] + [plan.front + plan.back])
    scratch = [
        vm(query.shape, bf),
        vm(query.shape, bf),
        vm(query.shape, bf),
        vm((plan.heads, rows, plan.positions, plan.depth), bf),
        vm((plan.heads, rows, plan.positions, plan.depth), bf),
        vm((1, rows), i32),
        vm((rows, plan.local), bf),
        vm((plan.slots, plan.depth_in, plan.chunk), bf),
        vm((2, rows, plan.chunk), bf),
        vm((plan.local // 128, 128), bf),
        vm((1, plan.local), f32),
        vm((plan.local, channels), bf),
        vm((1, rows), i32),
        vm((1, rows), i32),
        vm((tally, own), bf),
        vm((1, channels), f32),
        vm((taps, own), bf),
        vm((1, own), f32),
        vm((tally + 2 * plan.pad, channels), bf),
        vm((plan.late, own), bf),
        vm((n_mp, plan.pad, own), bf),
        vm((rows, plan.group * plan.positions), f32),
        vm((plan.late, rows), bf),
        vm((rows, plan.depth_in), bf),
        vm((plan.heads, rows, plan.group * plan.positions), f32),
        vm((plan.heads, rows, plan.group * plan.positions), bf),
        vm((plan.heads, rows, plan.depth), f32),
        vm((plan.steps, rows, plan.chunk), bf),
        vm((plan.steps, rows, plan.chunk), bf),
        vm((rows, plan.local), bf),
        vm((rows, channels), f32),
        vm((rows, 128), f32),
        vm((rows, own + 128), f32),
        vm((rows, own + 128), f32),
        vm((n_dp, CAP, own), bf),
        vm((n_mp, n_dp, CAP, own), bf),
        vm((n_mp, plan.near, CAP, own), bf),
        vm((plan.late, channels), f32),
        vm((plan.pad, channels), f32),
        vm((biggest, taps), bf),
        vm((tally, own), bf),
        dma((11,)),
        dma((plan.heads,)),
        dma((plan.heads,)),
        dma((plan.slots,)),
        dma((plan.steps,)),
        dma((KERNEL_TAPS,)),
        dma((4,)),
        dma((2,)),
        dma((2,)),
        dma((2, plan.send_blocks)),
        dma((2, n_mp)),
        dma((2, n_mp)),
        dma((2, plan.steps)),
        dma((2,)),
        dma((count,)),
        dma((count,)),
        dma((count,)),
        dma((plan.near * n_mp,)),
    ]
    anywhere = pl.BlockSpec(memory_space=pl.ANY)
    return pl.pallas_call(
        functools.partial(fused_kernel, plan),
        out_shape=(
            jax.ShapeDtypeStruct((rows, plan.local), bf),
            jax.ShapeDtypeStruct((tally, own), bf),
        ),
        in_specs=[anywhere] * 16,
        out_specs=(anywhere, anywhere),
        scratch_shapes=scratch,
        compiler_params=pltpu.CompilerParams(
            collective_id=1, has_side_effects=True, vmem_limit_bytes=VMEM_BYTES
        ),
    )(
        query,
        new_key,
        new_value,
        cache_key,
        cache_value,
        cache_len.reshape(1, -1),
        residual,
        out_weight,
        norm_gain.reshape(-1, 128),
        codec_weight,
        finished.reshape(1, -1),
        owner.reshape(1, -1),
        frames,
        snake_alpha.reshape(1, -1),
        filter_weight.reshape(taps, own),
        conv_bias.reshape(1, -1),
    )


VMEM_BYTES = 66 * 1000 * 1000


def step(*args):
    return fused(*args) if lax.axis_size("mp") == 2 else body(*args)


def solution(mesh):
    placed = (
        P("dp", "mp"),
        P("dp", "mp"),
        P("dp", "mp"),
        P("dp", "mp", None, None),
        P("dp", "mp", None, None),
        P("dp"),
        P("dp", None),
        P("mp", None),
        P("mp"),
        P("mp", None),
        P("dp"),
        P("dp"),
        P("dp", "mp"),
        P("mp"),
        P(None, None, "mp"),
        P("mp"),
    )
    return jax.shard_map(
        step, mesh=mesh, in_specs=placed, out_specs=(P("dp", "mp"), P("dp", "mp")), check_vma=False
    )
```

```python
import functools
import jax
import jax.numpy as jnp
from jax import lax
from jax.experimental import pallas as pl
from jax.experimental.pallas import tpu as pltpu
from jax.sharding import PartitionSpec as P

KERNEL_TAPS = 7
DILATION_STEP = 3
CAP = 4
ROW_TILE = 16


def swap(x):
    return lax.ppermute(x, "mp", [(0, 1), (1, 0)])


def gather_mp(x, axis):
    if lax.axis_size("mp") != 2:
        return lax.all_gather(x, "mp", axis=axis, tiled=True)
    other = swap(x)
    first = lax.axis_index("mp") == 0
    return jnp.concatenate([jnp.where(first, x, other), jnp.where(first, other, x)], axis=axis)


def sin_squared(x):
    turns = jnp.round(x * 0.3183098861837907)
    r = (x - turns * 3.140625) - turns * 0.0009676535897932
    q = r * r
    p = -2.5052108e-08 + q * 1.6059044e-10
    p = 2.7557319e-06 + q * p
    p = -1.9841270e-04 + q * p
    p = 8.3333333e-03 + q * p
    p = -1.6666667e-01 + q * p
    sine = r + r * (q * p)
    return sine * sine


def snake(mix, alpha):
    return (mix + sin_squared(alpha * mix) / alpha).astype(jnp.bfloat16)


def columns_kernel(start_ref, x_ref, w_ref, o_ref):
    del start_ref
    o_ref[...] = jnp.dot(x_ref[...], w_ref[...], preferred_element_type=jnp.float32).astype(
        o_ref.dtype
    )


def columns_dot(x, w, start, width, tile, dtype):
    rows, depth = x.shape
    return pl.pallas_call(
        columns_kernel,
        out_shape=jax.ShapeDtypeStruct((rows, width), dtype),
        grid_spec=pltpu.PrefetchScalarGridSpec(
            num_scalar_prefetch=1,
            grid=(width // tile,),
            in_specs=[
                pl.BlockSpec((rows, depth), lambda j, s: (0, 0)),
                pl.BlockSpec((depth, tile), lambda j, s: (0, s[0] + j)),
            ],
            out_specs=pl.BlockSpec((rows, tile), lambda j, s: (0, j)),
        ),
        compiler_params=pltpu.CompilerParams(vmem_limit_bytes=28 * 1024 * 1024),
        cost_estimate=pl.CostEstimate(
            flops=2 * rows * depth * width, bytes_accessed=2 * depth * width, transcendentals=0
        ),
    )(jnp.full((1,), start, jnp.int32), x, w)


def handoff_kernel(
    n_dp, n_mp, near, out_ref, a_ref, b_ref, land_a, land_b, send_a, recv_a, send_b, recv_b
):
    dp = lax.axis_index("dp")
    mp = lax.axis_index("mp")
    count = n_dp * n_mp
    me = dp * n_mp + mp
    barrier = pltpu.get_barrier_semaphore()

    def place(step):
        peer = lax.rem(me + step, count)
        return peer, peer // n_mp, lax.rem(peer, n_mp)

    def greet(step, carry):
        _, pd, pm = place(step)
        pl.semaphore_signal(
            barrier, inc=1, device_id=(pd, pm), device_id_type=pl.DeviceIdType.MESH
        )
        return carry

    lax.fori_loop(1, count, greet, 0)
    pl.semaphore_wait(barrier, count - 1)

    def copy_a(pd, pm, send, recv):
        return pltpu.make_async_remote_copy(
            src_ref=out_ref.at[pd],
            dst_ref=land_a.at[me],
            send_sem=send_a.at[send],
            recv_sem=recv_a.at[recv],
            device_id=(pd, pm),
            device_id_type=pl.DeviceIdType.MESH,
        )

    def copy_b(slot, pd, pm, send, recv):
        return pltpu.make_async_remote_copy(
            src_ref=out_ref.at[pd + 1],
            dst_ref=land_b.at[slot],
            send_sem=send_b.at[send],
            recv_sem=recv_b.at[recv],
            device_id=(pd, pm),
            device_id_type=pl.DeviceIdType.MESH,
        )

    def send(step, carry):
        peer, pd, pm = place(step)
        copy_a(pd, pm, peer, me).start()
        return carry

    def send_near(step, carry):
        peer, pd, pm = place(step)
        copy_b(me, pd, pm, peer, me).start()
        return carry

    @pl.when(dp < near)
    def _():
        lax.fori_loop(1, count, send_near, 0)

    lax.fori_loop(1, count, send, 0)
    land_a[me] = out_ref[dp]

    @pl.when(dp < near)
    def _():
        land_b[me] = out_ref[dp + 1]

    def finish(step, carry):
        peer, pd, pm = place(step)
        copy = copy_a(pd, pm, peer, peer)
        copy.wait_recv()
        copy.wait_send()
        return carry

    def finish_near(step, carry):
        peer, pd, pm = place(step)
        copy_b(me, pd, pm, peer, me).wait_send()
        return carry

    def take_near(sender, carry):
        @pl.when(sender != me)
        def _():
            copy_b(sender, 0, 0, sender, sender).wait_recv()

        return carry

    lax.fori_loop(1, count, finish, 0)

    @pl.when(dp < near)
    def _():
        lax.fori_loop(1, count, finish_near, 0)

    lax.fori_loop(0, near * n_mp, take_near, 0)

    def total_of(land, first):
        total = land[first].astype(jnp.float32)
        for m in range(1, n_mp):
            total = total + land[first + m].astype(jnp.float32)
        return total

    def put(d, carry):
        a_ref[d] = total_of(land_a, d * n_mp)
        return carry

    lax.fori_loop(0, n_dp, put, 0)
    for d in range(near):
        b_ref[d] = total_of(land_b, d * n_mp)


def handoff(outgoing, near):
    n_dp, n_mp = lax.axis_size("dp"), lax.axis_size("mp")
    count = n_dp * n_mp
    _, cap, width = outgoing.shape
    vmem = pl.BlockSpec(memory_space=pltpu.VMEM)
    return pl.pallas_call(
        functools.partial(handoff_kernel, n_dp, n_mp, near),
        out_shape=(
            jax.ShapeDtypeStruct((n_dp, cap, width), jnp.float32),
            jax.ShapeDtypeStruct((near, cap, width), jnp.float32),
        ),
        in_specs=[vmem],
        out_specs=(vmem, vmem),
        scratch_shapes=[
            pltpu.VMEM((count, cap, width), jnp.bfloat16),
            pltpu.VMEM((near * n_mp, cap, width), jnp.bfloat16),
            pltpu.SemaphoreType.DMA((count,)),
            pltpu.SemaphoreType.DMA((count,)),
            pltpu.SemaphoreType.DMA((count,)),
            pltpu.SemaphoreType.DMA((near * n_mp,)),
        ],
        compiler_params=pltpu.CompilerParams(
            collective_id=0, has_side_effects=True, vmem_limit_bytes=16 * 1024 * 1024
        ),
    )(outgoing)


def round_up(n, tile):
    return -(-n // tile) * tile


def taps_of(cells, rows):
    parts = [cells[t * DILATION_STEP : t * DILATION_STEP + rows] for t in range(KERNEL_TAPS)]
    return jnp.concatenate(parts, axis=1)


def attend(query, new_key, new_value, cache_key, cache_value, cache_len):
    count, heads, positions, depth = cache_key.shape
    scale = 1.0 / jnp.sqrt(jnp.float32(depth))
    queries = query.reshape(count, heads, depth)
    fresh_key = new_key.reshape(count, heads, depth)
    fresh_value = new_value.reshape(count, heads, depth)
    scores = (
        jnp.einsum("rhd,rhld->rhl", queries, cache_key, preferred_element_type=jnp.float32) * scale
    )
    own_score = (
        jnp.einsum("rhd,rhd->rh", queries, fresh_key, preferred_element_type=jnp.float32) * scale
    )
    valid = jnp.arange(positions, dtype=jnp.int32)[None, :] < cache_len[:, None]
    scores = jnp.where(valid[:, None, :], scores, -1e30)
    top = jnp.maximum(jnp.max(scores, axis=-1), own_score)
    expo = jnp.where(valid[:, None, :], jnp.exp(scores - top[..., None]), 0.0)
    own_expo = jnp.exp(own_score - top)
    total = jnp.sum(expo, axis=-1) + own_expo
    weights = (expo / total[..., None]).astype(jnp.bfloat16)
    own_weight = (own_expo / total).astype(jnp.bfloat16)
    mixed = jnp.einsum("rhl,rhld->rhd", weights, cache_value, preferred_element_type=jnp.float32)
    mixed = mixed + own_weight.astype(jnp.float32)[..., None] * fresh_value.astype(jnp.float32)
    return mixed.astype(jnp.bfloat16).reshape(count, heads * depth)


def body(
    query,
    new_key,
    new_value,
    cache_key,
    cache_value,
    cache_len,
    residual,
    out_weight,
    norm_gain,
    codec_weight,
    finished,
    owner,
    frames,
    snake_alpha,
    filter_weight,
    conv_bias,
):
    owners = lax.axis_size("dp")
    n_mp = lax.axis_size("mp")
    core = lax.axis_index("mp")
    tally, own = frames.shape
    span = KERNEL_TAPS // 2 * DILATION_STEP
    late = owners * CAP
    near = -(-span // CAP)
    front = round_up(late + span, ROW_TILE)
    back = round_up(span, ROW_TILE)

    wide_frames = frames.astype(jnp.float32)
    alpha_all = gather_mp(snake_alpha, 0)
    early = gather_mp(snake(wide_frames, snake_alpha), 1)
    head_frames = gather_mp(frames[:late], 1)
    before = lax.ppermute(early[tally - span :], "dp", [(i, i + 1) for i in range(owners - 1)])
    after_frames = lax.ppermute(
        head_frames[: near * CAP], "dp", [(i + 1, i) for i in range(owners - 1)]
    )
    middle = tally - front - back
    main = wide_frames[front : tally - back] + conv_bias
    for t in range(KERNEL_TAPS):
        start = front - span + t * DILATION_STEP
        main = main + jnp.dot(
            early[start : start + middle], filter_weight[t], preferred_element_type=jnp.float32
        )
    main = main.astype(jnp.bfloat16)

    attended = attend(query, new_key, new_value, cache_key, cache_value, cache_len)
    count = attended.shape[0]
    width = out_weight.shape[1]
    local_width = norm_gain.shape[0]
    residual_part = lax.dynamic_slice_in_dim(residual, core * local_width, local_width, 1)
    if n_mp == 2:
        tile = 1024
        theirs = columns_dot(
            attended, out_weight, (1 - core) * (local_width // tile), local_width, tile, jnp.bfloat16
        )
        arrived = swap(theirs)
        mine = columns_dot(
            attended, out_weight, core * (local_width // tile), local_width, tile, jnp.float32
        )
        projected = mine + arrived.astype(jnp.float32)
    else:
        term = jnp.dot(attended, out_weight, preferred_element_type=jnp.float32)
        projected = lax.psum_scatter(term, "mp", scatter_dimension=1, tiled=True)
    hidden = (residual_part.astype(jnp.float32) + projected).astype(jnp.bfloat16)
    wide = hidden.astype(jnp.float32)
    squares = jnp.sum(wide * wide, axis=-1)
    squares = squares + swap(squares) if n_mp == 2 else lax.psum(squares, "mp")
    meansq = squares / width
    normed = (wide * norm_gain.astype(jnp.float32)).astype(jnp.bfloat16)
    channels = codec_weight.shape[1]
    share = columns_dot(normed, codec_weight, 0, channels, 256, jnp.float32)
    share = (share * lax.rsqrt(meansq + 1e-05)[:, None]).astype(jnp.bfloat16)

    index = jnp.arange(count, dtype=jnp.int32)
    earlier = (
        (owner[:, None] == owner[None, :])
        & (finished[None, :] == 1)
        & (index[None, :] < index[:, None])
    )
    slot = jnp.sum(earlier.astype(jnp.int32), axis=1)
    target = owner * CAP + slot
    places = jnp.arange((owners + 1) * CAP, dtype=jnp.int32)
    onehot = ((places[:, None] == target[None, :]) & (finished[None, :] == 1)).astype(jnp.bfloat16)
    outgoing = jnp.dot(onehot, share, preferred_element_type=jnp.float32).astype(jnp.bfloat16)
    here, there = handoff(outgoing.reshape(owners + 1, CAP, channels), near)
    here = here.reshape(late, channels).astype(jnp.bfloat16).astype(jnp.float32)
    there = there.reshape(near * CAP, channels).astype(jnp.bfloat16).astype(jnp.float32)

    head_mix = head_frames.astype(jnp.float32) + here
    head_act = snake(head_mix, alpha_all)
    after = snake(after_frames.astype(jnp.float32) + there, alpha_all)[:span]
    cells_a = jnp.concatenate([before, head_act, early[late : front + span]], axis=0)
    cells_b = jnp.concatenate([early[tally - back - span :], after], axis=0)
    edges = jnp.concatenate([taps_of(cells_a, front), taps_of(cells_b, back)], axis=0)
    flat = filter_weight.reshape(KERNEL_TAPS * channels, own)
    own_mix = lax.dynamic_slice_in_dim(head_mix, core * own, own, 1)
    edge_mix = jnp.concatenate(
        [own_mix, wide_frames[late:front], wide_frames[tally - back :]], axis=0
    )
    edge = jnp.dot(edges, flat, preferred_element_type=jnp.float32) + edge_mix + conv_bias
    edge = edge.astype(jnp.bfloat16)
    audio = jnp.concatenate([edge[:front], main, edge[front:]], axis=0)
    return (hidden, audio)


MESH = pl.DeviceIdType.MESH
SIN_SQUARED = (
    1.0,
    -0.3333333134651184,
    0.04444440081715584,
    -0.003174516372382641,
    0.00014100516273174435,
    -4.2275191844964866e-06,
    8.055603473167139e-08,
)
ROUNDER = 12582912.0


def fast_snake(mix, alpha, turn, inverse):
    turns = (mix * turn + ROUNDER) - ROUNDER
    r = (mix * alpha - turns * 3.140625) - turns * 0.0009676535897932
    q = r * r
    p = SIN_SQUARED[-1] * q + SIN_SQUARED[-2]
    for c in SIN_SQUARED[-3::-1]:
        p = p * q + c
    return (mix + (q * p) * inverse).astype(jnp.bfloat16)


def iota(shape, axis):
    return lax.broadcasted_iota(jnp.int32, shape, axis)


def column_of(row, size):
    spread = jnp.broadcast_to(row, (size, size))
    return jnp.sum(
        jnp.where(iota((size, size), 0) == iota((size, size), 1), spread, 0), axis=1, keepdims=True
    )


class Plan:
    def __init__(self, query, cache_key, residual, norm_gain, codec_weight, frames):
        self.n_dp, self.n_mp = lax.axis_size("dp"), lax.axis_size("mp")
        self.rows, self.heads, self.positions, self.depth = cache_key.shape
        self.width = residual.shape[1]
        self.local = norm_gain.shape[0]
        self.channels = codec_weight.shape[1]
        self.tally, self.own = frames.shape
        self.late = self.n_dp * CAP
        self.span = KERNEL_TAPS // 2 * DILATION_STEP
        self.near = -(-self.span // CAP)
        self.pad = round_up(self.span, ROW_TILE)
        self.front = round_up(self.late + self.span, ROW_TILE)
        self.back = self.pad
        self.middle = self.tally - self.front - self.back
        self.chunk = 512
        self.steps = self.local // self.chunk
        self.slots = min(4, self.steps)
        self.group = ROW_TILE
        self.snake_rows = 32
        self.send_blocks = 4
        self.depth_in = self.heads * self.depth
        self.unroll = 4


def blocks_of(plan):
    count = 5
    unit = plan.middle // ROW_TILE
    sizes = [(unit // count + (1 if i < unit % count else 0)) * ROW_TILE for i in range(count)]
    starts = [plan.front + sum(sizes[:i]) for i in range(count)]
    return list(zip(starts, sizes))


def fused_kernel(
    P_,
    query,
    new_key,
    new_value,
    cache_key,
    cache_value,
    lens,
    residual,
    out_weight,
    gain,
    codec_weight,
    finished,
    owner,
    frames,
    alpha,
    filters,
    bias,
    hid_v,
    audio_v,
    q_v,
    nk_v,
    nv_v,
    k_v,
    v_v,
    len_v,
    res_v,
    w_v,
    normed_v,
    gain_raw,
    gain_v,
    cw_v,
    fin_v,
    own_v,
    fr_v,
    al_v,
    fw_v,
    bias_v,
    act_v,
    hf_v,
    af_v,
    valid_v,
    hot_v,
    att_v,
    score_v,
    p_v,
    o_v,
    out_v,
    in_v,
    acc_v,
    sq_v,
    sendc_v,
    recvc_v,
    sendh_v,
    land_v,
    near_v,
    here_v,
    there_v,
    lhs_v,
    s_in,
    s_k,
    s_v,
    s_w,
    s_cw,
    s_fw,
    x_alpha,
    x_head,
    x_early,
    x_before,
    x_after,
    x_part,
    x_codec,
    send_a,
    recv_a,
    send_b,
    recv_b,
):
    n_dp, n_mp = P_.n_dp, P_.n_mp
    count = n_dp * n_mp
    rows, heads, positions, depth = P_.rows, P_.heads, P_.positions, P_.depth
    chunk, steps, slots = P_.chunk, P_.steps, P_.slots
    own, channels, tally, pad = P_.own, P_.channels, P_.tally, P_.pad
    late, span, front, back = P_.late, P_.span, P_.front, P_.back
    dp = lax.axis_index("dp")
    core = lax.axis_index("mp")
    me = dp * n_mp + core
    other = 1 - core
    mine_cols = pl.ds(pl.multiple_of(core * own, own), own)
    local_cols = pl.ds(pl.multiple_of(core * P_.local, P_.local), P_.local)

    def local(src, dst, sem):
        return pltpu.make_async_copy(src, dst, sem)

    def remote(src, dst, send, recv, to_dp, to_mp):
        return pltpu.make_async_remote_copy(
            src_ref=src,
            dst_ref=dst,
            send_sem=send,
            recv_sem=recv,
            device_id=(to_dp, to_mp),
            device_id_type=MESH,
        )

    frames_in = local(frames, fr_v, s_in.at[0])
    alpha_in = local(alpha, al_v.at[:, mine_cols], s_in.at[1])
    lens_in = local(lens, len_v, s_in.at[2])
    fin_in = local(finished, fin_v, s_in.at[3])
    own_in = local(owner, own_v, s_in.at[4])
    q_in = local(query, q_v, s_in.at[5])
    nk_in = local(new_key, nk_v, s_in.at[6])
    nv_in = local(new_value, nv_v, s_in.at[7])
    res_in = local(residual.at[:, local_cols], res_v, s_in.at[8])
    gain_in = local(gain, gain_raw, s_in.at[9])
    bias_in = local(bias, bias_v, s_in.at[10])

    def key_in(h):
        return local(cache_key.at[:, h], k_v.at[h], s_k.at[h])

    def value_in(h):
        return local(cache_value.at[:, h], v_v.at[h], s_v.at[h])

    def weight_in(i):
        begin = lax.select(i < steps, other * P_.local, core * P_.local) + lax.rem(i, steps) * chunk
        return local(
            out_weight.at[:, pl.ds(pl.multiple_of(begin, chunk), chunk)],
            w_v.at[lax.rem(i, slots)],
            s_w.at[lax.rem(i, slots)],
        )

    def codec_in(i):
        part = pl.ds(pl.multiple_of(i * chunk, chunk), chunk)
        return local(codec_weight.at[part, :], cw_v.at[part, :], s_cw.at[i])

    def filter_in(t):
        part = pl.ds(pl.multiple_of(t * channels, channels), channels)
        return local(filters.at[part, :], fw_v.at[part, :], s_fw.at[t])

    for copy in (lens_in, q_in, nk_in):
        copy.start()

    def start_key(h, carry):
        key_in(h).start()
        return carry

    def start_value(h, carry):
        value_in(h).start()
        return carry

    lax.fori_loop(0, heads, start_key, 0)
    lax.fori_loop(0, heads, start_value, 0)
    for copy in (nv_in, alpha_in, fin_in, own_in, frames_in):
        copy.start()

    barrier = pltpu.get_barrier_semaphore()

    def place(step):
        peer = lax.rem(me + step, count)
        return peer, peer // n_mp, lax.rem(peer, n_mp)

    def greet(step, carry):
        _, pd, pm = place(step)
        pl.semaphore_signal(barrier, inc=1, device_id=(pd, pm), device_id_type=MESH)
        return carry

    lax.fori_loop(1, count, greet, 0)

    def start_weight(i, carry):
        weight_in(i).start()
        return carry

    lax.fori_loop(0, slots, start_weight, 0)
    for copy in (res_in, gain_in, bias_in):
        copy.start()

    def start_codec(i, carry):
        codec_in(i).start()
        return carry

    lax.fori_loop(0, steps, start_codec, 0)

    def start_filter(t, carry):
        filter_in(t).start()
        return carry

    lax.fori_loop(0, KERNEL_TAPS, start_filter, 0)

    for copy in (lens_in, fin_in, own_in):
        copy.wait()

    length = column_of(len_v[...], rows)
    lanes = P_.group * positions
    lane = iota((rows, lanes), 1)
    line = lax.rem(iota((rows, lanes), 0), P_.group)
    valid = (lane // positions == line) & (lax.rem(lane, positions) < length)
    valid_v[...] = jnp.where(valid, 0.0, -1e30)

    owner_row, done_row = own_v[...], fin_v[...]
    owner_col, done_col = column_of(owner_row, rows), column_of(done_row, rows)
    earlier = (
        (owner_col == owner_row)
        & (done_col == 1)
        & (iota((rows, rows), 0) < iota((rows, rows), 1))
    )
    slot = jnp.sum(jnp.where(earlier, 1, 0), axis=0, keepdims=True)
    target = jnp.where(done_row == 1, owner_row * CAP + slot, -1)
    hot_v[...] = jnp.where(iota((late, rows), 0) == target, 1.0, 0.0).astype(jnp.bfloat16)

    for copy in (q_in, nk_in, nv_in):
        copy.wait()
    scale = 1.0 / jnp.sqrt(jnp.float32(depth))

    def score_step(j, carry):
        for u in range(P_.unroll):
            key_in(j * P_.unroll + u).wait()
        for u in range(P_.unroll):
            h = j * P_.unroll + u
            cols = pl.ds(pl.multiple_of(h * depth, depth), depth)
            for g in range(rows // P_.group):
                part = slice(g * P_.group, (g + 1) * P_.group)
                keys = k_v[h, part].reshape(lanes, depth)
                score_v[h, part, :] = lax.dot_general(
                    q_v[part, cols],
                    keys,
                    (((1,), (1,)), ((), ())),
                    preferred_element_type=jnp.float32,
                )
        return carry

    lax.fori_loop(0, heads // P_.unroll, score_step, 0)

    def soft_step(h, carry):
        cols = pl.ds(pl.multiple_of(h * depth, depth), depth)
        s = jnp.where(valid_v[...] < 0.0, -1e30, score_v[h] * scale)
        mine = q_v[:, cols].astype(jnp.float32) * nk_v[:, cols].astype(jnp.float32)
        mine = jnp.sum(mine, axis=1, keepdims=True) * scale
        top = jnp.maximum(jnp.max(s, axis=1, keepdims=True), mine)
        expo = jnp.exp(s - top)
        mine_expo = jnp.exp(mine - top)
        share = 1.0 / (jnp.sum(expo, axis=1, keepdims=True) + mine_expo)
        p_v[h] = (expo * share).astype(jnp.bfloat16)
        mine_weight = (mine_expo * share).astype(jnp.bfloat16).astype(jnp.float32)
        o_v[h] = mine_weight * nv_v[:, cols].astype(jnp.float32)
        return carry

    lax.fori_loop(0, heads, soft_step, 0)

    def value_step(j, carry):
        for u in range(P_.unroll):
            value_in(j * P_.unroll + u).wait()
        for u in range(P_.unroll):
            h = j * P_.unroll + u
            cols = pl.ds(pl.multiple_of(h * depth, depth), depth)
            for g in range(rows // P_.group):
                part = slice(g * P_.group, (g + 1) * P_.group)
                values = v_v[h, part].reshape(lanes, depth)
                mixed = jnp.dot(p_v[h, part, :], values, preferred_element_type=jnp.float32)
                att_v[part, cols] = (mixed + o_v[h, part, :]).astype(jnp.bfloat16)
        return carry

    lax.fori_loop(0, heads // P_.unroll, value_step, 0)

    alpha_x = remote(
        alpha, al_v.at[:, mine_cols], x_alpha.at[0], x_alpha.at[1], dp, other
    )
    head_x = remote(frames.at[0:late], hf_v, x_head.at[0], x_head.at[1], dp, other)

    block = tally // P_.send_blocks

    def early_x(b):
        part = pl.ds(pl.multiple_of(pad + b * block, ROW_TILE), block)
        return remote(
            act_v.at[part, mine_cols],
            act_v.at[part, mine_cols],
            x_early.at[0, b],
            x_early.at[1, b],
            dp,
            other,
        )

    def before_x(m, to_dp, sender):
        cols = pl.ds(pl.multiple_of(sender * own, own), own)
        return remote(
            act_v.at[tally : tally + pad, mine_cols],
            act_v.at[0:pad, cols],
            x_before.at[0, m],
            x_before.at[1, sender],
            to_dp,
            m,
        )

    def after_x(m, to_dp, sender):
        return remote(
            frames.at[0:pad],
            af_v.at[sender],
            x_after.at[0, m],
            x_after.at[1, sender],
            to_dp,
            m,
        )

    pl.semaphore_wait(barrier, count - 1)
    alpha_x.start()
    head_x.start()

    @pl.when(dp > 0)
    def _():
        for m in range(n_mp):
            after_x(m, dp - 1, core).start()

    for copy in (alpha_in, frames_in):
        copy.wait()
    my_alpha = al_v[:, mine_cols]
    my_turn = my_alpha * 0.3183098861837907
    my_inverse = 1.0 / my_alpha
    snake_rows = tally // steps

    def part_x(i):
        return remote(out_v.at[i], in_v.at[i], x_part.at[0, i], x_part.at[1, i], dp, other)

    def their_step(i, carry):
        @pl.when(i > 0)
        def _():
            part_x(i - 1).start()

        weight_in(i).wait()
        for k in range(snake_rows // P_.snake_rows):
            begin = i * snake_rows + k * P_.snake_rows
            part = pl.ds(pl.multiple_of(begin, P_.snake_rows), P_.snake_rows)
            where_to = pl.ds(pl.multiple_of(pad + begin, ROW_TILE), P_.snake_rows)
            act_v[where_to, mine_cols] = fast_snake(
                fr_v[part, :].astype(jnp.float32), my_alpha, my_turn, my_inverse
            )
        out_v[i] = jnp.dot(
            att_v[...], w_v[lax.rem(i, slots)], preferred_element_type=jnp.float32
        ).astype(jnp.bfloat16)
        weight_in(i + slots).start()
        return carry

    lax.fori_loop(0, steps, their_step, 0)
    part_x(steps - 1).start()

    for b in range(P_.send_blocks):
        early_x(b).start()

    @pl.when(dp < n_dp - 1)
    def _():
        for m in range(n_mp):
            before_x(m, dp + 1, core).start()


    for copy in (res_in, gain_in, bias_in):
        copy.wait()
    gains = gain_raw[...].astype(jnp.float32)
    for k in range(P_.local // 128):
        gain_v[:, k * 128 : (k + 1) * 128] = gains[k : k + 1]
    acc_v[...] = jnp.zeros_like(acc_v)
    sq_v[...] = jnp.zeros_like(sq_v)

    def produce(i):
        cols = pl.ds(pl.multiple_of(i * chunk, chunk), chunk)
        total = jnp.dot(att_v[...], w_v[lax.rem(i, slots)], preferred_element_type=jnp.float32)
        total = total + in_v[i].astype(jnp.float32) + res_v[:, cols].astype(jnp.float32)
        hidden = total.astype(jnp.bfloat16)
        hid_v[:, cols] = hidden
        wide = hidden.astype(jnp.float32)
        square = wide * wide
        squares = square[:, :128]
        for k in range(1, chunk // 128):
            squares = squares + square[:, k * 128 : (k + 1) * 128]
        sq_v[...] += squares
        normed_v[lax.rem(i, 2)] = (wide * gain_v[:, cols]).astype(jnp.bfloat16)

    def consume(i):
        cols = pl.ds(pl.multiple_of(i * chunk, chunk), chunk)
        acc_v[...] += jnp.dot(
            normed_v[lax.rem(i, 2)], cw_v[cols, :], preferred_element_type=jnp.float32
        )

    def mine_step(i, carry):
        codec_in(i - 1).wait()
        weight_in(i + steps).wait()
        part_x(i).wait_recv()
        consume(i - 1)
        produce(i)

        @pl.when(i + slots < steps)
        def _():
            weight_in(i + steps + slots).start()

        return carry

    weight_in(jnp.int32(steps)).wait()
    part_x(0).wait_recv()
    produce(jnp.int32(0))
    if slots < steps:
        weight_in(jnp.int32(steps + slots)).start()
    lax.fori_loop(1, steps, mine_step, 0)
    codec_in(steps - 1).wait()
    consume(jnp.int32(steps - 1))

    other_cols = pl.ds(pl.multiple_of(other * own, own), own)
    sendc_v[:, :own] = acc_v[:, other_cols]
    sendc_v[:, own:] = sq_v[...]
    codec_x = remote(sendc_v, recvc_v, x_codec.at[0], x_codec.at[1], dp, other)
    codec_x.start()

    def conv_block(index):
        begin, size = blocks_of(P_)[index]
        for t in range(KERNEL_TAPS):
            at = pad + begin - span + t * DILATION_STEP
            lhs_v[:size, t * channels : (t + 1) * channels] = act_v[at : at + size, :]
        audio_v[begin : begin + size, :] = (
            jnp.dot(lhs_v[:size, :], fw_v[...], preferred_element_type=jnp.float32)
            + fr_v[begin : begin + size, :].astype(jnp.float32)
            + bias_v[...]
        ).astype(jnp.bfloat16)

    codec_x.wait_recv()
    square = jnp.sum(sq_v[...] + recvc_v[:, own:], axis=1, keepdims=True)
    latent = (
        (acc_v[:, mine_cols] + recvc_v[:, :own]) * lax.rsqrt(square / P_.width + 1e-05)
    ).astype(jnp.bfloat16)
    outgoing = jnp.dot(hot_v[...], latent, preferred_element_type=jnp.float32)
    for d in range(n_dp):
        sendh_v[d] = outgoing[d * CAP : (d + 1) * CAP].astype(jnp.bfloat16)

    def copy_a(pd, pm, src_dp, src_mp, send, recv):
        return remote(
            sendh_v.at[pd], land_v.at[src_mp, src_dp], send_a.at[send], recv_a.at[recv], pd, pm
        )

    def copy_b(pd, pm, src_dp, src_mp, send, recv):
        return remote(
            sendh_v.at[pd + 1], near_v.at[src_mp, src_dp], send_b.at[send], recv_b.at[recv], pd, pm
        )

    def send_near(step, carry):
        peer, pd, pm = place(step)

        @pl.when(pd < n_dp - 1)
        def _():
            copy_b(pd, pm, dp, core, peer, me).start()

        return carry

    def send(step, carry):
        peer, pd, pm = place(step)
        copy_a(pd, pm, dp, core, peer, me).start()
        return carry

    lax.fori_loop(1, count, send, 0)

    @pl.when(dp < P_.near)
    def _():
        lax.fori_loop(1, count, send_near, 0)

    land_v[core, dp] = sendh_v[dp]

    @pl.when(dp < P_.near)
    def _():
        near_v[core, dp] = sendh_v[lax.rem(dp + 1, n_dp)]

    def wait_filter(t, carry):
        filter_in(t).wait()
        return carry

    lax.fori_loop(0, KERNEL_TAPS, wait_filter, 0)
    for b in range(P_.send_blocks):
        early_x(b).wait_recv()

    for index in range(len(blocks_of(P_))):
        conv_block(index)

    alpha_x.wait_recv()
    head_x.wait_recv()

    def finish(step, carry):
        peer, pd, pm = place(step)
        copy_a(pd, pm, pd, pm, peer, peer).wait_recv()
        return carry

    lax.fori_loop(1, count, finish, 0)
    for s in range(n_dp):
        for m in range(n_mp):
            here_v[s * CAP : (s + 1) * CAP, m * own : (m + 1) * own] = land_v[m, s].astype(
                jnp.float32
            )
    for b in range(P_.send_blocks):
        early_x(b).wait_send()
    hf = hf_v[...].astype(jnp.float32)
    mf = fr_v[0:late, :].astype(jnp.float32)

    all_alpha = al_v[...]
    all_turn = all_alpha * 0.3183098861837907
    all_inverse = 1.0 / all_alpha
    here_v[:, mine_cols] += mf
    here_v[:, other_cols] += hf
    act_v[pad : pad + late, :] = fast_snake(here_v[...], all_alpha, all_turn, all_inverse)

    @pl.when(dp < n_dp - 1)
    def _():
        for m in range(n_mp):
            after_x(0, 0, m).wait_recv()

        def take_near(sender, carry):
            @pl.when(sender != me)
            def _():
                copy_b(0, 0, sender // n_mp, lax.rem(sender, n_mp), 0, sender).wait_recv()

            return carry

        lax.fori_loop(0, P_.near * n_mp, take_near, 0)
        for m in range(n_mp):
            there_v[:, m * own : (m + 1) * own] = af_v[m].astype(jnp.float32)
            for s in range(P_.near):
                there_v[s * CAP : (s + 1) * CAP, m * own : (m + 1) * own] += near_v[m, s].astype(
                    jnp.float32
                )
        act_v[pad + tally :, :] = fast_snake(there_v[...], all_alpha, all_turn, all_inverse)

    @pl.when(dp == n_dp - 1)
    def _():
        act_v[pad + tally :, :] = jnp.zeros((pad, channels), jnp.bfloat16)

    @pl.when(dp > 0)
    def _():
        for m in range(n_mp):
            before_x(0, 0, m).wait_recv()

    @pl.when(dp == 0)
    def _():
        act_v[0:pad, :] = jnp.zeros((pad, channels), jnp.bfloat16)

    for t in range(KERNEL_TAPS):
        cols = slice(t * channels, (t + 1) * channels)
        at = pad - span + t * DILATION_STEP
        lhs_v[:front, cols] = act_v[at : at + front, :]
        at = at + tally - back
        lhs_v[front : front + back, cols] = act_v[at : at + back, :]
    edge = (
        jnp.dot(lhs_v[: front + back, :], fw_v[...], preferred_element_type=jnp.float32)
        + bias_v[...]
    )
    audio_v[:late, :] = (edge[:late] + here_v[:, mine_cols]).astype(jnp.bfloat16)
    audio_v[late:front, :] = (edge[late:front] + fr_v[late:front, :].astype(jnp.float32)).astype(
        jnp.bfloat16
    )
    audio_v[tally - back :, :] = (edge[front:] + fr_v[tally - back :, :].astype(jnp.float32)).astype(
        jnp.bfloat16
    )

    alpha_x.wait_send()
    head_x.wait_send()

    @pl.when(dp < n_dp - 1)
    def _():
        for m in range(n_mp):
            before_x(m, 0, core).wait_send()

    @pl.when(dp > 0)
    def _():
        for m in range(n_mp):
            after_x(m, 0, core).wait_send()

    def part_sent(i, carry):
        part_x(i).wait_send()
        return carry

    lax.fori_loop(0, steps, part_sent, 0)
    codec_x.wait_send()

    def sent(step, carry):
        peer, pd, pm = place(step)
        copy_a(pd, pm, dp, core, peer, me).wait_send()
        return carry

    lax.fori_loop(1, count, sent, 0)

    def sent_near(step, carry):
        peer, pd, pm = place(step)

        @pl.when(pd < n_dp - 1)
        def _():
            copy_b(pd, pm, dp, core, peer, me).wait_send()

        return carry

    @pl.when(dp < P_.near)
    def _():
        lax.fori_loop(1, count, sent_near, 0)


def store_kernel(hidden, audio, hidden_out, audio_out, sems):
    copies = (
        pltpu.make_async_copy(hidden, hidden_out, sems.at[0]),
        pltpu.make_async_copy(audio, audio_out, sems.at[1]),
    )
    for copy in copies:
        copy.start()
    for copy in copies:
        copy.wait()


def fused(
    query,
    new_key,
    new_value,
    cache_key,
    cache_value,
    cache_len,
    residual,
    out_weight,
    norm_gain,
    codec_weight,
    finished,
    owner,
    frames,
    snake_alpha,
    filter_weight,
    conv_bias,
):
    plan = Plan(query, cache_key, residual, norm_gain, codec_weight, frames)
    n_dp, n_mp = plan.n_dp, plan.n_mp
    count = n_dp * n_mp
    bf, f32, i32 = jnp.bfloat16, jnp.float32, jnp.int32
    vm = pltpu.VMEM
    dma = pltpu.SemaphoreType.DMA
    rows, own, channels, tally = plan.rows, plan.own, plan.channels, plan.tally
    taps = KERNEL_TAPS * channels
    biggest = max([size for _, size in blocks_of(plan)] + [plan.front + plan.back])
    scratch = [
        vm(query.shape, bf),
        vm(query.shape, bf),
        vm(query.shape, bf),
        vm((plan.heads, rows, plan.positions, plan.depth), bf),
        vm((plan.heads, rows, plan.positions, plan.depth), bf),
        vm((1, rows), i32),
        vm((rows, plan.local), bf),
        vm((plan.slots, plan.depth_in, plan.chunk), bf),
        vm((2, rows, plan.chunk), bf),
        vm((plan.local // 128, 128), bf),
        vm((1, plan.local), f32),
        vm((plan.local, channels), bf),
        vm((1, rows), i32),
        vm((1, rows), i32),
        vm((tally, own), bf),
        vm((1, channels), f32),
        vm((taps, own), bf),
        vm((1, own), f32),
        vm((tally + 2 * plan.pad, channels), bf),
        vm((plan.late, own), bf),
        vm((n_mp, plan.pad, own), bf),
        vm((rows, plan.group * plan.positions), f32),
        vm((plan.late, rows), bf),
        vm((rows, plan.depth_in), bf),
        vm((plan.heads, rows, plan.group * plan.positions), f32),
        vm((plan.heads, rows, plan.group * plan.positions), bf),
        vm((plan.heads, rows, plan.depth), f32),
        vm((plan.steps, rows, plan.chunk), bf),
        vm((plan.steps, rows, plan.chunk), bf),
        vm((rows, channels), f32),
        vm((rows, 128), f32),
        vm((rows, own + 128), f32),
        vm((rows, own + 128), f32),
        vm((n_dp, CAP, own), bf),
        vm((n_mp, n_dp, CAP, own), bf),
        vm((n_mp, plan.near, CAP, own), bf),
        vm((plan.late, channels), f32),
        vm((plan.pad, channels), f32),
        vm((biggest, taps), bf),
        dma((11,)),
        dma((plan.heads,)),
        dma((plan.heads,)),
        dma((plan.slots,)),
        dma((plan.steps,)),
        dma((KERNEL_TAPS,)),
        dma((2,)),
        dma((2,)),
        dma((2, plan.send_blocks)),
        dma((2, n_mp)),
        dma((2, n_mp)),
        dma((2, plan.steps)),
        dma((2,)),
        dma((count,)),
        dma((count,)),
        dma((count,)),
        dma((plan.near * n_mp,)),
    ]
    anywhere = pl.BlockSpec(memory_space=pl.ANY)
    kept = pl.BlockSpec(memory_space=pltpu.VMEM)
    operands = [
        pltpu.with_memory_space_constraint(x, pltpu.HBM)
        for x in (
        query,
        new_key,
        new_value,
        cache_key,
        cache_value,
        cache_len.reshape(1, -1),
        residual,
        out_weight,
        norm_gain.reshape(-1, 128),
        codec_weight,
        finished.reshape(1, -1),
        owner.reshape(1, -1),
        frames,
        snake_alpha.reshape(1, -1),
        filter_weight.reshape(taps, own),
        conv_bias.reshape(1, -1),
        )
    ]
    kept_pair = pl.pallas_call(
        functools.partial(fused_kernel, plan),
        out_shape=(
            jax.ShapeDtypeStruct((rows, plan.local), bf),
            jax.ShapeDtypeStruct((tally, own), bf),
        ),
        in_specs=[pl.BlockSpec(memory_space=pltpu.HBM)] * 16,
        out_specs=(kept, kept),
        scratch_shapes=scratch,
        compiler_params=pltpu.CompilerParams(
            collective_id=1, has_side_effects=True, vmem_limit_bytes=VMEM_BYTES
        ),
    )(*operands)
    return pl.pallas_call(
        store_kernel,
        out_shape=(
            jax.ShapeDtypeStruct((rows, plan.local), bf),
            jax.ShapeDtypeStruct((tally, own), bf),
        ),
        in_specs=[kept, kept],
        out_specs=(anywhere, anywhere),
        scratch_shapes=[dma((2,))],
        compiler_params=pltpu.CompilerParams(vmem_limit_bytes=4 * 1024 * 1024),
    )(*kept_pair)


VMEM_BYTES = 48 * 1000 * 1000


def step(*args):
    return fused(*args) if lax.axis_size("mp") == 2 else body(*args)


def solution(mesh):
    placed = (
        P("dp", "mp"),
        P("dp", "mp"),
        P("dp", "mp"),
        P("dp", "mp", None, None),
        P("dp", "mp", None, None),
        P("dp"),
        P("dp", None),
        P("mp", None),
        P("mp"),
        P("mp", None),
        P("dp"),
        P("dp"),
        P("dp", "mp"),
        P("mp"),
        P(None, None, "mp"),
        P("mp"),
    )
    return jax.shard_map(
        step, mesh=mesh, in_specs=placed, out_specs=(P("dp", "mp"), P("dp", "mp")), check_vma=False
    )
```

```python
import functools
import jax
import jax.numpy as jnp
from jax import lax
from jax.experimental import pallas as pl
from jax.experimental.pallas import tpu as pltpu
from jax.sharding import PartitionSpec as P

KERNEL_TAPS = 7
DILATION_STEP = 3
CAP = 4
ROW_TILE = 16


def swap(x):
    return lax.ppermute(x, "mp", [(0, 1), (1, 0)])


def gather_mp(x, axis):
    if lax.axis_size("mp") != 2:
        return lax.all_gather(x, "mp", axis=axis, tiled=True)
    other = swap(x)
    first = lax.axis_index("mp") == 0
    return jnp.concatenate([jnp.where(first, x, other), jnp.where(first, other, x)], axis=axis)


def sin_squared(x):
    turns = jnp.round(x * 0.3183098861837907)
    r = (x - turns * 3.140625) - turns * 0.0009676535897932
    q = r * r
    p = -2.5052108e-08 + q * 1.6059044e-10
    p = 2.7557319e-06 + q * p
    p = -1.9841270e-04 + q * p
    p = 8.3333333e-03 + q * p
    p = -1.6666667e-01 + q * p
    sine = r + r * (q * p)
    return sine * sine


def snake(mix, alpha):
    return (mix + sin_squared(alpha * mix) / alpha).astype(jnp.bfloat16)


def columns_kernel(start_ref, x_ref, w_ref, o_ref):
    del start_ref
    o_ref[...] = jnp.dot(x_ref[...], w_ref[...], preferred_element_type=jnp.float32).astype(
        o_ref.dtype
    )


def columns_dot(x, w, start, width, tile, dtype):
    rows, depth = x.shape
    return pl.pallas_call(
        columns_kernel,
        out_shape=jax.ShapeDtypeStruct((rows, width), dtype),
        grid_spec=pltpu.PrefetchScalarGridSpec(
            num_scalar_prefetch=1,
            grid=(width // tile,),
            in_specs=[
                pl.BlockSpec((rows, depth), lambda j, s: (0, 0)),
                pl.BlockSpec((depth, tile), lambda j, s: (0, s[0] + j)),
            ],
            out_specs=pl.BlockSpec((rows, tile), lambda j, s: (0, j)),
        ),
        compiler_params=pltpu.CompilerParams(vmem_limit_bytes=28 * 1024 * 1024),
        cost_estimate=pl.CostEstimate(
            flops=2 * rows * depth * width, bytes_accessed=2 * depth * width, transcendentals=0
        ),
    )(jnp.full((1,), start, jnp.int32), x, w)


def handoff_kernel(
    n_dp, n_mp, near, out_ref, a_ref, b_ref, land_a, land_b, send_a, recv_a, send_b, recv_b
):
    dp = lax.axis_index("dp")
    mp = lax.axis_index("mp")
    count = n_dp * n_mp
    me = dp * n_mp + mp
    barrier = pltpu.get_barrier_semaphore()

    def place(step):
        peer = lax.rem(me + step, count)
        return peer, peer // n_mp, lax.rem(peer, n_mp)

    def greet(step, carry):
        _, pd, pm = place(step)
        pl.semaphore_signal(
            barrier, inc=1, device_id=(pd, pm), device_id_type=pl.DeviceIdType.MESH
        )
        return carry

    lax.fori_loop(1, count, greet, 0)
    pl.semaphore_wait(barrier, count - 1)

    def copy_a(pd, pm, send, recv):
        return pltpu.make_async_remote_copy(
            src_ref=out_ref.at[pd],
            dst_ref=land_a.at[me],
            send_sem=send_a.at[send],
            recv_sem=recv_a.at[recv],
            device_id=(pd, pm),
            device_id_type=pl.DeviceIdType.MESH,
        )

    def copy_b(slot, pd, pm, send, recv):
        return pltpu.make_async_remote_copy(
            src_ref=out_ref.at[pd + 1],
            dst_ref=land_b.at[slot],
            send_sem=send_b.at[send],
            recv_sem=recv_b.at[recv],
            device_id=(pd, pm),
            device_id_type=pl.DeviceIdType.MESH,
        )

    def send(step, carry):
        peer, pd, pm = place(step)
        copy_a(pd, pm, peer, me).start()
        return carry

    def send_near(step, carry):
        peer, pd, pm = place(step)
        copy_b(me, pd, pm, peer, me).start()
        return carry

    @pl.when(dp < near)
    def _():
        lax.fori_loop(1, count, send_near, 0)

    lax.fori_loop(1, count, send, 0)
    land_a[me] = out_ref[dp]

    @pl.when(dp < near)
    def _():
        land_b[me] = out_ref[dp + 1]

    def finish(step, carry):
        peer, pd, pm = place(step)
        copy = copy_a(pd, pm, peer, peer)
        copy.wait_recv()
        copy.wait_send()
        return carry

    def finish_near(step, carry):
        peer, pd, pm = place(step)
        copy_b(me, pd, pm, peer, me).wait_send()
        return carry

    def take_near(sender, carry):
        @pl.when(sender != me)
        def _():
            copy_b(sender, 0, 0, sender, sender).wait_recv()

        return carry

    lax.fori_loop(1, count, finish, 0)

    @pl.when(dp < near)
    def _():
        lax.fori_loop(1, count, finish_near, 0)

    lax.fori_loop(0, near * n_mp, take_near, 0)

    def total_of(land, first):
        total = land[first].astype(jnp.float32)
        for m in range(1, n_mp):
            total = total + land[first + m].astype(jnp.float32)
        return total

    def put(d, carry):
        a_ref[d] = total_of(land_a, d * n_mp)
        return carry

    lax.fori_loop(0, n_dp, put, 0)
    for d in range(near):
        b_ref[d] = total_of(land_b, d * n_mp)


def handoff(outgoing, near):
    n_dp, n_mp = lax.axis_size("dp"), lax.axis_size("mp")
    count = n_dp * n_mp
    _, cap, width = outgoing.shape
    vmem = pl.BlockSpec(memory_space=pltpu.VMEM)
    return pl.pallas_call(
        functools.partial(handoff_kernel, n_dp, n_mp, near),
        out_shape=(
            jax.ShapeDtypeStruct((n_dp, cap, width), jnp.float32),
            jax.ShapeDtypeStruct((near, cap, width), jnp.float32),
        ),
        in_specs=[vmem],
        out_specs=(vmem, vmem),
        scratch_shapes=[
            pltpu.VMEM((count, cap, width), jnp.bfloat16),
            pltpu.VMEM((near * n_mp, cap, width), jnp.bfloat16),
            pltpu.SemaphoreType.DMA((count,)),
            pltpu.SemaphoreType.DMA((count,)),
            pltpu.SemaphoreType.DMA((count,)),
            pltpu.SemaphoreType.DMA((near * n_mp,)),
        ],
        compiler_params=pltpu.CompilerParams(
            collective_id=0, has_side_effects=True, vmem_limit_bytes=16 * 1024 * 1024
        ),
    )(outgoing)


def round_up(n, tile):
    return -(-n // tile) * tile


def taps_of(cells, rows):
    parts = [cells[t * DILATION_STEP : t * DILATION_STEP + rows] for t in range(KERNEL_TAPS)]
    return jnp.concatenate(parts, axis=1)


def attend(query, new_key, new_value, cache_key, cache_value, cache_len):
    count, heads, positions, depth = cache_key.shape
    scale = 1.0 / jnp.sqrt(jnp.float32(depth))
    queries = query.reshape(count, heads, depth)
    fresh_key = new_key.reshape(count, heads, depth)
    fresh_value = new_value.reshape(count, heads, depth)
    scores = (
        jnp.einsum("rhd,rhld->rhl", queries, cache_key, preferred_element_type=jnp.float32) * scale
    )
    own_score = (
        jnp.einsum("rhd,rhd->rh", queries, fresh_key, preferred_element_type=jnp.float32) * scale
    )
    valid = jnp.arange(positions, dtype=jnp.int32)[None, :] < cache_len[:, None]
    scores = jnp.where(valid[:, None, :], scores, -1e30)
    top = jnp.maximum(jnp.max(scores, axis=-1), own_score)
    expo = jnp.where(valid[:, None, :], jnp.exp(scores - top[..., None]), 0.0)
    own_expo = jnp.exp(own_score - top)
    total = jnp.sum(expo, axis=-1) + own_expo
    weights = (expo / total[..., None]).astype(jnp.bfloat16)
    own_weight = (own_expo / total).astype(jnp.bfloat16)
    mixed = jnp.einsum("rhl,rhld->rhd", weights, cache_value, preferred_element_type=jnp.float32)
    mixed = mixed + own_weight.astype(jnp.float32)[..., None] * fresh_value.astype(jnp.float32)
    return mixed.astype(jnp.bfloat16).reshape(count, heads * depth)


def body(
    query,
    new_key,
    new_value,
    cache_key,
    cache_value,
    cache_len,
    residual,
    out_weight,
    norm_gain,
    codec_weight,
    finished,
    owner,
    frames,
    snake_alpha,
    filter_weight,
    conv_bias,
):
    owners = lax.axis_size("dp")
    n_mp = lax.axis_size("mp")
    core = lax.axis_index("mp")
    tally, own = frames.shape
    span = KERNEL_TAPS // 2 * DILATION_STEP
    late = owners * CAP
    near = -(-span // CAP)
    front = round_up(late + span, ROW_TILE)
    back = round_up(span, ROW_TILE)

    wide_frames = frames.astype(jnp.float32)
    alpha_all = gather_mp(snake_alpha, 0)
    early = gather_mp(snake(wide_frames, snake_alpha), 1)
    head_frames = gather_mp(frames[:late], 1)
    before = lax.ppermute(early[tally - span :], "dp", [(i, i + 1) for i in range(owners - 1)])
    after_frames = lax.ppermute(
        head_frames[: near * CAP], "dp", [(i + 1, i) for i in range(owners - 1)]
    )
    middle = tally - front - back
    main = wide_frames[front : tally - back] + conv_bias
    for t in range(KERNEL_TAPS):
        start = front - span + t * DILATION_STEP
        main = main + jnp.dot(
            early[start : start + middle], filter_weight[t], preferred_element_type=jnp.float32
        )
    main = main.astype(jnp.bfloat16)

    attended = attend(query, new_key, new_value, cache_key, cache_value, cache_len)
    count = attended.shape[0]
    width = out_weight.shape[1]
    local_width = norm_gain.shape[0]
    residual_part = lax.dynamic_slice_in_dim(residual, core * local_width, local_width, 1)
    if n_mp == 2:
        tile = 1024
        theirs = columns_dot(
            attended, out_weight, (1 - core) * (local_width // tile), local_width, tile, jnp.bfloat16
        )
        arrived = swap(theirs)
        mine = columns_dot(
            attended, out_weight, core * (local_width // tile), local_width, tile, jnp.float32
        )
        projected = mine + arrived.astype(jnp.float32)
    else:
        term = jnp.dot(attended, out_weight, preferred_element_type=jnp.float32)
        projected = lax.psum_scatter(term, "mp", scatter_dimension=1, tiled=True)
    hidden = (residual_part.astype(jnp.float32) + projected).astype(jnp.bfloat16)
    wide = hidden.astype(jnp.float32)
    squares = jnp.sum(wide * wide, axis=-1)
    squares = squares + swap(squares) if n_mp == 2 else lax.psum(squares, "mp")
    meansq = squares / width
    normed = (wide * norm_gain.astype(jnp.float32)).astype(jnp.bfloat16)
    channels = codec_weight.shape[1]
    share = columns_dot(normed, codec_weight, 0, channels, 256, jnp.float32)
    share = (share * lax.rsqrt(meansq + 1e-05)[:, None]).astype(jnp.bfloat16)

    index = jnp.arange(count, dtype=jnp.int32)
    earlier = (
        (owner[:, None] == owner[None, :])
        & (finished[None, :] == 1)
        & (index[None, :] < index[:, None])
    )
    slot = jnp.sum(earlier.astype(jnp.int32), axis=1)
    target = owner * CAP + slot
    places = jnp.arange((owners + 1) * CAP, dtype=jnp.int32)
    onehot = ((places[:, None] == target[None, :]) & (finished[None, :] == 1)).astype(jnp.bfloat16)
    outgoing = jnp.dot(onehot, share, preferred_element_type=jnp.float32).astype(jnp.bfloat16)
    here, there = handoff(outgoing.reshape(owners + 1, CAP, channels), near)
    here = here.reshape(late, channels).astype(jnp.bfloat16).astype(jnp.float32)
    there = there.reshape(near * CAP, channels).astype(jnp.bfloat16).astype(jnp.float32)

    head_mix = head_frames.astype(jnp.float32) + here
    head_act = snake(head_mix, alpha_all)
    after = snake(after_frames.astype(jnp.float32) + there, alpha_all)[:span]
    cells_a = jnp.concatenate([before, head_act, early[late : front + span]], axis=0)
    cells_b = jnp.concatenate([early[tally - back - span :], after], axis=0)
    edges = jnp.concatenate([taps_of(cells_a, front), taps_of(cells_b, back)], axis=0)
    flat = filter_weight.reshape(KERNEL_TAPS * channels, own)
    own_mix = lax.dynamic_slice_in_dim(head_mix, core * own, own, 1)
    edge_mix = jnp.concatenate(
        [own_mix, wide_frames[late:front], wide_frames[tally - back :]], axis=0
    )
    edge = jnp.dot(edges, flat, preferred_element_type=jnp.float32) + edge_mix + conv_bias
    edge = edge.astype(jnp.bfloat16)
    audio = jnp.concatenate([edge[:front], main, edge[front:]], axis=0)
    return (hidden, audio)


MESH = pl.DeviceIdType.MESH
SIN_SQUARED = (
    1.0,
    -0.3333333134651184,
    0.04444440081715584,
    -0.003174516372382641,
    0.00014100516273174435,
    -4.2275191844964866e-06,
    8.055603473167139e-08,
)
ROUNDER = 12582912.0


def fast_snake(mix, alpha, turn, inverse):
    turns = (mix * turn + ROUNDER) - ROUNDER
    r = (mix * alpha - turns * 3.140625) - turns * 0.0009676535897932
    q = r * r
    p = SIN_SQUARED[-1] * q + SIN_SQUARED[-2]
    for c in SIN_SQUARED[-3::-1]:
        p = p * q + c
    return (mix + (q * p) * inverse).astype(jnp.bfloat16)


def iota(shape, axis):
    return lax.broadcasted_iota(jnp.int32, shape, axis)


def column_of(row, size):
    spread = jnp.broadcast_to(row, (size, size))
    return jnp.sum(
        jnp.where(iota((size, size), 0) == iota((size, size), 1), spread, 0), axis=1, keepdims=True
    )


class Plan:
    def __init__(self, query, cache_key, residual, norm_gain, codec_weight, frames):
        self.n_dp, self.n_mp = lax.axis_size("dp"), lax.axis_size("mp")
        self.rows, self.heads, self.positions, self.depth = cache_key.shape
        self.width = residual.shape[1]
        self.local = norm_gain.shape[0]
        self.channels = codec_weight.shape[1]
        self.tally, self.own = frames.shape
        self.late = self.n_dp * CAP
        self.span = KERNEL_TAPS // 2 * DILATION_STEP
        self.near = -(-self.span // CAP)
        self.pad = round_up(self.span, ROW_TILE)
        self.front = round_up(self.late + self.span, ROW_TILE)
        self.back = self.pad
        self.middle = self.tally - self.front - self.back
        self.chunk = 512
        self.steps = self.local // self.chunk
        self.slots = min(6, self.steps)
        self.group = ROW_TILE
        self.snake_rows = 32
        self.send_blocks = 4
        self.depth_in = self.heads * self.depth
        self.unroll = 8
        self.octet = 8


def blocks_of(plan):
    count = 5
    unit = plan.middle // ROW_TILE
    sizes = [(unit // count + (1 if i < unit % count else 0)) * ROW_TILE for i in range(count)]
    starts = [plan.front + sum(sizes[:i]) for i in range(count)]
    return list(zip(starts, sizes))


def fused_kernel(
    P_,
    query,
    new_key,
    new_value,
    cache_key,
    cache_value,
    lens,
    residual,
    out_weight,
    gain,
    codec_weight,
    finished,
    owner,
    frames,
    alpha,
    filters,
    bias,
    hid_v,
    audio_v,
    q_v,
    nk_v,
    nv_v,
    k_v,
    v_v,
    len_v,
    res_v,
    w_v,
    normed_v,
    gain_raw,
    gain_v,
    cw_v,
    fin_v,
    own_v,
    fr_v,
    al_v,
    fw_v,
    bias_v,
    act_v,
    hf_v,
    af_v,
    valid_v,
    hot_v,
    att_v,
    score_v,
    p_v,
    o_v,
    out_v,
    in_v,
    acc_v,
    sq_v,
    sendc_v,
    recvc_v,
    sendh_v,
    land_v,
    near_v,
    here_v,
    there_v,
    lhs_v,
    s_in,
    s_k,
    s_v,
    s_w,
    s_cw,
    s_fw,
    x_alpha,
    x_head,
    x_early,
    x_before,
    x_after,
    x_part,
    x_codec,
    send_a,
    recv_a,
    send_b,
    recv_b,
):
    n_dp, n_mp = P_.n_dp, P_.n_mp
    count = n_dp * n_mp
    rows, heads, positions, depth = P_.rows, P_.heads, P_.positions, P_.depth
    chunk, steps, slots = P_.chunk, P_.steps, P_.slots
    own, channels, tally, pad = P_.own, P_.channels, P_.tally, P_.pad
    late, span, front, back = P_.late, P_.span, P_.front, P_.back
    dp = lax.axis_index("dp")
    core = lax.axis_index("mp")
    me = dp * n_mp + core
    other = 1 - core
    mine_cols = pl.ds(pl.multiple_of(core * own, own), own)
    local_cols = pl.ds(pl.multiple_of(core * P_.local, P_.local), P_.local)

    def local(src, dst, sem):
        return pltpu.make_async_copy(src, dst, sem)

    def remote(src, dst, send, recv, to_dp, to_mp):
        return pltpu.make_async_remote_copy(
            src_ref=src,
            dst_ref=dst,
            send_sem=send,
            recv_sem=recv,
            device_id=(to_dp, to_mp),
            device_id_type=MESH,
        )

    frames_in = local(frames, fr_v, s_in.at[0])
    alpha_in = local(alpha, al_v.at[:, mine_cols], s_in.at[1])
    lens_in = local(lens, len_v, s_in.at[2])
    fin_in = local(finished, fin_v, s_in.at[3])
    own_in = local(owner, own_v, s_in.at[4])
    q_in = local(query, q_v, s_in.at[5])
    nk_in = local(new_key, nk_v, s_in.at[6])
    nv_in = local(new_value, nv_v, s_in.at[7])
    res_in = local(residual.at[:, local_cols], res_v, s_in.at[8])
    gain_in = local(gain, gain_raw, s_in.at[9])
    bias_in = local(bias, bias_v, s_in.at[10])

    def key_in(h):
        return local(cache_key.at[:, h], k_v.at[h], s_k.at[h])

    def value_in(h):
        return local(cache_value.at[:, h], v_v.at[h], s_v.at[h])

    def weight_in(i):
        begin = lax.select(i < steps, other * P_.local, core * P_.local) + lax.rem(i, steps) * chunk
        return local(
            out_weight.at[:, pl.ds(pl.multiple_of(begin, chunk), chunk)],
            w_v.at[lax.rem(i, slots)],
            s_w.at[lax.rem(i, slots)],
        )

    def codec_in(i):
        part = pl.ds(pl.multiple_of(i * chunk, chunk), chunk)
        return local(codec_weight.at[part, :], cw_v.at[part, :], s_cw.at[i])

    def filter_in(t):
        part = pl.ds(pl.multiple_of(t * channels, channels), channels)
        return local(filters.at[part, :], fw_v.at[part, :], s_fw.at[t])

    for copy in (lens_in, q_in, nk_in):
        copy.start()

    def start_key(h, carry):
        key_in(h).start()
        return carry

    def start_value(h, carry):
        value_in(h).start()
        return carry

    lax.fori_loop(0, heads, start_key, 0)
    lax.fori_loop(0, heads, start_value, 0)
    for copy in (nv_in, alpha_in, fin_in, own_in, frames_in):
        copy.start()

    barrier = pltpu.get_barrier_semaphore()

    def place(step):
        peer = lax.rem(me + step, count)
        return peer, peer // n_mp, lax.rem(peer, n_mp)

    def greet(step, carry):
        _, pd, pm = place(step)
        pl.semaphore_signal(barrier, inc=1, device_id=(pd, pm), device_id_type=MESH)
        return carry

    lax.fori_loop(1, count, greet, 0)

    def start_weight(i, carry):
        weight_in(i).start()
        return carry

    lax.fori_loop(0, slots, start_weight, 0)
    for copy in (res_in, gain_in, bias_in):
        copy.start()

    def start_codec(i, carry):
        codec_in(i).start()
        return carry

    lax.fori_loop(0, steps, start_codec, 0)

    def start_filter(t, carry):
        filter_in(t).start()
        return carry

    for copy in (lens_in, fin_in, own_in):
        copy.wait()

    length = column_of(len_v[...], rows)
    lanes = P_.group * positions
    lane = iota((rows, lanes), 1)
    line = lax.rem(iota((rows, lanes), 0), P_.group)
    valid = (lane // positions == line) & (lax.rem(lane, positions) < length)
    valid_v[...] = jnp.where(valid, 0.0, -1e30)

    owner_row, done_row = own_v[...], fin_v[...]
    owner_col, done_col = column_of(owner_row, rows), column_of(done_row, rows)
    earlier = (
        (owner_col == owner_row)
        & (done_col == 1)
        & (iota((rows, rows), 0) < iota((rows, rows), 1))
    )
    slot = jnp.sum(jnp.where(earlier, 1, 0), axis=0, keepdims=True)
    target = jnp.where(done_row == 1, owner_row * CAP + slot, -1)
    hot_v[...] = jnp.where(iota((late, rows), 0) == target, 1.0, 0.0).astype(jnp.bfloat16)

    for copy in (q_in, nk_in, nv_in):
        copy.wait()
    scale = 1.0 / jnp.sqrt(jnp.float32(depth))

    def score_step(j, carry):
        for u in range(P_.octet):
            key_in(j * P_.octet + u).wait()
        lane_head = iota((depth, P_.octet * P_.group), 1) // P_.group
        for g in range(rows // P_.group):
            part = slice(g * P_.group, (g + 1) * P_.group)
            stacked, keys = [], []
            for u in range(P_.octet):
                h = j * P_.octet + u
                cols = pl.ds(pl.multiple_of(h * depth, depth), depth)
                stacked.append(q_v[part, cols].astype(jnp.float32))
                keys.append(k_v[h, part].reshape(lanes, depth))
            turned = jnp.concatenate(stacked, axis=0).T
            queries = [
                jnp.where(lane_head == u, turned, 0.0).astype(jnp.bfloat16)
                for u in range(P_.octet)
            ]
            found = jnp.dot(
                jnp.concatenate(keys, axis=1),
                jnp.concatenate(queries, axis=0),
                preferred_element_type=jnp.float32,
            ).T
            for u in range(P_.octet):
                score_v[j * P_.octet + u, part, :] = found[u * P_.group : (u + 1) * P_.group]
        return carry

    lax.fori_loop(0, heads // P_.octet, score_step, 0)

    def soft_step(h, carry):
        cols = pl.ds(pl.multiple_of(h * depth, depth), depth)
        s = jnp.where(valid_v[...] < 0.0, -1e30, score_v[h] * scale)
        mine = q_v[:, cols].astype(jnp.float32) * nk_v[:, cols].astype(jnp.float32)
        mine = jnp.sum(mine, axis=1, keepdims=True) * scale
        top = jnp.maximum(jnp.max(s, axis=1, keepdims=True), mine)
        expo = jnp.exp(s - top)
        mine_expo = jnp.exp(mine - top)
        share = 1.0 / (jnp.sum(expo, axis=1, keepdims=True) + mine_expo)
        p_v[h] = (expo * share).astype(jnp.bfloat16)
        mine_weight = (mine_expo * share).astype(jnp.bfloat16).astype(jnp.float32)
        o_v[h] = mine_weight * nv_v[:, cols].astype(jnp.float32)
        return carry

    lax.fori_loop(0, heads, soft_step, 0)

    def value_step(j, carry):
        for u in range(P_.unroll):
            value_in(j * P_.unroll + u).wait()
        for u in range(P_.unroll):
            h = j * P_.unroll + u
            cols = pl.ds(pl.multiple_of(h * depth, depth), depth)
            for g in range(rows // P_.group):
                part = slice(g * P_.group, (g + 1) * P_.group)
                values = v_v[h, part].reshape(lanes, depth)
                mixed = jnp.dot(p_v[h, part, :], values, preferred_element_type=jnp.float32)
                att_v[part, cols] = (mixed + o_v[h, part, :]).astype(jnp.bfloat16)
        return carry

    lax.fori_loop(0, heads // P_.unroll, value_step, 0)

    alpha_x = remote(
        alpha, al_v.at[:, mine_cols], x_alpha.at[0], x_alpha.at[1], dp, other
    )
    head_x = remote(frames.at[0:late], hf_v, x_head.at[0], x_head.at[1], dp, other)

    block = tally // P_.send_blocks

    def early_x(b):
        part = pl.ds(pl.multiple_of(pad + b * block, ROW_TILE), block)
        return remote(
            act_v.at[part, mine_cols],
            act_v.at[part, mine_cols],
            x_early.at[0, b],
            x_early.at[1, b],
            dp,
            other,
        )

    def before_x(m, to_dp, sender):
        cols = pl.ds(pl.multiple_of(sender * own, own), own)
        return remote(
            act_v.at[tally : tally + pad, mine_cols],
            act_v.at[0:pad, cols],
            x_before.at[0, m],
            x_before.at[1, sender],
            to_dp,
            m,
        )

    def after_x(m, to_dp, sender):
        return remote(
            frames.at[0:pad],
            af_v.at[sender],
            x_after.at[0, m],
            x_after.at[1, sender],
            to_dp,
            m,
        )

    pl.semaphore_wait(barrier, count - 1)
    alpha_x.start()
    head_x.start()

    @pl.when(dp > 0)
    def _():
        for m in range(n_mp):
            after_x(m, dp - 1, core).start()


    for copy in (alpha_in, frames_in):
        copy.wait()
    my_alpha = al_v[:, mine_cols]
    my_turn = my_alpha * 0.3183098861837907
    my_inverse = 1.0 / my_alpha
    snake_rows = tally // steps

    def part_x(i):
        return remote(out_v.at[i], in_v.at[i], x_part.at[0, i], x_part.at[1, i], dp, other)

    def their_step(i, carry):
        @pl.when(i > 0)
        def _():
            part_x(i - 1).start()

        weight_in(i).wait()
        for k in range(snake_rows // P_.snake_rows):
            begin = i * snake_rows + k * P_.snake_rows
            part = pl.ds(pl.multiple_of(begin, P_.snake_rows), P_.snake_rows)
            where_to = pl.ds(pl.multiple_of(pad + begin, ROW_TILE), P_.snake_rows)
            act_v[where_to, mine_cols] = fast_snake(
                fr_v[part, :].astype(jnp.float32), my_alpha, my_turn, my_inverse
            )
        out_v[i] = jnp.dot(
            att_v[...], w_v[lax.rem(i, slots)], preferred_element_type=jnp.float32
        ).astype(jnp.bfloat16)
        weight_in(i + slots).start()
        return carry

    lax.fori_loop(0, steps, their_step, 0)
    part_x(steps - 1).start()
    for b in range(P_.send_blocks):
        early_x(b).start()

    @pl.when(dp < n_dp - 1)
    def _():
        for m in range(n_mp):
            before_x(m, dp + 1, core).start()


    for copy in (res_in, gain_in, bias_in):
        copy.wait()
    gains = gain_raw[...].astype(jnp.float32)
    for k in range(P_.local // 128):
        gain_v[:, k * 128 : (k + 1) * 128] = gains[k : k + 1]
    acc_v[...] = jnp.zeros_like(acc_v)
    sq_v[...] = jnp.zeros_like(sq_v)

    def produce(i, first=False):
        cols = pl.ds(pl.multiple_of(i * chunk, chunk), chunk)
        total = jnp.dot(att_v[...], w_v[lax.rem(i + steps, slots)], preferred_element_type=jnp.float32)
        if first:
            part_x(0).wait_recv()
        total = total + in_v[i].astype(jnp.float32) + res_v[:, cols].astype(jnp.float32)
        hidden = total.astype(jnp.bfloat16)
        hid_v[:, cols] = hidden
        wide = hidden.astype(jnp.float32)
        square = wide * wide
        squares = square[:, :128]
        for k in range(1, chunk // 128):
            squares = squares + square[:, k * 128 : (k + 1) * 128]
        sq_v[...] += squares
        normed_v[lax.rem(i, 2)] = (wide * gain_v[:, cols]).astype(jnp.bfloat16)

    def consume(i):
        cols = pl.ds(pl.multiple_of(i * chunk, chunk), chunk)
        acc_v[...] += jnp.dot(
            normed_v[lax.rem(i, 2)], cw_v[cols, :], preferred_element_type=jnp.float32
        )

    def mine_step(i, carry):
        codec_in(i - 1).wait()
        weight_in(i + steps).wait()
        part_x(i).wait_recv()
        consume(i - 1)
        produce(i)

        @pl.when(i + slots < steps)
        def _():
            weight_in(i + steps + slots).start()

        @pl.when(i == max(1, steps - slots))
        def _():
            lax.fori_loop(0, KERNEL_TAPS, start_filter, 0)

        return carry

    weight_in(jnp.int32(steps)).wait()
    produce(jnp.int32(0), True)
    if slots < steps:
        weight_in(jnp.int32(steps + slots)).start()
    lax.fori_loop(1, steps, mine_step, 0)
    codec_in(steps - 1).wait()
    consume(jnp.int32(steps - 1))

    other_cols = pl.ds(pl.multiple_of(other * own, own), own)
    sendc_v[:, :own] = acc_v[:, other_cols]
    sendc_v[:, own:] = sq_v[...]
    codec_x = remote(sendc_v, recvc_v, x_codec.at[0], x_codec.at[1], dp, other)
    codec_x.start()

    def conv_block(index):
        begin, size = blocks_of(P_)[index]
        for t in range(KERNEL_TAPS):
            at = pad + begin - span + t * DILATION_STEP
            lhs_v[:size, t * channels : (t + 1) * channels] = act_v[at : at + size, :]
        audio_v[begin : begin + size, :] = (
            jnp.dot(lhs_v[:size, :], fw_v[...], preferred_element_type=jnp.float32)
            + fr_v[begin : begin + size, :].astype(jnp.float32)
            + bias_v[...]
        ).astype(jnp.bfloat16)

    codec_x.wait_recv()
    square = jnp.sum(sq_v[...] + recvc_v[:, own:], axis=1, keepdims=True)
    latent = (
        (acc_v[:, mine_cols] + recvc_v[:, :own]) * lax.rsqrt(square / P_.width + 1e-05)
    ).astype(jnp.bfloat16)
    outgoing = jnp.dot(hot_v[...], latent, preferred_element_type=jnp.float32)
    for d in range(n_dp):
        sendh_v[d] = outgoing[d * CAP : (d + 1) * CAP].astype(jnp.bfloat16)

    def copy_a(pd, pm, src_dp, src_mp, send, recv):
        return remote(
            sendh_v.at[pd], land_v.at[src_mp, src_dp], send_a.at[send], recv_a.at[recv], pd, pm
        )

    def copy_b(pd, pm, src_dp, src_mp, send, recv):
        return remote(
            sendh_v.at[pd + 1], near_v.at[src_mp, src_dp], send_b.at[send], recv_b.at[recv], pd, pm
        )

    def send_near(step, carry):
        peer, pd, pm = place(step)

        @pl.when(pd < n_dp - 1)
        def _():
            copy_b(pd, pm, dp, core, peer, me).start()

        return carry

    def send(step, carry):
        peer, pd, pm = place(step)
        copy_a(pd, pm, dp, core, peer, me).start()
        return carry

    lax.fori_loop(1, count, send, 0)

    @pl.when(dp < P_.near)
    def _():
        lax.fori_loop(1, count, send_near, 0)

    land_v[core, dp] = sendh_v[dp]

    @pl.when(dp < P_.near)
    def _():
        near_v[core, dp] = sendh_v[lax.rem(dp + 1, n_dp)]

    def wait_filter(t, carry):
        filter_in(t).wait()
        return carry

    lax.fori_loop(0, KERNEL_TAPS, wait_filter, 0)
    for b in range(P_.send_blocks):
        early_x(b).wait_recv()

    for index in range(len(blocks_of(P_))):
        conv_block(index)

    alpha_x.wait_recv()
    head_x.wait_recv()

    all_alpha = al_v[...]
    all_turn = all_alpha * 0.3183098861837907
    all_inverse = 1.0 / all_alpha
    here_v[:, mine_cols] = fr_v[0:late, :].astype(jnp.float32)
    here_v[:, other_cols] = hf_v[...].astype(jnp.float32)

    @pl.when(dp < n_dp - 1)
    def _():
        for m in range(n_mp):
            after_x(0, 0, m).wait_recv()
            there_v[:, m * own : (m + 1) * own] = af_v[m].astype(jnp.float32)

    for b in range(P_.send_blocks):
        early_x(b).wait_send()
    @pl.when(dp > 0)
    def _():
        for m in range(n_mp):
            before_x(0, 0, m).wait_recv()

    @pl.when(dp == 0)
    def _():
        act_v[0:pad, :] = jnp.zeros((pad, channels), jnp.bfloat16)

    alpha_x.wait_send()
    head_x.wait_send()

    @pl.when(dp < n_dp - 1)
    def _():
        for m in range(n_mp):
            before_x(m, 0, core).wait_send()

    @pl.when(dp > 0)
    def _():
        for m in range(n_mp):
            after_x(m, 0, core).wait_send()

    def part_sent(i, carry):
        part_x(i).wait_send()
        return carry

    lax.fori_loop(0, steps, part_sent, 0)
    codec_x.wait_send()

    def sent(step, carry):
        peer, pd, pm = place(step)
        copy_a(pd, pm, dp, core, peer, me).wait_send()
        return carry

    lax.fori_loop(1, count, sent, 0)

    def sent_near(step, carry):
        peer, pd, pm = place(step)

        @pl.when(pd < n_dp - 1)
        def _():
            copy_b(pd, pm, dp, core, peer, me).wait_send()

        return carry

    @pl.when(dp < P_.near)
    def _():
        lax.fori_loop(1, count, sent_near, 0)

    for s in range(n_dp):
        for m in range(n_mp):

            @pl.when(me != s * n_mp + m)
            def _(s=s, m=m):
                copy_a(0, 0, s, m, 0, s * n_mp + m).wait_recv()

            here_v[s * CAP : (s + 1) * CAP, m * own : (m + 1) * own] += land_v[m, s].astype(
                jnp.float32
            )
    act_v[pad : pad + late, :] = fast_snake(here_v[...], all_alpha, all_turn, all_inverse)

    @pl.when(dp < n_dp - 1)
    def _():
        def take_near(sender, carry):
            @pl.when(sender != me)
            def _():
                copy_b(0, 0, sender // n_mp, lax.rem(sender, n_mp), 0, sender).wait_recv()

            return carry

        lax.fori_loop(0, P_.near * n_mp, take_near, 0)
        for m in range(n_mp):
            for s in range(P_.near):
                there_v[s * CAP : (s + 1) * CAP, m * own : (m + 1) * own] += near_v[m, s].astype(
                    jnp.float32
                )
        act_v[pad + tally :, :] = fast_snake(there_v[...], all_alpha, all_turn, all_inverse)

    @pl.when(dp == n_dp - 1)
    def _():
        act_v[pad + tally :, :] = jnp.zeros((pad, channels), jnp.bfloat16)

    for t in range(KERNEL_TAPS):
        cols = slice(t * channels, (t + 1) * channels)
        at = pad - span + t * DILATION_STEP
        lhs_v[:front, cols] = act_v[at : at + front, :]
        at = at + tally - back
        lhs_v[front : front + back, cols] = act_v[at : at + back, :]
    edge = (
        jnp.dot(lhs_v[: front + back, :], fw_v[...], preferred_element_type=jnp.float32)
        + bias_v[...]
    )
    audio_v[:late, :] = (edge[:late] + here_v[:, mine_cols]).astype(jnp.bfloat16)
    audio_v[late:front, :] = (edge[late:front] + fr_v[late:front, :].astype(jnp.float32)).astype(
        jnp.bfloat16
    )
    audio_v[tally - back :, :] = (edge[front:] + fr_v[tally - back :, :].astype(jnp.float32)).astype(
        jnp.bfloat16
    )


def store_kernel(hidden, audio, hidden_out, audio_out, sems):
    copies = (
        pltpu.make_async_copy(hidden, hidden_out, sems.at[0]),
        pltpu.make_async_copy(audio, audio_out, sems.at[1]),
    )
    for copy in copies:
        copy.start()
    for copy in copies:
        copy.wait()


def fused(
    query,
    new_key,
    new_value,
    cache_key,
    cache_value,
    cache_len,
    residual,
    out_weight,
    norm_gain,
    codec_weight,
    finished,
    owner,
    frames,
    snake_alpha,
    filter_weight,
    conv_bias,
):
    plan = Plan(query, cache_key, residual, norm_gain, codec_weight, frames)
    n_dp, n_mp = plan.n_dp, plan.n_mp
    count = n_dp * n_mp
    bf, f32, i32 = jnp.bfloat16, jnp.float32, jnp.int32
    vm = pltpu.VMEM
    dma = pltpu.SemaphoreType.DMA
    rows, own, channels, tally = plan.rows, plan.own, plan.channels, plan.tally
    taps = KERNEL_TAPS * channels
    biggest = max([size for _, size in blocks_of(plan)] + [plan.front + plan.back])
    scratch = [
        vm(query.shape, bf),
        vm(query.shape, bf),
        vm(query.shape, bf),
        vm((plan.heads, rows, plan.positions, plan.depth), bf),
        vm((plan.heads, rows, plan.positions, plan.depth), bf),
        vm((1, rows), i32),
        vm((rows, plan.local), bf),
        vm((plan.slots, plan.depth_in, plan.chunk), bf),
        vm((2, rows, plan.chunk), bf),
        vm((plan.local // 128, 128), bf),
        vm((1, plan.local), f32),
        vm((plan.local, channels), bf),
        vm((1, rows), i32),
        vm((1, rows), i32),
        vm((tally, own), bf),
        vm((1, channels), f32),
        vm((taps, own), bf),
        vm((1, own), f32),
        vm((tally + 2 * plan.pad, channels), bf),
        vm((plan.late, own), bf),
        vm((n_mp, plan.pad, own), bf),
        vm((rows, plan.group * plan.positions), f32),
        vm((plan.late, rows), bf),
        vm((rows, plan.depth_in), bf),
        vm((plan.heads, rows, plan.group * plan.positions), f32),
        vm((plan.heads, rows, plan.group * plan.positions), bf),
        vm((plan.heads, rows, plan.depth), f32),
        vm((plan.steps, rows, plan.chunk), bf),
        vm((plan.steps, rows, plan.chunk), bf),
        vm((rows, channels), f32),
        vm((rows, 128), f32),
        vm((rows, own + 128), f32),
        vm((rows, own + 128), f32),
        vm((n_dp, CAP, own), bf),
        vm((n_mp, n_dp, CAP, own), bf),
        vm((n_mp, plan.near, CAP, own), bf),
        vm((plan.late, channels), f32),
        vm((plan.pad, channels), f32),
        vm((biggest, taps), bf),
        dma((11,)),
        dma((plan.heads,)),
        dma((plan.heads,)),
        dma((plan.slots,)),
        dma((plan.steps,)),
        dma((KERNEL_TAPS,)),
        dma((2,)),
        dma((2,)),
        dma((2, plan.send_blocks)),
        dma((2, n_mp)),
        dma((2, n_mp)),
        dma((2, plan.steps)),
        dma((2,)),
        dma((count,)),
        dma((count,)),
        dma((count,)),
        dma((plan.near * n_mp,)),
    ]
    anywhere = pl.BlockSpec(memory_space=pl.ANY)
    kept = pl.BlockSpec(memory_space=pltpu.VMEM)
    operands = [
        pltpu.with_memory_space_constraint(x, pltpu.HBM)
        for x in (
        query,
        new_key,
        new_value,
        cache_key,
        cache_value,
        cache_len.reshape(1, -1),
        residual,
        out_weight,
        norm_gain.reshape(-1, 128),
        codec_weight,
        finished.reshape(1, -1),
        owner.reshape(1, -1),
        frames,
        snake_alpha.reshape(1, -1),
        filter_weight.reshape(taps, own),
        conv_bias.reshape(1, -1),
        )
    ]
    kept_pair = pl.pallas_call(
        functools.partial(fused_kernel, plan),
        out_shape=(
            jax.ShapeDtypeStruct((rows, plan.local), bf),
            jax.ShapeDtypeStruct((tally, own), bf),
        ),
        in_specs=[pl.BlockSpec(memory_space=pltpu.HBM)] * 16,
        out_specs=(kept, kept),
        scratch_shapes=scratch,
        compiler_params=pltpu.CompilerParams(
            collective_id=1, has_side_effects=True, vmem_limit_bytes=VMEM_BYTES
        ),
    )(*operands)
    return pl.pallas_call(
        store_kernel,
        out_shape=(
            jax.ShapeDtypeStruct((rows, plan.local), bf),
            jax.ShapeDtypeStruct((tally, own), bf),
        ),
        in_specs=[kept, kept],
        out_specs=(anywhere, anywhere),
        scratch_shapes=[dma((2,))],
        compiler_params=pltpu.CompilerParams(vmem_limit_bytes=4 * 1024 * 1024),
    )(*kept_pair)


VMEM_BYTES = 53 * 1000 * 1000


def step(*args):
    return fused(*args) if lax.axis_size("mp") == 2 else body(*args)


def solution(mesh):
    placed = (
        P("dp", "mp"),
        P("dp", "mp"),
        P("dp", "mp"),
        P("dp", "mp", None, None),
        P("dp", "mp", None, None),
        P("dp"),
        P("dp", None),
        P("mp", None),
        P("mp"),
        P("mp", None),
        P("dp"),
        P("dp"),
        P("dp", "mp"),
        P("mp"),
        P(None, None, "mp"),
        P("mp"),
    )
    return jax.shard_map(
        step, mesh=mesh, in_specs=placed, out_specs=(P("dp", "mp"), P("dp", "mp")), check_vma=False
    )
```

```python
import functools
import jax
import jax.numpy as jnp
from jax import lax
from jax.experimental import pallas as pl
from jax.experimental.pallas import tpu as pltpu
from jax.sharding import PartitionSpec as P

KERNEL_TAPS = 7
DILATION_STEP = 3
CAP = 4
ROW_TILE = 16


def swap(x):
    return lax.ppermute(x, "mp", [(0, 1), (1, 0)])


def gather_mp(x, axis):
    if lax.axis_size("mp") != 2:
        return lax.all_gather(x, "mp", axis=axis, tiled=True)
    other = swap(x)
    first = lax.axis_index("mp") == 0
    return jnp.concatenate([jnp.where(first, x, other), jnp.where(first, other, x)], axis=axis)


def sin_squared(x):
    turns = jnp.round(x * 0.3183098861837907)
    r = (x - turns * 3.140625) - turns * 0.0009676535897932
    q = r * r
    p = -2.5052108e-08 + q * 1.6059044e-10
    p = 2.7557319e-06 + q * p
    p = -1.9841270e-04 + q * p
    p = 8.3333333e-03 + q * p
    p = -1.6666667e-01 + q * p
    sine = r + r * (q * p)
    return sine * sine


def snake(mix, alpha):
    return (mix + sin_squared(alpha * mix) / alpha).astype(jnp.bfloat16)


def columns_kernel(start_ref, x_ref, w_ref, o_ref):
    del start_ref
    o_ref[...] = jnp.dot(x_ref[...], w_ref[...], preferred_element_type=jnp.float32).astype(
        o_ref.dtype
    )


def columns_dot(x, w, start, width, tile, dtype):
    rows, depth = x.shape
    return pl.pallas_call(
        columns_kernel,
        out_shape=jax.ShapeDtypeStruct((rows, width), dtype),
        grid_spec=pltpu.PrefetchScalarGridSpec(
            num_scalar_prefetch=1,
            grid=(width // tile,),
            in_specs=[
                pl.BlockSpec((rows, depth), lambda j, s: (0, 0)),
                pl.BlockSpec((depth, tile), lambda j, s: (0, s[0] + j)),
            ],
            out_specs=pl.BlockSpec((rows, tile), lambda j, s: (0, j)),
        ),
        compiler_params=pltpu.CompilerParams(vmem_limit_bytes=28 * 1024 * 1024),
        cost_estimate=pl.CostEstimate(
            flops=2 * rows * depth * width, bytes_accessed=2 * depth * width, transcendentals=0
        ),
    )(jnp.full((1,), start, jnp.int32), x, w)


def handoff_kernel(
    n_dp, n_mp, near, out_ref, a_ref, b_ref, land_a, land_b, send_a, recv_a, send_b, recv_b
):
    dp = lax.axis_index("dp")
    mp = lax.axis_index("mp")
    count = n_dp * n_mp
    me = dp * n_mp + mp
    barrier = pltpu.get_barrier_semaphore()

    def place(step):
        peer = lax.rem(me + step, count)
        return peer, peer // n_mp, lax.rem(peer, n_mp)

    def greet(step, carry):
        _, pd, pm = place(step)
        pl.semaphore_signal(
            barrier, inc=1, device_id=(pd, pm), device_id_type=pl.DeviceIdType.MESH
        )
        return carry

    lax.fori_loop(1, count, greet, 0)
    pl.semaphore_wait(barrier, count - 1)

    def copy_a(pd, pm, send, recv):
        return pltpu.make_async_remote_copy(
            src_ref=out_ref.at[pd],
            dst_ref=land_a.at[me],
            send_sem=send_a.at[send],
            recv_sem=recv_a.at[recv],
            device_id=(pd, pm),
            device_id_type=pl.DeviceIdType.MESH,
        )

    def copy_b(slot, pd, pm, send, recv):
        return pltpu.make_async_remote_copy(
            src_ref=out_ref.at[pd + 1],
            dst_ref=land_b.at[slot],
            send_sem=send_b.at[send],
            recv_sem=recv_b.at[recv],
            device_id=(pd, pm),
            device_id_type=pl.DeviceIdType.MESH,
        )

    def send(step, carry):
        peer, pd, pm = place(step)
        copy_a(pd, pm, peer, me).start()
        return carry

    def send_near(step, carry):
        peer, pd, pm = place(step)
        copy_b(me, pd, pm, peer, me).start()
        return carry

    @pl.when(dp < near)
    def _():
        lax.fori_loop(1, count, send_near, 0)

    lax.fori_loop(1, count, send, 0)
    land_a[me] = out_ref[dp]

    @pl.when(dp < near)
    def _():
        land_b[me] = out_ref[dp + 1]

    def finish(step, carry):
        peer, pd, pm = place(step)
        copy = copy_a(pd, pm, peer, peer)
        copy.wait_recv()
        copy.wait_send()
        return carry

    def finish_near(step, carry):
        peer, pd, pm = place(step)
        copy_b(me, pd, pm, peer, me).wait_send()
        return carry

    def take_near(sender, carry):
        @pl.when(sender != me)
        def _():
            copy_b(sender, 0, 0, sender, sender).wait_recv()

        return carry

    lax.fori_loop(1, count, finish, 0)

    @pl.when(dp < near)
    def _():
        lax.fori_loop(1, count, finish_near, 0)

    lax.fori_loop(0, near * n_mp, take_near, 0)

    def total_of(land, first):
        total = land[first].astype(jnp.float32)
        for m in range(1, n_mp):
            total = total + land[first + m].astype(jnp.float32)
        return total

    def put(d, carry):
        a_ref[d] = total_of(land_a, d * n_mp)
        return carry

    lax.fori_loop(0, n_dp, put, 0)
    for d in range(near):
        b_ref[d] = total_of(land_b, d * n_mp)


def handoff(outgoing, near):
    n_dp, n_mp = lax.axis_size("dp"), lax.axis_size("mp")
    count = n_dp * n_mp
    _, cap, width = outgoing.shape
    vmem = pl.BlockSpec(memory_space=pltpu.VMEM)
    return pl.pallas_call(
        functools.partial(handoff_kernel, n_dp, n_mp, near),
        out_shape=(
            jax.ShapeDtypeStruct((n_dp, cap, width), jnp.float32),
            jax.ShapeDtypeStruct((near, cap, width), jnp.float32),
        ),
        in_specs=[vmem],
        out_specs=(vmem, vmem),
        scratch_shapes=[
            pltpu.VMEM((count, cap, width), jnp.bfloat16),
            pltpu.VMEM((near * n_mp, cap, width), jnp.bfloat16),
            pltpu.SemaphoreType.DMA((count,)),
            pltpu.SemaphoreType.DMA((count,)),
            pltpu.SemaphoreType.DMA((count,)),
            pltpu.SemaphoreType.DMA((near * n_mp,)),
        ],
        compiler_params=pltpu.CompilerParams(
            collective_id=0, has_side_effects=True, vmem_limit_bytes=16 * 1024 * 1024
        ),
    )(outgoing)


def round_up(n, tile):
    return -(-n // tile) * tile


def taps_of(cells, rows):
    parts = [cells[t * DILATION_STEP : t * DILATION_STEP + rows] for t in range(KERNEL_TAPS)]
    return jnp.concatenate(parts, axis=1)


def attend(query, new_key, new_value, cache_key, cache_value, cache_len):
    count, heads, positions, depth = cache_key.shape
    scale = 1.0 / jnp.sqrt(jnp.float32(depth))
    queries = query.reshape(count, heads, depth)
    fresh_key = new_key.reshape(count, heads, depth)
    fresh_value = new_value.reshape(count, heads, depth)
    scores = (
        jnp.einsum("rhd,rhld->rhl", queries, cache_key, preferred_element_type=jnp.float32) * scale
    )
    own_score = (
        jnp.einsum("rhd,rhd->rh", queries, fresh_key, preferred_element_type=jnp.float32) * scale
    )
    valid = jnp.arange(positions, dtype=jnp.int32)[None, :] < cache_len[:, None]
    scores = jnp.where(valid[:, None, :], scores, -1e30)
    top = jnp.maximum(jnp.max(scores, axis=-1), own_score)
    expo = jnp.where(valid[:, None, :], jnp.exp(scores - top[..., None]), 0.0)
    own_expo = jnp.exp(own_score - top)
    total = jnp.sum(expo, axis=-1) + own_expo
    weights = (expo / total[..., None]).astype(jnp.bfloat16)
    own_weight = (own_expo / total).astype(jnp.bfloat16)
    mixed = jnp.einsum("rhl,rhld->rhd", weights, cache_value, preferred_element_type=jnp.float32)
    mixed = mixed + own_weight.astype(jnp.float32)[..., None] * fresh_value.astype(jnp.float32)
    return mixed.astype(jnp.bfloat16).reshape(count, heads * depth)


def body(
    query,
    new_key,
    new_value,
    cache_key,
    cache_value,
    cache_len,
    residual,
    out_weight,
    norm_gain,
    codec_weight,
    finished,
    owner,
    frames,
    snake_alpha,
    filter_weight,
    conv_bias,
):
    owners = lax.axis_size("dp")
    n_mp = lax.axis_size("mp")
    core = lax.axis_index("mp")
    tally, own = frames.shape
    span = KERNEL_TAPS // 2 * DILATION_STEP
    late = owners * CAP
    near = -(-span // CAP)
    front = round_up(late + span, ROW_TILE)
    back = round_up(span, ROW_TILE)

    wide_frames = frames.astype(jnp.float32)
    alpha_all = gather_mp(snake_alpha, 0)
    early = gather_mp(snake(wide_frames, snake_alpha), 1)
    head_frames = gather_mp(frames[:late], 1)
    before = lax.ppermute(early[tally - span :], "dp", [(i, i + 1) for i in range(owners - 1)])
    after_frames = lax.ppermute(
        head_frames[: near * CAP], "dp", [(i + 1, i) for i in range(owners - 1)]
    )
    middle = tally - front - back
    main = wide_frames[front : tally - back] + conv_bias
    for t in range(KERNEL_TAPS):
        start = front - span + t * DILATION_STEP
        main = main + jnp.dot(
            early[start : start + middle], filter_weight[t], preferred_element_type=jnp.float32
        )
    main = main.astype(jnp.bfloat16)

    attended = attend(query, new_key, new_value, cache_key, cache_value, cache_len)
    count = attended.shape[0]
    width = out_weight.shape[1]
    local_width = norm_gain.shape[0]
    residual_part = lax.dynamic_slice_in_dim(residual, core * local_width, local_width, 1)
    if n_mp == 2:
        tile = 1024
        theirs = columns_dot(
            attended, out_weight, (1 - core) * (local_width // tile), local_width, tile, jnp.bfloat16
        )
        arrived = swap(theirs)
        mine = columns_dot(
            attended, out_weight, core * (local_width // tile), local_width, tile, jnp.float32
        )
        projected = mine + arrived.astype(jnp.float32)
    else:
        term = jnp.dot(attended, out_weight, preferred_element_type=jnp.float32)
        projected = lax.psum_scatter(term, "mp", scatter_dimension=1, tiled=True)
    hidden = (residual_part.astype(jnp.float32) + projected).astype(jnp.bfloat16)
    wide = hidden.astype(jnp.float32)
    squares = jnp.sum(wide * wide, axis=-1)
    squares = squares + swap(squares) if n_mp == 2 else lax.psum(squares, "mp")
    meansq = squares / width
    normed = (wide * norm_gain.astype(jnp.float32)).astype(jnp.bfloat16)
    channels = codec_weight.shape[1]
    share = columns_dot(normed, codec_weight, 0, channels, 256, jnp.float32)
    share = (share * lax.rsqrt(meansq + 1e-05)[:, None]).astype(jnp.bfloat16)

    index = jnp.arange(count, dtype=jnp.int32)
    earlier = (
        (owner[:, None] == owner[None, :])
        & (finished[None, :] == 1)
        & (index[None, :] < index[:, None])
    )
    slot = jnp.sum(earlier.astype(jnp.int32), axis=1)
    target = owner * CAP + slot
    places = jnp.arange((owners + 1) * CAP, dtype=jnp.int32)
    onehot = ((places[:, None] == target[None, :]) & (finished[None, :] == 1)).astype(jnp.bfloat16)
    outgoing = jnp.dot(onehot, share, preferred_element_type=jnp.float32).astype(jnp.bfloat16)
    here, there = handoff(outgoing.reshape(owners + 1, CAP, channels), near)
    here = here.reshape(late, channels).astype(jnp.bfloat16).astype(jnp.float32)
    there = there.reshape(near * CAP, channels).astype(jnp.bfloat16).astype(jnp.float32)

    head_mix = head_frames.astype(jnp.float32) + here
    head_act = snake(head_mix, alpha_all)
    after = snake(after_frames.astype(jnp.float32) + there, alpha_all)[:span]
    cells_a = jnp.concatenate([before, head_act, early[late : front + span]], axis=0)
    cells_b = jnp.concatenate([early[tally - back - span :], after], axis=0)
    edges = jnp.concatenate([taps_of(cells_a, front), taps_of(cells_b, back)], axis=0)
    flat = filter_weight.reshape(KERNEL_TAPS * channels, own)
    own_mix = lax.dynamic_slice_in_dim(head_mix, core * own, own, 1)
    edge_mix = jnp.concatenate(
        [own_mix, wide_frames[late:front], wide_frames[tally - back :]], axis=0
    )
    edge = jnp.dot(edges, flat, preferred_element_type=jnp.float32) + edge_mix + conv_bias
    edge = edge.astype(jnp.bfloat16)
    audio = jnp.concatenate([edge[:front], main, edge[front:]], axis=0)
    return (hidden, audio)


MESH = pl.DeviceIdType.MESH
SIN_SQUARED = (
    1.0,
    -0.3333333134651184,
    0.04444440081715584,
    -0.003174516372382641,
    0.00014100516273174435,
    -4.2275191844964866e-06,
    8.055603473167139e-08,
)
ROUNDER = 12582912.0


def fast_snake(mix, alpha, turn, inverse):
    turns = (mix * turn + ROUNDER) - ROUNDER
    r = (mix * alpha - turns * 3.140625) - turns * 0.0009676535897932
    q = r * r
    p = SIN_SQUARED[-1] * q + SIN_SQUARED[-2]
    for c in SIN_SQUARED[-3::-1]:
        p = p * q + c
    return (mix + (q * p) * inverse).astype(jnp.bfloat16)


def iota(shape, axis):
    return lax.broadcasted_iota(jnp.int32, shape, axis)


def column_of(row, size):
    spread = jnp.broadcast_to(row, (size, size))
    return jnp.sum(
        jnp.where(iota((size, size), 0) == iota((size, size), 1), spread, 0), axis=1, keepdims=True
    )


class Plan:
    def __init__(self, query, cache_key, residual, norm_gain, codec_weight, frames):
        self.n_dp, self.n_mp = lax.axis_size("dp"), lax.axis_size("mp")
        self.rows, self.heads, self.positions, self.depth = cache_key.shape
        self.width = residual.shape[1]
        self.local = norm_gain.shape[0]
        self.channels = codec_weight.shape[1]
        self.tally, self.own = frames.shape
        self.late = self.n_dp * CAP
        self.span = KERNEL_TAPS // 2 * DILATION_STEP
        self.near = -(-self.span // CAP)
        self.pad = round_up(self.span, ROW_TILE)
        self.front = round_up(self.late + self.span, ROW_TILE)
        self.back = self.pad
        self.middle = self.tally - self.front - self.back
        self.chunk = 512
        self.steps = self.local // self.chunk
        self.slots = min(6, self.steps)
        self.group = ROW_TILE
        self.snake_rows = 32
        self.send_blocks = 4
        self.depth_in = self.heads * self.depth
        self.unroll = 8
        self.octet = 8


def blocks_of(plan):
    count = 5
    unit = plan.middle // ROW_TILE
    sizes = [(unit // count + (1 if i < unit % count else 0)) * ROW_TILE for i in range(count)]
    starts = [plan.front + sum(sizes[:i]) for i in range(count)]
    return list(zip(starts, sizes))


def fused_kernel(
    P_,
    query,
    new_key,
    new_value,
    cache_key,
    cache_value,
    lens,
    residual,
    out_weight,
    gain,
    codec_weight,
    finished,
    owner,
    frames,
    alpha,
    filters,
    bias,
    hid_v,
    audio_v,
    q_v,
    nk_v,
    nv_v,
    k_v,
    v_v,
    len_v,
    res_v,
    w_v,
    normed_v,
    gain_raw,
    gain_v,
    cw_v,
    fin_v,
    own_v,
    fr_v,
    al_v,
    fw_v,
    bias_v,
    act_v,
    hf_v,
    af_v,
    valid_v,
    hot_v,
    att_v,
    score_v,
    p_v,
    o_v,
    out_v,
    in_v,
    acc_v,
    sq_v,
    sendc_v,
    recvc_v,
    sendh_v,
    land_v,
    near_v,
    here_v,
    there_v,
    lhs_v,
    s_in,
    s_k,
    s_v,
    s_w,
    s_cw,
    s_fw,
    x_alpha,
    x_head,
    x_early,
    x_before,
    x_after,
    x_part,
    x_codec,
    send_a,
    recv_a,
    send_b,
    recv_b,
):
    n_dp, n_mp = P_.n_dp, P_.n_mp
    count = n_dp * n_mp
    rows, heads, positions, depth = P_.rows, P_.heads, P_.positions, P_.depth
    chunk, steps, slots = P_.chunk, P_.steps, P_.slots
    own, channels, tally, pad = P_.own, P_.channels, P_.tally, P_.pad
    late, span, front, back = P_.late, P_.span, P_.front, P_.back
    dp = lax.axis_index("dp")
    core = lax.axis_index("mp")
    me = dp * n_mp + core
    other = 1 - core
    mine_cols = pl.ds(pl.multiple_of(core * own, own), own)
    local_cols = pl.ds(pl.multiple_of(core * P_.local, P_.local), P_.local)

    def local(src, dst, sem):
        return pltpu.make_async_copy(src, dst, sem)

    def remote(src, dst, send, recv, to_dp, to_mp):
        return pltpu.make_async_remote_copy(
            src_ref=src,
            dst_ref=dst,
            send_sem=send,
            recv_sem=recv,
            device_id=(to_dp, to_mp),
            device_id_type=MESH,
        )

    frames_in = local(frames, fr_v, s_in.at[0])
    alpha_in = local(alpha, al_v.at[:, mine_cols], s_in.at[1])
    lens_in = local(lens, len_v, s_in.at[2])
    fin_in = local(finished, fin_v, s_in.at[3])
    own_in = local(owner, own_v, s_in.at[4])
    q_in = local(query, q_v, s_in.at[5])
    nk_in = local(new_key, nk_v, s_in.at[6])
    nv_in = local(new_value, nv_v, s_in.at[7])
    res_in = local(residual.at[:, local_cols], res_v, s_in.at[8])
    gain_in = local(gain, gain_raw, s_in.at[9])
    bias_in = local(bias, bias_v, s_in.at[10])

    def key_in(h):
        return local(cache_key.at[:, h], k_v.at[h], s_k.at[h])

    def value_in(h):
        return local(cache_value.at[:, h], v_v.at[h], s_v.at[h])

    def weight_in(i):
        begin = lax.select(i < steps, other * P_.local, core * P_.local) + lax.rem(i, steps) * chunk
        return local(
            out_weight.at[:, pl.ds(pl.multiple_of(begin, chunk), chunk)],
            w_v.at[lax.rem(i, slots)],
            s_w.at[lax.rem(i, slots)],
        )

    def codec_in(i):
        part = pl.ds(pl.multiple_of(i * chunk, chunk), chunk)
        return local(codec_weight.at[part, :], cw_v.at[part, :], s_cw.at[i])

    def filter_in(t):
        part = pl.ds(pl.multiple_of(t * channels, channels), channels)
        return local(filters.at[part, :], fw_v.at[part, :], s_fw.at[t])

    for copy in (lens_in, q_in, nk_in):
        copy.start()

    def start_key(h, carry):
        key_in(h).start()
        return carry

    def start_value(h, carry):
        value_in(h).start()
        return carry

    lax.fori_loop(0, heads, start_key, 0)
    lax.fori_loop(0, heads, start_value, 0)
    for copy in (nv_in, alpha_in, fin_in, own_in, frames_in):
        copy.start()

    barrier = pltpu.get_barrier_semaphore()

    def place(step):
        peer = lax.rem(me + step, count)
        return peer, peer // n_mp, lax.rem(peer, n_mp)

    def greet(step, carry):
        _, pd, pm = place(step)
        pl.semaphore_signal(barrier, inc=1, device_id=(pd, pm), device_id_type=MESH)
        return carry

    lax.fori_loop(1, count, greet, 0)

    def start_weight(i, carry):
        weight_in(i).start()
        return carry

    lax.fori_loop(0, slots, start_weight, 0)
    for copy in (res_in, gain_in, bias_in):
        copy.start()

    def start_codec(i, carry):
        codec_in(i).start()
        return carry

    lax.fori_loop(0, steps, start_codec, 0)

    def start_filter(t, carry):
        filter_in(t).start()
        return carry

    for copy in (lens_in, fin_in, own_in):
        copy.wait()

    length = column_of(len_v[...], rows)
    lanes = P_.group * positions
    lane = iota((rows, lanes), 1)
    line = lax.rem(iota((rows, lanes), 0), P_.group)
    valid = (lane // positions == line) & (lax.rem(lane, positions) < length)
    valid_v[...] = jnp.where(valid, 0.0, -1e30)

    owner_row, done_row = own_v[...], fin_v[...]
    owner_col, done_col = column_of(owner_row, rows), column_of(done_row, rows)
    earlier = (
        (owner_col == owner_row)
        & (done_col == 1)
        & (iota((rows, rows), 0) < iota((rows, rows), 1))
    )
    slot = jnp.sum(jnp.where(earlier, 1, 0), axis=0, keepdims=True)
    target = jnp.where(done_row == 1, owner_row * CAP + slot, -1)
    hot_v[...] = jnp.where(iota((late, rows), 0) == target, 1.0, 0.0).astype(jnp.bfloat16)

    for copy in (q_in, nk_in, nv_in):
        copy.wait()
    scale = 1.0 / jnp.sqrt(jnp.float32(depth))

    def score_step(j, carry):
        for u in range(P_.octet):
            key_in(j * P_.octet + u).wait()
        lane_head = iota((depth, P_.octet * P_.group), 1) // P_.group
        for g in range(rows // P_.group):
            part = slice(g * P_.group, (g + 1) * P_.group)
            stacked, keys = [], []
            for u in range(P_.octet):
                h = j * P_.octet + u
                cols = pl.ds(pl.multiple_of(h * depth, depth), depth)
                stacked.append(q_v[part, cols].astype(jnp.float32))
                keys.append(k_v[h, part].reshape(lanes, depth))
            turned = jnp.concatenate(stacked, axis=0).T
            queries = [
                jnp.where(lane_head == u, turned, 0.0).astype(jnp.bfloat16)
                for u in range(P_.octet)
            ]
            found = jnp.dot(
                jnp.concatenate(keys, axis=1),
                jnp.concatenate(queries, axis=0),
                preferred_element_type=jnp.float32,
            ).T
            for u in range(P_.octet):
                score_v[j * P_.octet + u, part, :] = found[u * P_.group : (u + 1) * P_.group]
        return carry

    lax.fori_loop(0, heads // P_.octet, score_step, 0)

    def soft_step(h, carry):
        cols = pl.ds(pl.multiple_of(h * depth, depth), depth)
        s = jnp.where(valid_v[...] < 0.0, -1e30, score_v[h] * scale)
        mine = q_v[:, cols].astype(jnp.float32) * nk_v[:, cols].astype(jnp.float32)
        mine = jnp.sum(mine, axis=1, keepdims=True) * scale
        top = jnp.maximum(jnp.max(s, axis=1, keepdims=True), mine)
        expo = jnp.exp(s - top)
        mine_expo = jnp.exp(mine - top)
        share = 1.0 / (jnp.sum(expo, axis=1, keepdims=True) + mine_expo)
        p_v[h] = (expo * share).astype(jnp.bfloat16)
        mine_weight = (mine_expo * share).astype(jnp.bfloat16).astype(jnp.float32)
        o_v[h] = mine_weight * nv_v[:, cols].astype(jnp.float32)
        return carry

    lax.fori_loop(0, heads, soft_step, 0)

    def value_step(j, carry):
        for u in range(P_.unroll):
            value_in(j * P_.unroll + u).wait()
        for u in range(P_.unroll):
            h = j * P_.unroll + u
            cols = pl.ds(pl.multiple_of(h * depth, depth), depth)
            for g in range(rows // P_.group):
                part = slice(g * P_.group, (g + 1) * P_.group)
                values = v_v[h, part].reshape(lanes, depth)
                mixed = jnp.dot(p_v[h, part, :], values, preferred_element_type=jnp.float32)
                att_v[part, cols] = (mixed + o_v[h, part, :]).astype(jnp.bfloat16)
        return carry

    lax.fori_loop(0, heads // P_.unroll, value_step, 0)

    alpha_x = remote(
        alpha, al_v.at[:, mine_cols], x_alpha.at[0], x_alpha.at[1], dp, other
    )
    head_x = remote(frames.at[0:late], hf_v, x_head.at[0], x_head.at[1], dp, other)

    block = tally // P_.send_blocks

    def early_x(b):
        part = pl.ds(pl.multiple_of(pad + b * block, ROW_TILE), block)
        return remote(
            act_v.at[part, mine_cols],
            act_v.at[part, mine_cols],
            x_early.at[0, b],
            x_early.at[1, b],
            dp,
            other,
        )

    def before_x(m, to_dp, sender):
        cols = pl.ds(pl.multiple_of(sender * own, own), own)
        return remote(
            act_v.at[tally : tally + pad, mine_cols],
            act_v.at[0:pad, cols],
            x_before.at[0, m],
            x_before.at[1, sender],
            to_dp,
            m,
        )

    def after_x(m, to_dp, sender):
        return remote(
            frames.at[0:pad],
            af_v.at[sender],
            x_after.at[0, m],
            x_after.at[1, sender],
            to_dp,
            m,
        )

    pl.semaphore_wait(barrier, count - 1)
    alpha_x.start()
    head_x.start()

    @pl.when(dp > 0)
    def _():
        for m in range(n_mp):
            after_x(m, dp - 1, core).start()


    for copy in (alpha_in, frames_in):
        copy.wait()
    my_alpha = al_v[:, mine_cols]
    my_turn = my_alpha * 0.3183098861837907
    my_inverse = 1.0 / my_alpha
    snake_rows = tally // steps

    def part_x(i):
        return remote(out_v.at[i], in_v.at[i], x_part.at[0, i], x_part.at[1, i], dp, other)

    def their_step(i, carry):
        @pl.when(i > 0)
        def _():
            part_x(i - 1).start()

        weight_in(i).wait()
        for k in range(snake_rows // P_.snake_rows):
            begin = i * snake_rows + k * P_.snake_rows
            part = pl.ds(pl.multiple_of(begin, P_.snake_rows), P_.snake_rows)
            where_to = pl.ds(pl.multiple_of(pad + begin, ROW_TILE), P_.snake_rows)
            act_v[where_to, mine_cols] = fast_snake(
                fr_v[part, :].astype(jnp.float32), my_alpha, my_turn, my_inverse
            )
        out_v[i] = jnp.dot(
            att_v[...], w_v[lax.rem(i, slots)], preferred_element_type=jnp.float32
        ).astype(jnp.bfloat16)
        weight_in(i + slots).start()
        return carry

    lax.fori_loop(0, steps, their_step, 0)
    part_x(steps - 1).start()
    for b in range(P_.send_blocks):
        early_x(b).start()

    @pl.when(dp < n_dp - 1)
    def _():
        for m in range(n_mp):
            before_x(m, dp + 1, core).start()


    for copy in (res_in, gain_in, bias_in):
        copy.wait()
    gains = gain_raw[...].astype(jnp.float32)
    for k in range(P_.local // 128):
        gain_v[:, k * 128 : (k + 1) * 128] = gains[k : k + 1]
    acc_v[...] = jnp.zeros_like(acc_v)
    sq_v[...] = jnp.zeros_like(sq_v)

    def produce(i, first=False):
        cols = pl.ds(pl.multiple_of(i * chunk, chunk), chunk)
        total = jnp.dot(att_v[...], w_v[lax.rem(i + steps, slots)], preferred_element_type=jnp.float32)
        if first:
            part_x(0).wait_recv()
        total = total + in_v[i].astype(jnp.float32) + res_v[:, cols].astype(jnp.float32)
        hidden = total.astype(jnp.bfloat16)
        hid_v[:, cols] = hidden
        wide = hidden.astype(jnp.float32)
        square = wide * wide
        squares = square[:, :128]
        for k in range(1, chunk // 128):
            squares = squares + square[:, k * 128 : (k + 1) * 128]
        sq_v[...] += squares
        normed_v[lax.rem(i, 2)] = (wide * gain_v[:, cols]).astype(jnp.bfloat16)

    def consume(i):
        cols = pl.ds(pl.multiple_of(i * chunk, chunk), chunk)
        acc_v[...] += jnp.dot(
            normed_v[lax.rem(i, 2)], cw_v[cols, :], preferred_element_type=jnp.float32
        )

    def mine_step(i, carry):
        codec_in(i - 1).wait()
        weight_in(i + steps).wait()
        part_x(i).wait_recv()
        consume(i - 1)
        produce(i)

        @pl.when(i + slots < steps)
        def _():
            weight_in(i + steps + slots).start()

        @pl.when(i == max(1, steps - slots))
        def _():
            lax.fori_loop(0, KERNEL_TAPS, start_filter, 0)

        return carry

    weight_in(jnp.int32(steps)).wait()
    produce(jnp.int32(0), True)
    if slots < steps:
        weight_in(jnp.int32(steps + slots)).start()
    lax.fori_loop(1, steps, mine_step, 0)
    codec_in(steps - 1).wait()
    consume(jnp.int32(steps - 1))

    other_cols = pl.ds(pl.multiple_of(other * own, own), own)
    sendc_v[:, :own] = acc_v[:, other_cols]
    sendc_v[:, own:] = sq_v[...]
    codec_x = remote(sendc_v, recvc_v, x_codec.at[0], x_codec.at[1], dp, other)
    codec_x.start()

    def conv_block(index):
        begin, size = blocks_of(P_)[index]
        for t in range(KERNEL_TAPS):
            at = pad + begin - span + t * DILATION_STEP
            lhs_v[:size, t * channels : (t + 1) * channels] = act_v[at : at + size, :]
        audio_v[begin : begin + size, :] = (
            jnp.dot(lhs_v[:size, :], fw_v[...], preferred_element_type=jnp.float32)
            + fr_v[begin : begin + size, :].astype(jnp.float32)
            + bias_v[...]
        ).astype(jnp.bfloat16)

    codec_x.wait_recv()
    square = jnp.sum(sq_v[...] + recvc_v[:, own:], axis=1, keepdims=True)
    latent = (
        (acc_v[:, mine_cols] + recvc_v[:, :own]) * lax.rsqrt(square / P_.width + 1e-05)
    ).astype(jnp.bfloat16)
    outgoing = jnp.dot(hot_v[...], latent, preferred_element_type=jnp.float32)
    for d in range(n_dp):
        sendh_v[d] = outgoing[d * CAP : (d + 1) * CAP].astype(jnp.bfloat16)

    def copy_a(pd, pm, src_dp, src_mp, send, recv):
        return remote(
            sendh_v.at[pd], land_v.at[src_mp, src_dp], send_a.at[send], recv_a.at[recv], pd, pm
        )

    def copy_b(pd, pm, src_dp, src_mp, send, recv):
        return remote(
            sendh_v.at[pd + 1], near_v.at[src_mp, src_dp], send_b.at[send], recv_b.at[recv], pd, pm
        )

    def send_near(step, carry):
        peer, pd, pm = place(step)

        @pl.when(pd < n_dp - 1)
        def _():
            copy_b(pd, pm, dp, core, peer, me).start()

        return carry

    def send(step, carry):
        peer, pd, pm = place(step)
        copy_a(pd, pm, dp, core, peer, me).start()
        return carry

    lax.fori_loop(1, count, send, 0, unroll=True)

    @pl.when(dp < P_.near)
    def _():
        lax.fori_loop(1, count, send_near, 0, unroll=True)

    land_v[core, dp] = sendh_v[dp]

    @pl.when(dp < P_.near)
    def _():
        near_v[core, dp] = sendh_v[lax.rem(dp + 1, n_dp)]

    def wait_filter(t, carry):
        filter_in(t).wait()
        return carry

    lax.fori_loop(0, KERNEL_TAPS, wait_filter, 0)
    for b in range(P_.send_blocks):
        early_x(b).wait_recv()

    for index in range(len(blocks_of(P_))):
        conv_block(index)

    alpha_x.wait_recv()
    head_x.wait_recv()

    all_alpha = al_v[...]
    all_turn = all_alpha * 0.3183098861837907
    all_inverse = 1.0 / all_alpha
    here_v[:, mine_cols] = fr_v[0:late, :].astype(jnp.float32)
    here_v[:, other_cols] = hf_v[...].astype(jnp.float32)

    @pl.when(dp < n_dp - 1)
    def _():
        for m in range(n_mp):
            after_x(0, 0, m).wait_recv()
            there_v[:, m * own : (m + 1) * own] = af_v[m].astype(jnp.float32)

    for b in range(P_.send_blocks):
        early_x(b).wait_send()
    @pl.when(dp > 0)
    def _():
        for m in range(n_mp):
            before_x(0, 0, m).wait_recv()

    @pl.when(dp == 0)
    def _():
        act_v[0:pad, :] = jnp.zeros((pad, channels), jnp.bfloat16)

    alpha_x.wait_send()
    head_x.wait_send()

    @pl.when(dp < n_dp - 1)
    def _():
        for m in range(n_mp):
            before_x(m, 0, core).wait_send()

    @pl.when(dp > 0)
    def _():
        for m in range(n_mp):
            after_x(m, 0, core).wait_send()

    def part_sent(i, carry):
        part_x(i).wait_send()
        return carry

    lax.fori_loop(0, steps, part_sent, 0)
    codec_x.wait_send()

    def sent(step, carry):
        peer, pd, pm = place(step)
        copy_a(pd, pm, dp, core, peer, me).wait_send()
        return carry

    lax.fori_loop(1, count, sent, 0)

    def sent_near(step, carry):
        peer, pd, pm = place(step)

        @pl.when(pd < n_dp - 1)
        def _():
            copy_b(pd, pm, dp, core, peer, me).wait_send()

        return carry

    @pl.when(dp < P_.near)
    def _():
        lax.fori_loop(1, count, sent_near, 0)

    for s in range(n_dp):
        for m in range(n_mp):

            @pl.when(me != s * n_mp + m)
            def _(s=s, m=m):
                copy_a(0, 0, s, m, 0, s * n_mp + m).wait_recv()

            here_v[s * CAP : (s + 1) * CAP, m * own : (m + 1) * own] += land_v[m, s].astype(
                jnp.float32
            )
    act_v[pad : pad + late, :] = fast_snake(here_v[...], all_alpha, all_turn, all_inverse)

    @pl.when(dp < n_dp - 1)
    def _():
        def take_near(sender, carry):
            @pl.when(sender != me)
            def _():
                copy_b(0, 0, sender // n_mp, lax.rem(sender, n_mp), 0, sender).wait_recv()

            return carry

        lax.fori_loop(0, P_.near * n_mp, take_near, 0)
        for m in range(n_mp):
            for s in range(P_.near):
                there_v[s * CAP : (s + 1) * CAP, m * own : (m + 1) * own] += near_v[m, s].astype(
                    jnp.float32
                )
        act_v[pad + tally :, :] = fast_snake(there_v[...], all_alpha, all_turn, all_inverse)

    @pl.when(dp == n_dp - 1)
    def _():
        act_v[pad + tally :, :] = jnp.zeros((pad, channels), jnp.bfloat16)

    for t in range(KERNEL_TAPS):
        cols = slice(t * channels, (t + 1) * channels)
        at = pad - span + t * DILATION_STEP
        lhs_v[:front, cols] = act_v[at : at + front, :]
        at = at + tally - back
        lhs_v[front : front + back, cols] = act_v[at : at + back, :]
    edge = (
        jnp.dot(lhs_v[: front + back, :], fw_v[...], preferred_element_type=jnp.float32)
        + bias_v[...]
    )
    audio_v[:late, :] = (edge[:late] + here_v[:, mine_cols]).astype(jnp.bfloat16)
    audio_v[late:front, :] = (edge[late:front] + fr_v[late:front, :].astype(jnp.float32)).astype(
        jnp.bfloat16
    )
    audio_v[tally - back :, :] = (edge[front:] + fr_v[tally - back :, :].astype(jnp.float32)).astype(
        jnp.bfloat16
    )


def store_kernel(hidden, audio, hidden_out, audio_out, sems):
    copies = (
        pltpu.make_async_copy(hidden, hidden_out, sems.at[0]),
        pltpu.make_async_copy(audio, audio_out, sems.at[1]),
    )
    for copy in copies:
        copy.start()
    for copy in copies:
        copy.wait()


def fused(
    query,
    new_key,
    new_value,
    cache_key,
    cache_value,
    cache_len,
    residual,
    out_weight,
    norm_gain,
    codec_weight,
    finished,
    owner,
    frames,
    snake_alpha,
    filter_weight,
    conv_bias,
):
    plan = Plan(query, cache_key, residual, norm_gain, codec_weight, frames)
    n_dp, n_mp = plan.n_dp, plan.n_mp
    count = n_dp * n_mp
    bf, f32, i32 = jnp.bfloat16, jnp.float32, jnp.int32
    vm = pltpu.VMEM
    dma = pltpu.SemaphoreType.DMA
    rows, own, channels, tally = plan.rows, plan.own, plan.channels, plan.tally
    taps = KERNEL_TAPS * channels
    biggest = max([size for _, size in blocks_of(plan)] + [plan.front + plan.back])
    scratch = [
        vm(query.shape, bf),
        vm(query.shape, bf),
        vm(query.shape, bf),
        vm((plan.heads, rows, plan.positions, plan.depth), bf),
        vm((plan.heads, rows, plan.positions, plan.depth), bf),
        vm((1, rows), i32),
        vm((rows, plan.local), bf),
        vm((plan.slots, plan.depth_in, plan.chunk), bf),
        vm((2, rows, plan.chunk), bf),
        vm((plan.local // 128, 128), bf),
        vm((1, plan.local), f32),
        vm((plan.local, channels), bf),
        vm((1, rows), i32),
        vm((1, rows), i32),
        vm((tally, own), bf),
        vm((1, channels), f32),
        vm((taps, own), bf),
        vm((1, own), f32),
        vm((tally + 2 * plan.pad, channels), bf),
        vm((plan.late, own), bf),
        vm((n_mp, plan.pad, own), bf),
        vm((rows, plan.group * plan.positions), f32),
        vm((plan.late, rows), bf),
        vm((rows, plan.depth_in), bf),
        vm((plan.heads, rows, plan.group * plan.positions), f32),
        vm((plan.heads, rows, plan.group * plan.positions), bf),
        vm((plan.heads, rows, plan.depth), f32),
        vm((plan.steps, rows, plan.chunk), bf),
        vm((plan.steps, rows, plan.chunk), bf),
        vm((rows, channels), f32),
        vm((rows, 128), f32),
        vm((rows, own + 128), f32),
        vm((rows, own + 128), f32),
        vm((n_dp, CAP, own), bf),
        vm((n_mp, n_dp, CAP, own), bf),
        vm((n_mp, plan.near, CAP, own), bf),
        vm((plan.late, channels), f32),
        vm((plan.pad, channels), f32),
        vm((biggest, taps), bf),
        dma((11,)),
        dma((plan.heads,)),
        dma((plan.heads,)),
        dma((plan.slots,)),
        dma((plan.steps,)),
        dma((KERNEL_TAPS,)),
        dma((2,)),
        dma((2,)),
        dma((2, plan.send_blocks)),
        dma((2, n_mp)),
        dma((2, n_mp)),
        dma((2, plan.steps)),
        dma((2,)),
        dma((count,)),
        dma((count,)),
        dma((count,)),
        dma((plan.near * n_mp,)),
    ]
    anywhere = pl.BlockSpec(memory_space=pl.ANY)
    kept = pl.BlockSpec(memory_space=pltpu.VMEM)
    operands = [
        pltpu.with_memory_space_constraint(x, pltpu.HBM)
        for x in (
        query,
        new_key,
        new_value,
        cache_key,
        cache_value,
        cache_len.reshape(1, -1),
        residual,
        out_weight,
        norm_gain.reshape(-1, 128),
        codec_weight,
        finished.reshape(1, -1),
        owner.reshape(1, -1),
        frames,
        snake_alpha.reshape(1, -1),
        filter_weight.reshape(taps, own),
        conv_bias.reshape(1, -1),
        )
    ]
    kept_pair = pl.pallas_call(
        functools.partial(fused_kernel, plan),
        out_shape=(
            jax.ShapeDtypeStruct((rows, plan.local), bf),
            jax.ShapeDtypeStruct((tally, own), bf),
        ),
        in_specs=[pl.BlockSpec(memory_space=pltpu.HBM)] * 16,
        out_specs=(kept, kept),
        scratch_shapes=scratch,
        compiler_params=pltpu.CompilerParams(
            collective_id=1, has_side_effects=True, vmem_limit_bytes=VMEM_BYTES
        ),
    )(*operands)
    return pl.pallas_call(
        store_kernel,
        out_shape=(
            jax.ShapeDtypeStruct((rows, plan.local), bf),
            jax.ShapeDtypeStruct((tally, own), bf),
        ),
        in_specs=[kept, kept],
        out_specs=(anywhere, anywhere),
        scratch_shapes=[dma((2,))],
        compiler_params=pltpu.CompilerParams(vmem_limit_bytes=4 * 1024 * 1024),
    )(*kept_pair)


VMEM_BYTES = 53 * 1000 * 1000


def step(*args):
    return fused(*args) if lax.axis_size("mp") == 2 else body(*args)


def solution(mesh):
    placed = (
        P("dp", "mp"),
        P("dp", "mp"),
        P("dp", "mp"),
        P("dp", "mp", None, None),
        P("dp", "mp", None, None),
        P("dp"),
        P("dp", None),
        P("mp", None),
        P("mp"),
        P("mp", None),
        P("dp"),
        P("dp"),
        P("dp", "mp"),
        P("mp"),
        P(None, None, "mp"),
        P("mp"),
    )
    return jax.shard_map(
        step, mesh=mesh, in_specs=placed, out_specs=(P("dp", "mp"), P("dp", "mp")), check_vma=False
    )
```
